512 devices in a mesh: gx: 8 (over z_lo, core), gz: 16 (over y, z_hi), gy: 4 (over x).
Axes of the slice: x: 4, y: 8, z: 8 (z_hi: 2, z_lo: 4; z = z_hi * 4 + z_lo), core: 2. Of those that a mesh axis runs over, the one named last changes fastest.
Arguments:
- spectral: float32 [2, 512, 32, 2048], P(None, 'gz', 'gy', 'gx'), may hold values from -6 to 6
- shifts: int32 [512, 32], P('gz', 'gy'), may hold values from 0 to 2047
- colour: int32 [32, 2048], P('gy', 'gx'), may hold values 0 or 1
- pressure: float32 [512, 32, 2048], P('gz', 'gy', 'gx'), may hold values from -5 to 7
- source: float32 [512, 32, 2048], P('gz', 'gy', 'gx'), may hold values from -4.5 to 7
Outputs:
- log_perm: float32 [512, 32, 2048], P('gz', 'gy', 'gx')
- smoothed: float32 [512, 32, 2048], P('gz', 'gy', 'gx')
The draws below stay inside these ranges and needn't reach their ends.
All inputs are finite; a program needn't handle non-finite values. No bound on the sum of `colour` on one device may be relied on, other than what follows from the above.
Results may differ from the reference program's by a relative error of at most 0.0038.
Values sent between devices are 32-bit elements; how exact they have to be, the bound alone decides.
A program may use at most 128 MiB of HBM per device.

```python
import math
import jax
import jax.numpy as jnp
from jax import lax

NX = 2048
NY = 32
NZ = 512
VERT = 65536


def drawn_field(key, level_lo, level_hi):
    level_key, noise_key = jax.random.split(key)
    level = jax.random.uniform(level_key, (1, NY, NX), jnp.float32, level_lo, level_hi)
    rough = jnp.clip(jax.random.normal(noise_key, (NZ, NY, NX), jnp.float32), -5.0, 5.0)
    return (level + rough).astype(jnp.float32)


def draw_pressure(key, part):
    field_key = jax.random.fold_in(key, 11)
    return drawn_field(field_key, 0.0, 2.0)


def draw_source(key, part):
    field_key = jax.random.fold_in(key, 23)
    return drawn_field(field_key, 0.5, 2.0)


def touch_ends(drawn, rng, smallest, largest):
    extent = drawn.shape
    place = [jax.random.randint(jax.random.fold_in(rng, axis), (), 0, extent[axis]) for axis in range(len(extent))]
    drawn = drawn.at[tuple(place)].set(smallest)
    longest = extent.index(max(extent))
    place[longest] = (place[longest] + 1) % extent[longest]
    return drawn.at[tuple(place)].set(largest)


def level_of(own_key, dims, pieces, low, largest):
    def one(axis_at, blocks):
        draws = jax.random.uniform(jax.random.fold_in(jax.random.fold_in(own_key, 6), axis_at), (blocks,), jnp.float32, low / len(pieces), largest / len(pieces))
        return jnp.repeat(jnp.exp(draws), dims[axis_at] // blocks).reshape((-1,) + (1,) * (len(dims) - axis_at - 1))

    factor_of = one(*pieces[0])
    for cut in pieces[1:]:
        factor_of = factor_of * one(*cut)
    return factor_of


def gaussian(rng, extent, spread, bound, shards=(), kind=jnp.bfloat16):
    values = jax.random.normal(rng, extent, jnp.float32) * spread
    if len(shards) > 0:
        values = level_of(rng, extent, shards, -0.22, 0.18) * values
    return jnp.clip(values, min=-bound, max=bound).astype(kind)


def setup_inputs(seed: int = 0) -> dict:
    seeds = jax.random.split(jax.random.key(seed), 6)
    spectral = gaussian(seeds[0], (2, NZ, NY, NX), 1.0, 6.0, ((1, 16), (2, 4), (3, 8)), jnp.float32)
    shifts = touch_ends(jax.random.randint(seeds[1], (NZ, NY), 0, NX), jax.random.fold_in(seeds[1], 1), 0, NX - 1).astype(jnp.int32)
    colour = touch_ends((jax.random.randint(seeds[2], (NY, NX), 0, 2) < 1).astype(jnp.int32), jax.random.fold_in(seeds[2], 1), 0, 1)
    pressure = draw_pressure(jax.random.fold_in(seeds[5], 71), 0)
    source = draw_source(jax.random.fold_in(seeds[5], 71), 0)
    return {"spectral": spectral, "shifts": shifts, "colour": colour, "pressure": pressure, "source": source}


STORE = 1.0

def spectral_slice(packed):
    coeff_slice, shift_row = packed
    wave_index = jnp.arange(NX, dtype=jnp.int32)
    wave_turns = shift_row[:, None] * wave_index[None, :] % NX
    phase_angle = wave_turns.astype(jnp.float32) * (2.0 * math.pi / NX)
    cosine = jnp.cos(phase_angle)
    sine_part = jnp.sin(phase_angle)
    real_part = coeff_slice[0] * cosine - coeff_slice[1] * sine_part
    imag_part = coeff_slice[0] * sine_part + coeff_slice[1] * cosine
    spectrum = lax.complex(real_part, imag_part)
    return jnp.real(jnp.fft.ifft(spectrum, axis=-1)) * math.sqrt(NX)

def harmonic(center, beside):
    return 2.0 * center * beside / (center + beside)

def thomas(lower_diagonal, main_diagonal, upper_diagonal, right_hand_side):

    def forward_scan(carried_state, row_entries):
        previous_ratio, previous_eliminated = carried_state
        column_lower, main_c, sup_c, column_right_hand = row_entries
        present_denominator = main_c - column_lower * previous_ratio
        present_ratio = sup_c / present_denominator
        present_eliminated = (column_right_hand - column_lower * previous_eliminated) / present_denominator
        return ((present_ratio, present_eliminated), (present_ratio, present_eliminated))
    zeroed_layer = jnp.zeros(right_hand_side.shape[1:], right_hand_side.dtype)
    unused_output, (ratio_rows, eliminated_rows) = lax.scan(forward_scan, (zeroed_layer, zeroed_layer), (lower_diagonal, main_diagonal, upper_diagonal, right_hand_side))

    def backward_scan(following_value, row_entries):
        column_ratio, column_eliminated = row_entries
        present_value = column_eliminated - column_ratio * following_value
        return (present_value, present_value)
    unused_output, solved_values = lax.scan(backward_scan, zeroed_layer, (ratio_rows, eliminated_rows), reverse=True)
    return solved_values

def reference(spectral, shifts, colour, pressure, source):
    vert_factor = float(VERT)
    log_perm = lax.map(spectral_slice, (jnp.moveaxis(spectral, 1, 0), shifts))
    perm = jnp.exp(log_perm)
    padded = jnp.pad(perm, 1)
    w_zm = vert_factor * harmonic(perm, padded[:-2, 1:-1, 1:-1])
    w_zp = vert_factor * harmonic(perm, padded[2:, 1:-1, 1:-1])
    w_ym = harmonic(perm, padded[1:-1, :-2, 1:-1])
    w_yp = harmonic(perm, padded[1:-1, 2:, 1:-1])
    w_xm = harmonic(perm, padded[1:-1, 1:-1, :-2])
    w_xp = harmonic(perm, padded[1:-1, 1:-1, 2:])
    main_diagonal = STORE + w_xm + w_xp + w_ym + w_yp + w_zm + w_zp

    def line_solve(current):
        cycle = jnp.pad(current, ((0, 0), (1, 1), (1, 1)))
        right_hand_side = source + w_xm * cycle[:, 1:-1, :-2] + w_xp * cycle[:, 1:-1, 2:]
        right_hand_side = right_hand_side + w_ym * cycle[:, :-2, 1:-1] + w_yp * cycle[:, 2:, 1:-1]
        return thomas(-w_zm, main_diagonal, -w_zp, right_hand_side)
    half = jnp.where((colour == 0)[None], line_solve(pressure), pressure)
    smoothed = jnp.where((colour == 1)[None], line_solve(half), half)
    return (log_perm, smoothed)
```

```python
import functools
import math

import jax
import jax.numpy as jnp
import ml_dtypes
import numpy as np
from jax import lax
from jax.experimental import pallas as pl
from jax.experimental.pallas import tpu as pltpu
from jax.sharding import PartitionSpec as P

NX = 2048
STORE = 1.0
VERT = 65536.0
MESH = pl.DeviceIdType.MESH
GX = 8
GY = 4
GZ = 16
DEPTH = 32
ITEMS = 8
WIDTH = 256
ROWS = 32
F32 = jnp.float32
BF16 = jnp.bfloat16


def tables():
    j = np.arange(WIDTH)
    angle = 2.0 * np.pi * ((j[:, None] * j[None, :]) % WIDTH) / WIDTH
    dft = np.concatenate([np.cos(angle), -np.sin(angle)], axis=0) / math.sqrt(NX)
    high = dft.astype(ml_dtypes.bfloat16)
    low = (dft - high.astype(np.float64)).astype(ml_dtypes.bfloat16)
    dft_pair = np.stack([high, low])
    r = np.arange(GX)
    turn = 2.0 * np.pi * (r[:, None] * j[None, :]) / NX
    twiddle = np.stack([np.cos(turn), np.sin(turn)]).astype(np.float32)
    order = np.zeros((WIDTH, WIDTH), np.float32)
    for rr in range(8):
        for p in range(32):
            order[32 * rr + p, 8 * p + rr] = 1.0
    return dft_pair, twiddle, order.astype(ml_dtypes.bfloat16)


def cos_sin(turns):
    quadrant = (turns + 256) >> 9
    x = (turns - (quadrant << 9)).astype(F32) * (2.0 * math.pi / NX)
    x2 = x * x
    sine = x * (1.0 + x2 * (-1.0 / 6 + x2 * (1.0 / 120 + x2 * (-1.0 / 5040 + x2 * (1.0 / 362880)))))
    cosine = 1.0 + x2 * (-0.5 + x2 * (1.0 / 24 + x2 * (-1.0 / 720 + x2 * (1.0 / 40320))))
    swap = (quadrant & 1) == 1
    c = jnp.where(swap, sine, cosine)
    s = jnp.where(swap, cosine, sine)
    c = jnp.where(((quadrant + 1) & 2) == 2, -c, c)
    s = jnp.where((quadrant & 2) == 2, -s, s)
    return c, s


def dft4(z):
    (r0, i0), (r1, i1), (r2, i2), (r3, i3) = z
    ar, ai, br, bi = r0 + r2, i0 + i2, r0 - r2, i0 - i2
    cr, ci, dr, di = r1 + r3, i1 + i3, r1 - r3, i1 - i3
    return [(ar + cr, ai + ci), (br - di, bi + dr), (ar - cr, ai - ci), (br + di, bi - dr)]


def dft8(t):
    root = math.sqrt(0.5)
    even = [(t[k][0] + t[k + 4][0], t[k][1] + t[k + 4][1]) for k in range(4)]
    odd = [(t[k][0] - t[k + 4][0], t[k][1] - t[k + 4][1]) for k in range(4)]
    o1 = (root * (odd[1][0] - odd[1][1]), root * (odd[1][0] + odd[1][1]))
    o2 = (-odd[2][1], odd[2][0])
    o3 = (-root * (odd[3][0] + odd[3][1]), root * (odd[3][0] - odd[3][1]))
    ev = dft4(even)
    od = dft4([odd[0], o1, o2, o3])
    out = []
    for m in range(4):
        out += [ev[m], od[m]]
    return out


def split(value):
    high = value.astype(BF16)
    return high, (value - high.astype(F32)).astype(BF16)


def spectral_kernel(
    spec, shifts, dft_hbm, twiddle, order_hbm, out,
    xb, trig, lhs_hi, lhs_lo, zb, wb_hi, wb_lo, sb, dft, order,
    send1, recv1, send2, recv2, local,
):
    me = lax.axis_index("gx")
    barrier = pltpu.get_barrier_semaphore()

    def mine(slot):
        return pl.ds(4 * slot, 4)

    own = pltpu.make_async_copy(spec.at[:, mine(me)], xb.at[me], local.at[0])
    own.start()
    dft_copy = pltpu.make_async_copy(dft_hbm, dft, local.at[1])
    dft_copy.start()
    order_copy = pltpu.make_async_copy(order_hbm, order, local.at[2])
    order_copy.start()
    for i in range(1, GX):
        peer = lax.rem(me + i, GX)
        pl.semaphore_signal(barrier, inc=1, device_id={"gx": peer}, device_id_type=MESH)
    pl.semaphore_wait(barrier, GX - 1)

    def first(peer, slot, who):
        return pltpu.make_async_remote_copy(
            src_ref=spec.at[:, mine(peer)], dst_ref=xb.at[slot],
            send_sem=send1.at[peer], recv_sem=recv1.at[slot],
            device_id={"gx": who}, device_id_type=MESH,
        )

    for i in range(1, GX):
        peer = lax.rem(me + i, GX)
        first(peer, me, peer).start()

    lane = lax.broadcasted_iota(jnp.int32, (8, WIDTH), 1)
    lane1 = lax.broadcasted_iota(jnp.int32, (8, 128), 1)
    sub1 = lax.broadcasted_iota(jnp.int32, (8, 128), 0)
    for z in range(4):
        row = shifts[pl.ds(4 * me + z, 1), :].astype(F32)
        row = jnp.concatenate([row, jnp.zeros((1, 120), F32)], axis=1)
        row = jnp.where(lane1 == sub1, jnp.broadcast_to(row, (8, 128)), 0.0)
        shift = jnp.sum(row, axis=1, keepdims=True).astype(jnp.int32)
        shift = jnp.broadcast_to(shift, (8, WIDTH))

        def make_trig(d, carry, z=z, shift=shift):
            c, s = cos_sin((shift * (lane + d * WIDTH)) & (NX - 1))
            trig[0, d, pl.ds(8 * z, 8), :] = c
            trig[1, d, pl.ds(8 * z, 8), :] = s
            return carry

        lax.fori_loop(0, GX, make_trig, 0)

    own.wait()
    for i in range(1, GX):
        peer = lax.rem(me + GX - i, GX)
        first(peer, peer, peer).wait_recv()

    for zz in range(2):
        rows = pl.ds(16 * zz, 16)
        for h in range(2):
            cols = pl.ds(128 * h, 128)
            t = []
            for d in range(GX):
                xr = xb[d, 0, pl.ds(2 * zz, 2), :, cols].reshape(16, 128)
                xi = xb[d, 1, pl.ds(2 * zz, 2), :, cols].reshape(16, 128)
                c = trig[0, d, rows, cols]
                s = trig[1, d, rows, cols]
                t.append((xr * c - xi * s, xr * s + xi * c))
            y = dft8(t)
            for r in range(8):
                yr, yi = y[r]
                if r > 0:
                    c = twiddle[0, pl.ds(r, 1), cols]
                    s = twiddle[1, pl.ds(r, 1), cols]
                    yr, yi = yr * c - yi * s, yr * s + yi * c
                place = pl.ds(32 * r + 16 * zz, 16)
                hi, lo = split(yr)
                lhs_hi[place, pl.ds(128 * h, 128)] = hi
                lhs_lo[place, pl.ds(128 * h, 128)] = lo
                hi, lo = split(yi)
                lhs_hi[place, pl.ds(256 + 128 * h, 128)] = hi
                lhs_lo[place, pl.ds(256 + 128 * h, 128)] = lo

    dft_copy.wait()
    zb[...] = (
        jnp.dot(lhs_hi[...], dft[0], preferred_element_type=F32)
        + jnp.dot(lhs_hi[...], dft[1], preferred_element_type=F32)
        + jnp.dot(lhs_lo[...], dft[0], preferred_element_type=F32)
    )
    group = lax.broadcasted_iota(jnp.int32, (ROWS, 128), 1) // 32
    for e in range(8):
        column, g = e // 4, e % 4
        for h in range(2):
            total = None
            for rr in range(4):
                r = 4 * h + rr
                tile = zb[pl.ds(32 * r, 32), pl.ds(128 * column, 128)]
                turn = (32 * (rr - g)) % 128
                if turn:
                    tile = pltpu.roll(tile, turn, 1)
                total = tile if total is None else jnp.where(group == rr, tile, total)
            hi, lo = split(total)
            wb_hi[pl.ds(32 * e, 32), pl.ds(128 * h, 128)] = hi
            wb_lo[pl.ds(32 * e, 32), pl.ds(128 * h, 128)] = lo
    order_copy.wait()
    natural = jnp.dot(wb_hi[...], order[...], preferred_element_type=F32) + jnp.dot(
        wb_lo[...], order[...], preferred_element_type=F32
    )
    sb[...] = natural.reshape(8, 4, 8, WIDTH)

    def second(peer, slot, who):
        return pltpu.make_async_remote_copy(
            src_ref=sb.at[peer], dst_ref=out.at[mine(slot)],
            send_sem=send2.at[peer], recv_sem=recv2.at[slot],
            device_id={"gx": who}, device_id_type=MESH,
        )

    for i in range(1, GX):
        peer = lax.rem(me + i, GX)
        second(peer, me, peer).start()
    out[mine(me)] = sb[me]
    for i in range(1, GX):
        peer = lax.rem(me + GX - i, GX)
        second(peer, peer, peer).wait_recv()
    for i in range(1, GX):
        peer = lax.rem(me + i, GX)
        first(peer, me, peer).wait_send()
        second(peer, me, peer).wait_send()


def spectral_call(spectral, shifts):
    dft_pair, twiddle, order = tables()
    vmem = pl.BlockSpec(memory_space=pltpu.VMEM)
    anywhere = pl.BlockSpec(memory_space=pl.ANY)
    return pl.pallas_call(
        spectral_kernel,
        out_shape=jax.ShapeDtypeStruct((DEPTH, ITEMS, WIDTH), F32),
        in_specs=[anywhere, vmem, anywhere, vmem, anywhere],
        out_specs=vmem,
        scratch_shapes=[
            pltpu.VMEM((GX, 2, 4, 8, WIDTH), F32),
            pltpu.VMEM((2, GX, ROWS, WIDTH), F32),
            pltpu.VMEM((256, 512), BF16),
            pltpu.VMEM((256, 512), BF16),
            pltpu.VMEM((256, WIDTH), F32),
            pltpu.VMEM((256, WIDTH), BF16),
            pltpu.VMEM((256, WIDTH), BF16),
            pltpu.VMEM((GX, 4, 8, WIDTH), F32),
            pltpu.VMEM((2, 512, WIDTH), BF16),
            pltpu.VMEM((WIDTH, WIDTH), BF16),
            pltpu.SemaphoreType.DMA((GX,)),
            pltpu.SemaphoreType.DMA((GX,)),
            pltpu.SemaphoreType.DMA((GX,)),
            pltpu.SemaphoreType.DMA((GX,)),
            pltpu.SemaphoreType.DMA((3,)),
        ],
        compiler_params=pltpu.CompilerParams(
            collective_id=0, has_side_effects=True, vmem_limit_bytes=32 << 20
        ),
        name="spectral",
    )(spectral, shifts, jnp.asarray(dft_pair), jnp.asarray(twiddle), jnp.asarray(order))


def harmonic(center, beside):
    return 2.0 * center * beside / (center + beside)


LEVELS = (
    [(n, n - 1, n + 1) for n in range(1, 31, 2)],
    [(n, n - 2, min(n + 2, 31)) for n in range(2, 31, 4)],
    [(n, n - 4, min(n + 4, 31)) for n in range(4, 31, 8)],
    [(8, 0, 16), (24, 16, 31)],
    [(16, 0, 31)],
)


def sweep_kernel(
    log_perm, pressure, source, colour, out,
    perm, half, ww, we, ws, wn, dd, ff, cc, ll, rr, iv,
    xs1, xh1, ys1, yh1, zh, xs2, xh2, ys2, yh2,
    msg, got, ans, sol, msg2, got2, ans2, sol2,
    halo_send, halo_recv, gz_send, gz_recv,
):
    gx = lax.axis_index("gx")
    gy = lax.axis_index("gy")
    gz = lax.axis_index("gz")
    left, right = lax.rem(gx + GX - 1, GX), lax.rem(gx + 1, GX)
    south, north = lax.rem(gy + GY - 1, GY), lax.rem(gy + 1, GY)
    below, above = lax.rem(gz + GZ - 1, GZ), lax.rem(gz + 1, GZ)
    barrier = pltpu.get_barrier_semaphore()
    for who in ({"gx": left}, {"gx": right}, {"gy": south}, {"gy": north}):
        pl.semaphore_signal(barrier, inc=1, device_id=who, device_id_type=MESH)

    def greet(i, carry):
        peer = lax.rem(gz + i, GZ)
        pl.semaphore_signal(barrier, inc=1, device_id={"gz": peer}, device_id_type=MESH)
        return carry

    lax.fori_loop(1, GZ, greet, 0)

    lane1 = lax.broadcasted_iota(jnp.int32, (8, 128), 1)
    lane = lax.broadcasted_iota(jnp.int32, (8, WIDTH), 1)
    sub = lax.broadcasted_iota(jnp.int32, (8, WIDTH), 0)

    def pack(source_ref, slot, xs, ys):
        west = jnp.zeros((8, 128), F32)
        east = jnp.zeros((8, 128), F32)
        for z in range(DEPTH):
            tile = source_ref[z]
            west = jnp.where(lane1 == z, tile[:, 0:1], west)
            east = jnp.where(lane1 == z, tile[:, 255:256], east)
            ys[0, slot, pl.ds(z, 1), :] = tile[0:1, :]
            ys[1, slot, pl.ds(z, 1), :] = tile[7:8, :]
        xs[0, pl.ds(8 * slot, 8), :] = west
        xs[1, pl.ds(8 * slot, 8), :] = east

    def exchange(src, dst, index, who):
        return pltpu.make_async_remote_copy(
            src_ref=src, dst_ref=dst, send_sem=halo_send.at[index], recv_sem=halo_recv.at[index],
            device_id=who, device_id_type=MESH,
        )

    def make_perm(z, carry):
        perm[z] = jnp.exp(log_perm[z])
        return carry

    lax.fori_loop(0, DEPTH, make_perm, 0, unroll=4)
    pack(perm, 0, xs1, ys1)
    pack(pressure, 1, xs1, ys1)
    pl.semaphore_wait(barrier, 4 + GZ - 1)
    halos = [
        exchange(xs1.at[0], xh1.at[1], 0, {"gx": left}),
        exchange(xs1.at[1], xh1.at[0], 1, {"gx": right}),
        exchange(ys1.at[0], yh1.at[1], 2, {"gy": south}),
        exchange(ys1.at[1], yh1.at[0], 3, {"gy": north}),
        exchange(perm.at[0], zh.at[1], 4, {"gz": below}),
        exchange(perm.at[DEPTH - 1], zh.at[0], 5, {"gz": above}),
    ]
    for copy in halos:
        copy.start()
    for copy in halos:
        copy.wait_recv()

    west_open = (gx > 0).astype(F32)
    east_open = (gx < GX - 1).astype(F32)
    south_open = (gy > 0).astype(F32)
    north_open = (gy < GY - 1).astype(F32)

    def beside(value, west, east, lower, upper):
        vw = jnp.where(lane == 0, west, pltpu.roll(value, 1, 1))
        ve = jnp.where(lane == WIDTH - 1, east, pltpu.roll(value, WIDTH - 1, 1))
        vs = jnp.where(sub == 0, lower, pltpu.roll(value, 1, 0))
        vn = jnp.where(sub == 7, upper, pltpu.roll(value, 7, 0))
        return vw, ve, vs, vn

    def edges(z, xh, yh, slot):
        west = xh[0, pl.ds(8 * slot, 8), :][:, z:z + 1]
        east = xh[1, pl.ds(8 * slot, 8), :][:, z:z + 1]
        lower = yh[0, slot, pl.ds(z, 1), :]
        upper = yh[1, slot, pl.ds(z, 1), :]
        return west, east, lower, upper

    for z in range(DEPTH):
        p = perm[z]
        west, east, lower, upper = edges(z, xh1, yh1, 0)
        pw, pe, ps, pn = beside(
            p, west * west_open, east * east_open, lower * south_open, upper * north_open
        )
        aw, ae, as_, an = harmonic(p, pw), harmonic(p, pe), harmonic(p, ps), harmonic(p, pn)
        ww[z], we[z], ws[z], wn[z] = aw, ae, as_, an
        dd[z] = STORE + aw + ae + as_ + an
        vw, ve, vs, vn = beside(pressure[z], *edges(z, xh1, yh1, 1))
        ff[z] = source[z] + aw * vw + ae * ve + as_ * vs + an * vn
        if z < DEPTH - 1:
            cc[z] = VERT * harmonic(p, perm[z + 1])
    top_open = (gz < GZ - 1).astype(F32)
    w_top = VERT * harmonic(perm[DEPTH - 1], zh[1] * top_open)

    for level in LEVELS:
        for n, a, b in level:
            wl, wr, d, f = cc[a], cc[n], dd[n], ff[n]
            inv = 1.0 / (d + wl + wr)
            l, r = wl * inv, wr * inv
            ll[n], rr[n], iv[n] = l, r, inv
            cc[a] = l * wr
            dd[a] = dd[a] + l * d
            dd[b] = dd[b] + r * d
            ff[a] = ff[a] + l * f
            ff[b] = ff[b] + r * f

    def put(ref, kind, value):
        for h in range(2):
            ref[pl.ds(8 * h + kind, 8, stride=16), :] = value[:, 128 * h:128 * h + 128]

    def take(ref, kind):
        return jnp.concatenate(
            [ref[pl.ds(8 * h + kind, 8, stride=16), :] for h in range(2)], axis=1
        )

    def tile(index):
        return pl.ds(pl.multiple_of(8 * index, 8), 8)

    def everyone(src, dst, phase):
        def copy(peer, slot, who):
            return pltpu.make_async_remote_copy(
                src_ref=src.at[tile(peer)], dst_ref=dst.at[tile(slot)],
                send_sem=gz_send.at[phase, peer], recv_sem=gz_recv.at[phase, slot],
                device_id={"gz": who}, device_id_type=MESH,
            )

        def start(i, carry):
            peer = lax.rem(gz + i, GZ)
            copy(peer, gz, peer).start()
            return carry

        def finish(i, carry):
            peer = lax.rem(gz + GZ - i, GZ)
            copy(peer, peer, peer).wait_recv()
            return carry

        def drain(i, carry):
            peer = lax.rem(gz + i, GZ)
            copy(peer, gz, peer).wait_send()
            return carry

        lax.fori_loop(1, GZ, start, 0)
        dst[tile(gz), :] = src[tile(gz), :]
        lax.fori_loop(1, GZ, finish, 0)
        return lambda: lax.fori_loop(1, GZ, drain, 0)

    put(msg, 0, dd[0])
    put(msg, 1, dd[DEPTH - 1])
    put(msg, 2, cc[0])
    put(msg, 3, w_top)
    put(msg, 4, ff[0])
    put(msg, 5, ff[DEPTH - 1])
    drains = [everyone(msg, got, 0)]

    def kind(ref, k):
        return ref[pl.ds(k, GZ, stride=8), :]

    d0, d1, c, w = kind(got, 0), kind(got, 1), kind(got, 2), kind(got, 3)
    f0, f1 = kind(got, 4), kind(got, 5)
    last_inv = 1.0 / (d1 + c + w)
    last_l, last_r = c * last_inv, w * last_inv

    def up(value, step):
        return pltpu.roll(value, step, 0)

    def down(value, step):
        return pltpu.roll(value, GZ - step, 0)

    e = d0 + last_l * d1 + up(last_r * d1, 1)
    b = last_l * w
    a = up(b, 1)
    alphas = []
    for step in (1, 2, 4, 8):
        inv = 1.0 / (e + a + b)
        alpha, beta = a * up(inv, step), b * down(inv, step)
        alphas.append((step, alpha, beta))
        e = e + alpha * up(e, step) + beta * down(e, step)
        if step < 8:
            a, b = alpha * up(a, step), beta * down(b, step)
    final_inv = 1.0 / e

    def reduced(f0, f1, ans):
        f = f0 + last_l * f1 + up(last_r * f1, 1)
        for step, alpha, beta in alphas:
            f = f + alpha * up(f, step) + beta * down(f, step)
        first = f * final_inv
        last = f1 * last_inv + last_l * first + last_r * down(first, 1)
        ans[pl.ds(0, GZ, stride=8), :] = first
        ans[pl.ds(1, GZ, stride=8), :] = last

    msg2[...] = jnp.zeros_like(msg2)
    ans[...] = jnp.zeros_like(ans)
    ans2[...] = jnp.zeros_like(ans2)
    reduced(f0, f1, ans)
    drains.append(everyone(ans, sol, 1))

    def substitute(sol, merge):
        u = {0: take(sol, 0), DEPTH - 1: take(sol, 1)}
        merge(0, u[0])
        merge(DEPTH - 1, u[DEPTH - 1])
        for level in reversed(LEVELS):
            for n, a, b in level:
                u[n] = ff[n] * iv[n] + ll[n] * u[a] + rr[n] * u[b]
                merge(n, u[n])

    tint = colour[...]

    def merge_half(z, u):
        half[z] = jnp.where(tint == 0, u, pressure[z])

    substitute(sol, merge_half)
    pack(half, 0, xs2, ys2)
    halos2 = [
        exchange(xs2.at[0], xh2.at[1], 6, {"gx": left}),
        exchange(xs2.at[1], xh2.at[0], 7, {"gx": right}),
        exchange(ys2.at[0], yh2.at[1], 8, {"gy": south}),
        exchange(ys2.at[1], yh2.at[0], 9, {"gy": north}),
    ]
    for copy in halos2:
        copy.start()
    for copy in halos2:
        copy.wait_recv()
    for z in range(DEPTH):
        vw, ve, vs, vn = beside(half[z], *edges(z, xh2, yh2, 0))
        ff[z] = source[z] + ww[z] * vw + we[z] * ve + ws[z] * vs + wn[z] * vn
    for level in LEVELS:
        for n, a, b in level:
            f = ff[n]
            ff[a] = ff[a] + ll[n] * f
            ff[b] = ff[b] + rr[n] * f
    put(msg2, 0, ff[0])
    put(msg2, 1, ff[DEPTH - 1])
    drains.append(everyone(msg2, got2, 2))
    reduced(kind(got2, 0), kind(got2, 1), ans2)
    drains.append(everyone(ans2, sol2, 3))

    def merge_out(z, u):
        out[z] = jnp.where(tint == 1, u, half[z])

    substitute(sol2, merge_out)
    for copy in halos + halos2:
        copy.wait_send()
    for drain in drains:
        drain()


def sweep_call(log_perm, pressure, source, colour):
    vmem = pl.BlockSpec(memory_space=pltpu.VMEM)
    field = pltpu.VMEM((DEPTH, ITEMS, WIDTH), F32)
    board = pltpu.VMEM((8 * GZ, 128), F32)
    return pl.pallas_call(
        sweep_kernel,
        out_shape=jax.ShapeDtypeStruct((DEPTH, ITEMS, WIDTH), F32),
        in_specs=[vmem] * 4,
        out_specs=vmem,
        scratch_shapes=[field] * 12
        + [
            pltpu.VMEM((2, 16, 128), F32),
            pltpu.VMEM((2, 16, 128), F32),
            pltpu.VMEM((2, 2, DEPTH, WIDTH), F32),
            pltpu.VMEM((2, 2, DEPTH, WIDTH), F32),
            pltpu.VMEM((2, ITEMS, WIDTH), F32),
            pltpu.VMEM((2, 8, 128), F32),
            pltpu.VMEM((2, 8, 128), F32),
            pltpu.VMEM((2, 1, DEPTH, WIDTH), F32),
            pltpu.VMEM((2, 1, DEPTH, WIDTH), F32),
        ]
        + [board] * 8
        + [
            pltpu.SemaphoreType.DMA((10,)),
            pltpu.SemaphoreType.DMA((10,)),
            pltpu.SemaphoreType.DMA((4, GZ)),
            pltpu.SemaphoreType.DMA((4, GZ)),
        ],
        compiler_params=pltpu.CompilerParams(
            collective_id=1, has_side_effects=True, vmem_limit_bytes=32 << 20
        ),
        name="sweep",
    )(log_perm, pressure, source, colour)


def body(spectral, shifts, colour, pressure, source):
    log_perm = spectral_call(spectral, shifts)
    smoothed = sweep_call(log_perm, pressure, source, colour)
    return (log_perm, smoothed)


def solution(mesh):
    in_specs = (
        P(None, "gz", "gy", "gx"),
        P("gz", "gy"),
        P("gy", "gx"),
        P("gz", "gy", "gx"),
        P("gz", "gy", "gx"),
    )
    out_specs = (P("gz", "gy", "gx"), P("gz", "gy", "gx"))
    return jax.shard_map(body, mesh=mesh, in_specs=in_specs, out_specs=out_specs, check_vma=False)
```

```python
import functools
import math

import jax
import jax.numpy as jnp
import ml_dtypes
import numpy as np
from jax import lax
from jax.experimental import pallas as pl
from jax.experimental.pallas import tpu as pltpu
from jax.sharding import PartitionSpec as P

NX = 2048
STORE = 1.0
VERT = 65536.0
MESH = pl.DeviceIdType.MESH
GX = 8
GY = 4
GZ = 16
DEPTH = 32
ITEMS = 8
WIDTH = 256
ROWS = 32
F32 = jnp.float32
BF16 = jnp.bfloat16


def tables():
    j = np.arange(WIDTH)
    angle = 2.0 * np.pi * ((j[:, None] * j[None, :]) % WIDTH) / WIDTH
    dft = np.concatenate([np.cos(angle), -np.sin(angle)], axis=0) / math.sqrt(NX)
    high = dft.astype(ml_dtypes.bfloat16)
    low = (dft - high.astype(np.float64)).astype(ml_dtypes.bfloat16)
    dft_pair = np.stack([high, low])
    r = np.arange(GX)
    turn = 2.0 * np.pi * (r[:, None] * j[None, :]) / NX
    twiddle = np.stack([np.cos(turn), np.sin(turn)]).astype(np.float32)
    order = np.zeros((WIDTH, WIDTH), np.float32)
    for rr in range(8):
        for p in range(32):
            order[32 * rr + p, 8 * p + rr] = 1.0
    return dft_pair, twiddle, order.astype(ml_dtypes.bfloat16)


def cos_sin(turns):
    quadrant = (turns + 256) >> 9
    x = (turns - (quadrant << 9)).astype(F32) * (2.0 * math.pi / NX)
    x2 = x * x
    sine = x * (1.0 + x2 * (-1.0 / 6 + x2 * (1.0 / 120 + x2 * (-1.0 / 5040 + x2 * (1.0 / 362880)))))
    cosine = 1.0 + x2 * (-0.5 + x2 * (1.0 / 24 + x2 * (-1.0 / 720 + x2 * (1.0 / 40320))))
    swap = (quadrant & 1) == 1
    c = jnp.where(swap, sine, cosine)
    s = jnp.where(swap, cosine, sine)
    c = jnp.where(((quadrant + 1) & 2) == 2, -c, c)
    s = jnp.where((quadrant & 2) == 2, -s, s)
    return c, s


def dft4(z):
    (r0, i0), (r1, i1), (r2, i2), (r3, i3) = z
    ar, ai, br, bi = r0 + r2, i0 + i2, r0 - r2, i0 - i2
    cr, ci, dr, di = r1 + r3, i1 + i3, r1 - r3, i1 - i3
    return [(ar + cr, ai + ci), (br - di, bi + dr), (ar - cr, ai - ci), (br + di, bi - dr)]


def dft8(t):
    root = math.sqrt(0.5)
    even = [(t[k][0] + t[k + 4][0], t[k][1] + t[k + 4][1]) for k in range(4)]
    odd = [(t[k][0] - t[k + 4][0], t[k][1] - t[k + 4][1]) for k in range(4)]
    o1 = (root * (odd[1][0] - odd[1][1]), root * (odd[1][0] + odd[1][1]))
    o2 = (-odd[2][1], odd[2][0])
    o3 = (-root * (odd[3][0] + odd[3][1]), root * (odd[3][0] - odd[3][1]))
    ev = dft4(even)
    od = dft4([odd[0], o1, o2, o3])
    out = []
    for m in range(4):
        out += [ev[m], od[m]]
    return out


def split(value):
    high = value.astype(BF16)
    return high, (value - high.astype(F32)).astype(BF16)


def spectral_part(
    spec, shifts, dft_hbm, twiddle_hbm, order_hbm, out,
    xb, trig, lhs_hi, lhs_lo, zb, wb_hi, wb_lo, sb, dft, twiddle, order,
    send1, recv1, send2, recv2, local, greet_all, meanwhile,
):
    me = lax.axis_index("gx")

    def mine(slot):
        return pl.ds(4 * slot, 4)

    own = pltpu.make_async_copy(spec.at[:, mine(me)], xb.at[me], local.at[0])
    own.start()
    dft_copy = pltpu.make_async_copy(dft_hbm, dft, local.at[1])
    dft_copy.start()
    order_copy = pltpu.make_async_copy(order_hbm, order, local.at[2])
    order_copy.start()
    twiddle_copy = pltpu.make_async_copy(twiddle_hbm, twiddle, local.at[3])
    twiddle_copy.start()
    greet_all()

    def first(peer, slot, who):
        return pltpu.make_async_remote_copy(
            src_ref=spec.at[:, mine(peer)], dst_ref=xb.at[slot],
            send_sem=send1.at[peer], recv_sem=recv1.at[slot],
            device_id={"gx": who}, device_id_type=MESH,
        )

    for i in range(1, GX):
        peer = lax.rem(me + i, GX)
        first(peer, me, peer).start()
    meanwhile()

    lane = lax.broadcasted_iota(jnp.int32, (8, WIDTH), 1)
    lane0 = lax.broadcasted_iota(jnp.int32, (ITEMS, DEPTH), 1)
    for z in range(4):
        row = jnp.where(lane0 == 4 * me + z, shifts[...].astype(F32), 0.0)
        shift = jnp.sum(row, axis=1, keepdims=True).astype(jnp.int32)
        shift = jnp.broadcast_to(shift, (8, WIDTH))

        def make_trig(d, carry, z=z, shift=shift):
            c, s = cos_sin((shift * (lane + d * WIDTH)) & (NX - 1))
            trig[0, d, pl.ds(8 * z, 8), :] = c
            trig[1, d, pl.ds(8 * z, 8), :] = s
            return carry

        lax.fori_loop(0, GX, make_trig, 0)

    own.wait()
    for i in range(1, GX):
        peer = lax.rem(me + GX - i, GX)
        first(peer, peer, peer).wait_recv()

    twiddle_copy.wait()
    for zz in range(2):
        rows = pl.ds(16 * zz, 16)
        for h in range(2):
            cols = pl.ds(128 * h, 128)
            t = []
            for d in range(GX):
                xr = xb[d, 0, pl.ds(2 * zz, 2), :, cols].reshape(16, 128)
                xi = xb[d, 1, pl.ds(2 * zz, 2), :, cols].reshape(16, 128)
                c = trig[0, d, rows, cols]
                s = trig[1, d, rows, cols]
                t.append((xr * c - xi * s, xr * s + xi * c))
            y = dft8(t)
            for r in range(8):
                yr, yi = y[r]
                if r > 0:
                    c = twiddle[0, pl.ds(r, 1), cols]
                    s = twiddle[1, pl.ds(r, 1), cols]
                    yr, yi = yr * c - yi * s, yr * s + yi * c
                place = pl.ds(32 * r + 16 * zz, 16)
                hi, lo = split(yr)
                lhs_hi[place, pl.ds(128 * h, 128)] = hi
                lhs_lo[place, pl.ds(128 * h, 128)] = lo
                hi, lo = split(yi)
                lhs_hi[place, pl.ds(256 + 128 * h, 128)] = hi
                lhs_lo[place, pl.ds(256 + 128 * h, 128)] = lo

    dft_copy.wait()
    zb[...] = (
        jnp.dot(lhs_hi[...], dft[0], preferred_element_type=F32)
        + jnp.dot(lhs_hi[...], dft[1], preferred_element_type=F32)
        + jnp.dot(lhs_lo[...], dft[0], preferred_element_type=F32)
    )
    group = lax.broadcasted_iota(jnp.int32, (ROWS, 128), 1) // 32
    for e in range(8):
        column, g = e // 4, e % 4
        for h in range(2):
            total = None
            for rr in range(4):
                r = 4 * h + rr
                tile = zb[pl.ds(32 * r, 32), pl.ds(128 * column, 128)]
                turn = (32 * (rr - g)) % 128
                if turn:
                    tile = pltpu.roll(tile, turn, 1)
                total = tile if total is None else jnp.where(group == rr, tile, total)
            hi, lo = split(total)
            wb_hi[pl.ds(32 * e, 32), pl.ds(128 * h, 128)] = hi
            wb_lo[pl.ds(32 * e, 32), pl.ds(128 * h, 128)] = lo
    order_copy.wait()
    natural = jnp.dot(wb_hi[...], order[...], preferred_element_type=F32) + jnp.dot(
        wb_lo[...], order[...], preferred_element_type=F32
    )
    sb[...] = natural.reshape(8, 4, 8, WIDTH)

    def second(peer, slot, who):
        return pltpu.make_async_remote_copy(
            src_ref=sb.at[peer], dst_ref=out.at[mine(slot)],
            send_sem=send2.at[peer], recv_sem=recv2.at[slot],
            device_id={"gx": who}, device_id_type=MESH,
        )

    for i in range(1, GX):
        peer = lax.rem(me + i, GX)
        second(peer, me, peer).start()
    out[mine(me)] = sb[me]
    for i in range(1, GX):
        peer = lax.rem(me + GX - i, GX)
        second(peer, peer, peer).wait_recv()

    def drain():
        for i in range(1, GX):
            peer = lax.rem(me + i, GX)
            first(peer, me, peer).wait_send()
            second(peer, me, peer).wait_send()

    return drain


def harmonic(center, beside):
    return 2.0 * center * beside / (center + beside)


LEVELS = (
    [(n, n - 1, n + 1) for n in range(1, 31, 2)],
    [(n, n - 2, min(n + 2, 31)) for n in range(2, 31, 4)],
    [(n, n - 4, min(n + 4, 31)) for n in range(4, 31, 8)],
    [(8, 0, 16), (24, 16, 31)],
    [(16, 0, 31)],
)


def field_kernel(
    spec, shifts, dft_hbm, twiddle_hbm, order_hbm, pressure_hbm, source_hbm, colour_hbm,
    log_perm, out, *scratch,
):
    (
        xb, trig, lhs_hi, lhs_lo, zb, wb_hi, wb_lo, sb, dft, twiddle, order,
        send1, recv1, send2, recv2, local,
        pressure, source, colour,
        perm, half, ww, we, ws, wn, dd, ff, cc, ll, rr, iv,
        xs0, xh0, ys0, yh0, xs1, xh1, ys1, yh1, xs2, xh2, ys2, yh2,
        msg, got, ans, sol, msg2, got2, ans2, sol2,
        halo_send, halo_recv, gz_send, gz_recv,
    ) = scratch
    gx = lax.axis_index("gx")
    gy = lax.axis_index("gy")
    gz = lax.axis_index("gz")
    left, right = lax.rem(gx + GX - 1, GX), lax.rem(gx + 1, GX)
    south, north = lax.rem(gy + GY - 1, GY), lax.rem(gy + 1, GY)
    drains = []

    pressure_copy = pltpu.make_async_copy(pressure_hbm, pressure, local.at[4])
    source_copy = pltpu.make_async_copy(source_hbm, source, local.at[5])
    colour_copy = pltpu.make_async_copy(colour_hbm, colour, local.at[6])

    def greet_all():
        barrier = pltpu.get_barrier_semaphore()

        def greet(i, carry):
            peer = lax.rem(gz + i, GZ)
            pl.semaphore_signal(barrier, inc=1, device_id={"gz": peer}, device_id_type=MESH)
            return carry

        lax.fori_loop(1, GZ, greet, 0)
        for i in range(1, GX):
            peer = lax.rem(gx + i, GX)
            pl.semaphore_signal(barrier, inc=1, device_id={"gx": peer}, device_id_type=MESH)
        for who in (south, north):
            pl.semaphore_signal(barrier, inc=1, device_id={"gy": who}, device_id_type=MESH)
        pressure_copy.start()
        source_copy.start()
        colour_copy.start()
        pl.semaphore_wait(barrier, GX - 1 + GZ - 1 + 2)

    lane1 = lax.broadcasted_iota(jnp.int32, (8, 128), 1)
    lane = lax.broadcasted_iota(jnp.int32, (8, WIDTH), 1)
    sub = lax.broadcasted_iota(jnp.int32, (8, WIDTH), 0)

    def pack(source_ref, xs, ys):
        west = jnp.zeros((8, 128), F32)
        east = jnp.zeros((8, 128), F32)
        for z in range(DEPTH):
            tile = source_ref[z]
            west = jnp.where(lane1 == z, tile[:, 0:1], west)
            east = jnp.where(lane1 == z, tile[:, 255:256], east)
            ys[0, pl.ds(z, 1), :] = tile[0:1, :]
            ys[1, pl.ds(z, 1), :] = tile[7:8, :]
        xs[0] = west
        xs[1] = east

    sides = (
        (0, 1, {"gx": left}, gx > 0, gx < GX - 1),
        (1, 0, {"gx": right}, gx < GX - 1, gx > 0),
        (0, 1, {"gy": south}, gy > 0, gy < GY - 1),
        (1, 0, {"gy": north}, gy < GY - 1, gy > 0),
    )

    def halo(phase, xs, xh, ys, yh):
        def copy(k):
            src, dst = (xs, xh) if k < 2 else (ys, yh)
            side, there, who, _, _ = sides[k]
            return pltpu.make_async_remote_copy(
                src_ref=src.at[side], dst_ref=dst.at[there],
                send_sem=halo_send.at[phase, k], recv_sem=halo_recv.at[phase, k],
                device_id=who, device_id_type=MESH,
            )

        def each(which, action):
            for k in range(4):
                pl.when(sides[k][which])(functools.partial(action, k))

        def blank(k):
            dst = xh if k < 2 else yh
            there = sides[k][1]

            def fill():
                dst[there] = jnp.zeros(dst.shape[1:], F32)

            pl.when(jnp.logical_not(sides[k][4]))(fill)

        each(3, lambda k: copy(k).start())
        for k in range(4):
            blank(k)
        drains.append(lambda: each(3, lambda k: copy(k).wait_send()))
        return lambda: each(4, lambda k: copy(k).wait_recv())

    arrived = []

    def meanwhile():
        pressure_copy.wait()
        pack(pressure, xs0, ys0)
        arrived.append(halo(0, xs0, xh0, ys0, yh0))

    drains.append(
        spectral_part(
            spec, shifts, dft_hbm, twiddle_hbm, order_hbm, log_perm,
            xb, trig, lhs_hi, lhs_lo, zb, wb_hi, wb_lo, sb, dft, twiddle, order,
            send1, recv1, send2, recv2, local, greet_all, meanwhile,
        )
    )

    def make_perm(z, carry):
        perm[z] = jnp.exp(log_perm[z])
        return carry

    lax.fori_loop(0, DEPTH, make_perm, 0, unroll=4)
    pack(perm, xs1, ys1)
    wait_perm = halo(1, xs1, xh1, ys1, yh1)
    source_copy.wait()
    colour_copy.wait()
    arrived[0]()
    wait_perm()

    def beside(value, west, east, lower, upper):
        vw = jnp.where(lane == 0, west, pltpu.roll(value, 1, 1))
        ve = jnp.where(lane == WIDTH - 1, east, pltpu.roll(value, WIDTH - 1, 1))
        vs = jnp.where(sub == 0, lower, pltpu.roll(value, 1, 0))
        vn = jnp.where(sub == 7, upper, pltpu.roll(value, 7, 0))
        return vw, ve, vs, vn

    def edges(z, xh, yh):
        west = xh[0][:, z:z + 1]
        east = xh[1][:, z:z + 1]
        lower = yh[0, pl.ds(z, 1), :]
        upper = yh[1, pl.ds(z, 1), :]
        return west, east, lower, upper

    for z in range(DEPTH):
        p = perm[z]
        pw, pe, ps, pn = beside(p, *edges(z, xh1, yh1))
        aw, ae, as_, an = harmonic(p, pw), harmonic(p, pe), harmonic(p, ps), harmonic(p, pn)
        ww[z], we[z], ws[z], wn[z] = aw, ae, as_, an
        dd[z] = STORE + aw + ae + as_ + an
        vw, ve, vs, vn = beside(pressure[z], *edges(z, xh0, yh0))
        ff[z] = source[z] + aw * vw + ae * ve + as_ * vs + an * vn
        if z < DEPTH - 1:
            cc[z] = VERT * harmonic(p, perm[z + 1])

    for level in LEVELS:
        for n, a, b in level:
            wl, wr, d, f = cc[a], cc[n], dd[n], ff[n]
            inv = 1.0 / (d + wl + wr)
            l, r = wl * inv, wr * inv
            ll[n], rr[n], iv[n] = l, r, inv
            cc[a] = l * wr
            dd[a] = dd[a] + l * d
            dd[b] = dd[b] + r * d
            ff[a] = ff[a] + l * f
            ff[b] = ff[b] + r * f

    def put(ref, kind, value):
        for h in range(2):
            ref[pl.ds(8 * h + kind, 8, stride=16), :] = value[:, 128 * h:128 * h + 128]

    def take(ref, kind):
        return jnp.concatenate(
            [ref[pl.ds(8 * h + kind, 8, stride=16), :] for h in range(2)], axis=1
        )

    def tile(index):
        return pl.ds(pl.multiple_of(8 * index, 8), 8)

    def everyone(src, dst, phase):
        def copy(peer, slot, who):
            return pltpu.make_async_remote_copy(
                src_ref=src.at[tile(peer)], dst_ref=dst.at[tile(slot)],
                send_sem=gz_send.at[phase, peer], recv_sem=gz_recv.at[phase, slot],
                device_id={"gz": who}, device_id_type=MESH,
            )

        def start(i, carry):
            peer = lax.rem(gz + i, GZ)
            copy(peer, gz, peer).start()
            return carry

        def finish(i, carry):
            peer = lax.rem(gz + GZ - i, GZ)
            copy(peer, peer, peer).wait_recv()
            return carry

        def drain(i, carry):
            peer = lax.rem(gz + i, GZ)
            copy(peer, gz, peer).wait_send()
            return carry

        lax.fori_loop(1, GZ, start, 0)
        dst[tile(gz), :] = src[tile(gz), :]
        lax.fori_loop(1, GZ, finish, 0)
        return lambda: lax.fori_loop(1, GZ, drain, 0)

    put(msg, 0, dd[0])
    put(msg, 1, dd[DEPTH - 1])
    put(msg, 2, cc[0])
    put(msg, 3, perm[0])
    put(msg, 4, perm[DEPTH - 1])
    put(msg, 5, ff[0])
    put(msg, 6, ff[DEPTH - 1])
    put(msg, 7, ff[0])
    drains.append(everyone(msg, got, 0))

    def kind(ref, k):
        return ref[pl.ds(k, GZ, stride=8), :]

    d0, d1, c, p0, p1 = (kind(got, k) for k in range(5))
    f0, f1 = kind(got, 5), kind(got, 6)
    segment = lax.broadcasted_iota(jnp.int32, (GZ, 128), 0)
    w = jnp.where(segment < GZ - 1, VERT * harmonic(p1, pltpu.roll(p0, GZ - 1, 0)), 0.0)
    last_inv = 1.0 / (d1 + c + w)
    last_l, last_r = c * last_inv, w * last_inv

    def up(value, step):
        return pltpu.roll(value, step, 0)

    def down(value, step):
        return pltpu.roll(value, GZ - step, 0)

    e = d0 + last_l * d1 + up(last_r * d1, 1)
    b = last_l * w
    a = up(b, 1)
    alphas = []
    for step in (1, 2, 4, 8):
        inv = 1.0 / (e + a + b)
        alpha, beta = a * up(inv, step), b * down(inv, step)
        alphas.append((step, alpha, beta))
        e = e + alpha * up(e, step) + beta * down(e, step)
        if step < 8:
            a, b = alpha * up(a, step), beta * down(b, step)
    final_inv = 1.0 / e

    def reduced(f0, f1, ans):
        f = f0 + last_l * f1 + up(last_r * f1, 1)
        for step, alpha, beta in alphas:
            f = f + alpha * up(f, step) + beta * down(f, step)
        first = f * final_inv
        last = f1 * last_inv + last_l * first + last_r * down(first, 1)
        ans[pl.ds(0, GZ, stride=8), :] = first
        ans[pl.ds(1, GZ, stride=8), :] = last

    msg2[...] = jnp.zeros_like(msg2)
    ans[...] = jnp.zeros_like(ans)
    ans2[...] = jnp.zeros_like(ans2)
    reduced(f0, f1, ans)
    drains.append(everyone(ans, sol, 1))

    def substitute(sol, merge):
        u = {0: take(sol, 0), DEPTH - 1: take(sol, 1)}
        merge(0, u[0])
        merge(DEPTH - 1, u[DEPTH - 1])
        for level in reversed(LEVELS):
            for n, a, b in level:
                u[n] = ff[n] * iv[n] + ll[n] * u[a] + rr[n] * u[b]
                merge(n, u[n])

    tint = colour[...]

    def merge_half(z, u):
        half[z] = jnp.where(tint == 0, u, pressure[z])

    substitute(sol, merge_half)
    pack(half, xs2, ys2)
    halo(2, xs2, xh2, ys2, yh2)()
    for z in range(DEPTH):
        vw, ve, vs, vn = beside(half[z], *edges(z, xh2, yh2))
        ff[z] = source[z] + ww[z] * vw + we[z] * ve + ws[z] * vs + wn[z] * vn
    for level in LEVELS:
        for n, a, b in level:
            f = ff[n]
            ff[a] = ff[a] + ll[n] * f
            ff[b] = ff[b] + rr[n] * f
    put(msg2, 0, ff[0])
    put(msg2, 1, ff[DEPTH - 1])
    drains.append(everyone(msg2, got2, 2))
    reduced(kind(got2, 0), kind(got2, 1), ans2)
    drains.append(everyone(ans2, sol2, 3))

    def merge_out(z, u):
        out[z] = jnp.where(tint == 1, u, half[z])

    substitute(sol2, merge_out)
    for drain in drains:
        drain()


def field_call(spectral, shifts, colour, pressure, source):
    dft_pair, twiddle, order = tables()
    vmem = pl.BlockSpec(memory_space=pltpu.VMEM)
    hbm = pl.BlockSpec(memory_space=pltpu.HBM)
    block = (DEPTH, ITEMS, WIDTH)
    field = pltpu.VMEM(block, F32)
    board = pltpu.VMEM((8 * GZ, 128), F32)
    columns = pltpu.VMEM((2, ITEMS, 128), F32)
    rows = pltpu.VMEM((2, DEPTH, WIDTH), F32)
    dma = pltpu.SemaphoreType.DMA
    return pl.pallas_call(
        field_kernel,
        out_shape=[jax.ShapeDtypeStruct(block, F32)] * 2,
        in_specs=[hbm, vmem] + [hbm] * 6,
        out_specs=[vmem, vmem],
        scratch_shapes=[
            pltpu.VMEM((GX, 2, 4, 8, WIDTH), F32),
            pltpu.VMEM((2, GX, ROWS, WIDTH), F32),
            pltpu.VMEM((256, 512), BF16),
            pltpu.VMEM((256, 512), BF16),
            pltpu.VMEM((256, WIDTH), F32),
            pltpu.VMEM((256, WIDTH), BF16),
            pltpu.VMEM((256, WIDTH), BF16),
            pltpu.VMEM((GX, 4, 8, WIDTH), F32),
            pltpu.VMEM((2, 512, WIDTH), BF16),
            pltpu.VMEM((2, GX, WIDTH), F32),
            pltpu.VMEM((WIDTH, WIDTH), BF16),
            dma((GX,)), dma((GX,)), dma((GX,)), dma((GX,)), dma((7,)),
            field, field, pltpu.VMEM((ITEMS, WIDTH), jnp.int32),
        ]
        + [field] * 12
        + [columns, columns, rows, rows] * 3
        + [board] * 8
        + [dma((3, 4)), dma((3, 4)), dma((4, GZ)), dma((4, GZ))],
        compiler_params=pltpu.CompilerParams(
            collective_id=0, has_side_effects=True, vmem_limit_bytes=32 << 20
        ),
        name="field",
    )(
        spectral, shifts.T, jnp.asarray(dft_pair), jnp.asarray(twiddle), jnp.asarray(order),
        pressure, source, colour,
    )


def body(spectral, shifts, colour, pressure, source):
    log_perm, smoothed = field_call(spectral, shifts, colour, pressure, source)
    return (log_perm, smoothed)


def solution(mesh):
    in_specs = (
        P(None, "gz", "gy", "gx"),
        P("gz", "gy"),
        P("gy", "gx"),
        P("gz", "gy", "gx"),
        P("gz", "gy", "gx"),
    )
    out_specs = (P("gz", "gy", "gx"), P("gz", "gy", "gx"))
    return jax.shard_map(body, mesh=mesh, in_specs=in_specs, out_specs=out_specs, check_vma=False)
```

```python
import functools
import math

import jax
import jax.numpy as jnp
import ml_dtypes
import numpy as np
from jax import lax
from jax.experimental import pallas as pl
from jax.experimental.pallas import tpu as pltpu
from jax.sharding import PartitionSpec as P

NX = 2048
STORE = 1.0
VERT = 65536.0
MESH = pl.DeviceIdType.MESH
GX = 8
GY = 4
GZ = 16
DEPTH = 32
ITEMS = 8
WIDTH = 256
ROWS = 32
F32 = jnp.float32
BF16 = jnp.bfloat16


def tables():
    j = np.arange(WIDTH)
    angle = 2.0 * np.pi * ((j[:, None] * j[None, :]) % WIDTH) / WIDTH
    dft = np.concatenate([np.cos(angle), -np.sin(angle)], axis=0) / math.sqrt(NX)
    high = dft.astype(ml_dtypes.bfloat16)
    low = (dft - high.astype(np.float64)).astype(ml_dtypes.bfloat16)
    dft_pair = np.stack([high, low])
    r = np.arange(GX)
    turn = 2.0 * np.pi * (r[:, None] * j[None, :]) / NX
    twiddle = np.stack([np.cos(turn), np.sin(turn)]).astype(np.float32)
    order = np.zeros((WIDTH, WIDTH), np.float32)
    for rr in range(8):
        for p in range(32):
            order[32 * rr + p, 8 * p + rr] = 1.0
    return dft_pair, twiddle, order.astype(ml_dtypes.bfloat16)


def cos_sin(turns):
    quadrant = (turns + 256) >> 9
    x = (turns - (quadrant << 9)).astype(F32) * (2.0 * math.pi / NX)
    x2 = x * x
    sine = x * (1.0 + x2 * (-1.0 / 6 + x2 * (1.0 / 120 + x2 * (-1.0 / 5040 + x2 * (1.0 / 362880)))))
    cosine = 1.0 + x2 * (-0.5 + x2 * (1.0 / 24 + x2 * (-1.0 / 720 + x2 * (1.0 / 40320))))
    swap = (quadrant & 1) == 1
    c = jnp.where(swap, sine, cosine)
    s = jnp.where(swap, cosine, sine)
    c = jnp.where(((quadrant + 1) & 2) == 2, -c, c)
    s = jnp.where((quadrant & 2) == 2, -s, s)
    return c, s


def dft4(z):
    (r0, i0), (r1, i1), (r2, i2), (r3, i3) = z
    ar, ai, br, bi = r0 + r2, i0 + i2, r0 - r2, i0 - i2
    cr, ci, dr, di = r1 + r3, i1 + i3, r1 - r3, i1 - i3
    return [(ar + cr, ai + ci), (br - di, bi + dr), (ar - cr, ai - ci), (br + di, bi - dr)]


def dft8(t):
    root = math.sqrt(0.5)
    even = [(t[k][0] + t[k + 4][0], t[k][1] + t[k + 4][1]) for k in range(4)]
    odd = [(t[k][0] - t[k + 4][0], t[k][1] - t[k + 4][1]) for k in range(4)]
    o1 = (root * (odd[1][0] - odd[1][1]), root * (odd[1][0] + odd[1][1]))
    o2 = (-odd[2][1], odd[2][0])
    o3 = (-root * (odd[3][0] + odd[3][1]), root * (odd[3][0] - odd[3][1]))
    ev = dft4(even)
    od = dft4([odd[0], o1, o2, o3])
    out = []
    for m in range(4):
        out += [ev[m], od[m]]
    return out


def split(value):
    high = value.astype(BF16)
    return high, (value - high.astype(F32)).astype(BF16)


def spectral_part(
    spec, shifts, dft_hbm, twiddle_hbm, order_hbm, out,
    xb, trig, lhs_hi, lhs_lo, zb, wb_hi, wb_lo, sb, dft, twiddle, order,
    send1, recv1, send2, recv2, local, greet_all, meanwhile,
):
    me = lax.axis_index("gx")

    def mine(slot):
        return pl.ds(4 * slot, 4)

    own = pltpu.make_async_copy(spec.at[:, mine(me)], xb.at[me], local.at[0])
    own.start()
    dft_copy = pltpu.make_async_copy(dft_hbm, dft, local.at[1])
    dft_copy.start()
    order_copy = pltpu.make_async_copy(order_hbm, order, local.at[2])
    order_copy.start()
    twiddle_copy = pltpu.make_async_copy(twiddle_hbm, twiddle, local.at[3])
    twiddle_copy.start()
    greet_all()

    def first(peer, slot, who):
        return pltpu.make_async_remote_copy(
            src_ref=spec.at[:, mine(peer)], dst_ref=xb.at[slot],
            send_sem=send1.at[peer], recv_sem=recv1.at[slot],
            device_id={"gx": who}, device_id_type=MESH,
        )

    for i in range(1, GX):
        peer = lax.rem(me + i, GX)
        first(peer, me, peer).start()
    meanwhile()

    lane = lax.broadcasted_iota(jnp.int32, (8, WIDTH), 1)
    lane0 = lax.broadcasted_iota(jnp.int32, (ITEMS, DEPTH), 1)
    for z in range(4):
        row = jnp.where(lane0 == 4 * me + z, shifts[...].astype(F32), 0.0)
        shift = jnp.sum(row, axis=1, keepdims=True).astype(jnp.int32)
        shift = jnp.broadcast_to(shift, (8, WIDTH))

        def make_trig(d, carry, z=z, shift=shift):
            c, s = cos_sin((shift * (lane + d * WIDTH)) & (NX - 1))
            trig[0, d, pl.ds(8 * z, 8), :] = c
            trig[1, d, pl.ds(8 * z, 8), :] = s
            return carry

        lax.fori_loop(0, GX, make_trig, 0)

    own.wait()
    for i in range(1, GX):
        peer = lax.rem(me + GX - i, GX)
        first(peer, peer, peer).wait_recv()

    twiddle_copy.wait()
    for zz in range(2):
        rows = pl.ds(16 * zz, 16)
        for h in range(2):
            cols = pl.ds(128 * h, 128)
            t = []
            for d in range(GX):
                xr = xb[d, 0, pl.ds(2 * zz, 2), :, cols].reshape(16, 128)
                xi = xb[d, 1, pl.ds(2 * zz, 2), :, cols].reshape(16, 128)
                c = trig[0, d, rows, cols]
                s = trig[1, d, rows, cols]
                t.append((xr * c - xi * s, xr * s + xi * c))
            y = dft8(t)
            for r in range(8):
                yr, yi = y[r]
                if r > 0:
                    c = twiddle[0, pl.ds(r, 1), cols]
                    s = twiddle[1, pl.ds(r, 1), cols]
                    yr, yi = yr * c - yi * s, yr * s + yi * c
                place = pl.ds(32 * r + 16 * zz, 16)
                hi, lo = split(yr)
                lhs_hi[place, pl.ds(128 * h, 128)] = hi
                lhs_lo[place, pl.ds(128 * h, 128)] = lo
                hi, lo = split(yi)
                lhs_hi[place, pl.ds(256 + 128 * h, 128)] = hi
                lhs_lo[place, pl.ds(256 + 128 * h, 128)] = lo

    dft_copy.wait()
    zb[...] = (
        jnp.dot(lhs_hi[...], dft[0], preferred_element_type=F32)
        + jnp.dot(lhs_hi[...], dft[1], preferred_element_type=F32)
        + jnp.dot(lhs_lo[...], dft[0], preferred_element_type=F32)
    )
    group = lax.broadcasted_iota(jnp.int32, (ROWS, 128), 1) // 32
    for e in range(8):
        column, g = e // 4, e % 4
        for h in range(2):
            total = None
            for rr in range(4):
                r = 4 * h + rr
                tile = zb[pl.ds(32 * r, 32), pl.ds(128 * column, 128)]
                turn = (32 * (rr - g)) % 128
                if turn:
                    tile = pltpu.roll(tile, turn, 1)
                total = tile if total is None else jnp.where(group == rr, tile, total)
            hi, lo = split(total)
            wb_hi[pl.ds(32 * e, 32), pl.ds(128 * h, 128)] = hi
            wb_lo[pl.ds(32 * e, 32), pl.ds(128 * h, 128)] = lo
    order_copy.wait()
    natural = jnp.dot(wb_hi[...], order[...], preferred_element_type=F32) + jnp.dot(
        wb_lo[...], order[...], preferred_element_type=F32
    )
    sb[...] = natural.reshape(8, 4, 8, WIDTH)

    def second(peer, slot, who):
        return pltpu.make_async_remote_copy(
            src_ref=sb.at[peer], dst_ref=out.at[mine(slot)],
            send_sem=send2.at[peer], recv_sem=recv2.at[slot],
            device_id={"gx": who}, device_id_type=MESH,
        )

    for i in range(1, GX):
        peer = lax.rem(me + i, GX)
        second(peer, me, peer).start()
    out[mine(me)] = sb[me]
    for i in range(1, GX):
        peer = lax.rem(me + GX - i, GX)
        second(peer, peer, peer).wait_recv()

    def drain():
        for i in range(1, GX):
            peer = lax.rem(me + i, GX)
            first(peer, me, peer).wait_send()
            second(peer, me, peer).wait_send()

    return drain


def harmonic(center, beside):
    return 2.0 * center * beside / (center + beside)


LEVELS = (
    [(n, n - 1, n + 1) for n in range(1, 31, 2)],
    [(n, n - 2, min(n + 2, 31)) for n in range(2, 31, 4)],
    [(n, n - 4, min(n + 4, 31)) for n in range(4, 31, 8)],
    [(8, 0, 16), (24, 16, 31)],
    [(16, 0, 31)],
)


def field_kernel(
    spec, shifts, dft_hbm, twiddle_hbm, order_hbm, pressure_hbm, source_hbm, colour_hbm,
    log_perm_hbm, out, *scratch,
):
    (
        xb, trig, lhs_hi, lhs_lo, zb, wb_hi, wb_lo, sb, dft, twiddle, order,
        send1, recv1, send2, recv2, local,
        pressure, source, colour, log_perm,
        perm, half, ww, we, ws, wn, dd, ff, cc, ll, rr, iv,
        xs0, xh0, ys0, yh0, xs1, xh1, ys1, yh1, xs2, xh2, ys2, yh2,
        msg, got, ans, sol, msg2, got2, ans2, sol2,
        halo_send, halo_recv, gz_send, gz_recv,
    ) = scratch
    gx = lax.axis_index("gx")
    gy = lax.axis_index("gy")
    gz = lax.axis_index("gz")
    left, right = lax.rem(gx + GX - 1, GX), lax.rem(gx + 1, GX)
    south, north = lax.rem(gy + GY - 1, GY), lax.rem(gy + 1, GY)
    drains = []

    pressure_copy = pltpu.make_async_copy(pressure_hbm, pressure, local.at[4])
    source_copy = pltpu.make_async_copy(source_hbm, source, local.at[5])
    colour_copy = pltpu.make_async_copy(colour_hbm, colour, local.at[6])

    def greet_all():
        barrier = pltpu.get_barrier_semaphore()

        def greet(i, carry):
            peer = lax.rem(gz + i, GZ)
            pl.semaphore_signal(barrier, inc=1, device_id={"gz": peer}, device_id_type=MESH)
            return carry

        lax.fori_loop(1, GZ, greet, 0)
        for i in range(1, GX):
            peer = lax.rem(gx + i, GX)
            pl.semaphore_signal(barrier, inc=1, device_id={"gx": peer}, device_id_type=MESH)
        for who in (south, north):
            pl.semaphore_signal(barrier, inc=1, device_id={"gy": who}, device_id_type=MESH)
        pressure_copy.start()
        source_copy.start()
        colour_copy.start()
        pl.semaphore_wait(barrier, GX - 1 + GZ - 1 + 2)

    lane1 = lax.broadcasted_iota(jnp.int32, (8, 128), 1)
    lane = lax.broadcasted_iota(jnp.int32, (8, WIDTH), 1)
    sub = lax.broadcasted_iota(jnp.int32, (8, WIDTH), 0)

    def pack(source_ref, xs, ys):
        west = jnp.zeros((8, 128), F32)
        east = jnp.zeros((8, 128), F32)
        for z in range(DEPTH):
            tile = source_ref[z]
            west = jnp.where(lane1 == z, tile[:, 0:1], west)
            east = jnp.where(lane1 == z, tile[:, 255:256], east)
            ys[0, pl.ds(z, 1), :] = tile[0:1, :]
            ys[1, pl.ds(z, 1), :] = tile[7:8, :]
        xs[0] = west
        xs[1] = east

    sides = (
        (0, 1, {"gx": left}, gx > 0, gx < GX - 1),
        (1, 0, {"gx": right}, gx < GX - 1, gx > 0),
        (0, 1, {"gy": south}, gy > 0, gy < GY - 1),
        (1, 0, {"gy": north}, gy < GY - 1, gy > 0),
    )

    def halo(phase, xs, xh, ys, yh):
        def copy(k):
            src, dst = (xs, xh) if k < 2 else (ys, yh)
            side, there, who, _, _ = sides[k]
            return pltpu.make_async_remote_copy(
                src_ref=src.at[side], dst_ref=dst.at[there],
                send_sem=halo_send.at[phase, k], recv_sem=halo_recv.at[phase, k],
                device_id=who, device_id_type=MESH,
            )

        def each(which, action):
            for k in range(4):
                pl.when(sides[k][which])(functools.partial(action, k))

        def blank(k):
            dst = xh if k < 2 else yh
            there = sides[k][1]

            def fill():
                dst[there] = jnp.zeros(dst.shape[1:], F32)

            pl.when(jnp.logical_not(sides[k][4]))(fill)

        each(3, lambda k: copy(k).start())
        for k in range(4):
            blank(k)
        drains.append(lambda: each(3, lambda k: copy(k).wait_send()))
        return lambda: each(4, lambda k: copy(k).wait_recv())

    arrived = []

    def meanwhile():
        pressure_copy.wait()
        pack(pressure, xs0, ys0)
        arrived.append(halo(0, xs0, xh0, ys0, yh0))

    drains.append(
        spectral_part(
            spec, shifts, dft_hbm, twiddle_hbm, order_hbm, log_perm,
            xb, trig, lhs_hi, lhs_lo, zb, wb_hi, wb_lo, sb, dft, twiddle, order,
            send1, recv1, send2, recv2, local, greet_all, meanwhile,
        )
    )

    def make_perm(z, carry):
        perm[z] = jnp.exp(log_perm[z])
        return carry

    log_perm_copy = pltpu.make_async_copy(log_perm, log_perm_hbm, local.at[7])
    log_perm_copy.start()
    drains.append(log_perm_copy.wait)
    lax.fori_loop(0, DEPTH, make_perm, 0, unroll=4)
    pack(perm, xs1, ys1)
    wait_perm = halo(1, xs1, xh1, ys1, yh1)
    source_copy.wait()
    colour_copy.wait()
    arrived[0]()
    wait_perm()

    def beside(value, west, east, lower, upper):
        vw = jnp.where(lane == 0, west, pltpu.roll(value, 1, 1))
        ve = jnp.where(lane == WIDTH - 1, east, pltpu.roll(value, WIDTH - 1, 1))
        vs = jnp.where(sub == 0, lower, pltpu.roll(value, 1, 0))
        vn = jnp.where(sub == 7, upper, pltpu.roll(value, 7, 0))
        return vw, ve, vs, vn

    def edges(z, xh, yh):
        west = xh[0][:, z:z + 1]
        east = xh[1][:, z:z + 1]
        lower = yh[0, pl.ds(z, 1), :]
        upper = yh[1, pl.ds(z, 1), :]
        return west, east, lower, upper

    for z in range(DEPTH):
        p = perm[z]
        pw, pe, ps, pn = beside(p, *edges(z, xh1, yh1))
        aw, ae, as_, an = harmonic(p, pw), harmonic(p, pe), harmonic(p, ps), harmonic(p, pn)
        ww[z], we[z], ws[z], wn[z] = aw, ae, as_, an
        dd[z] = STORE + aw + ae + as_ + an
        vw, ve, vs, vn = beside(pressure[z], *edges(z, xh0, yh0))
        ff[z] = source[z] + aw * vw + ae * ve + as_ * vs + an * vn
        if z < DEPTH - 1:
            cc[z] = VERT * harmonic(p, perm[z + 1])

    for level in LEVELS:
        for n, a, b in level:
            wl, wr, d, f = cc[a], cc[n], dd[n], ff[n]
            inv = 1.0 / (d + wl + wr)
            l, r = wl * inv, wr * inv
            ll[n], rr[n], iv[n] = l, r, inv
            cc[a] = l * wr
            dd[a] = dd[a] + l * d
            dd[b] = dd[b] + r * d
            ff[a] = ff[a] + l * f
            ff[b] = ff[b] + r * f

    def put(ref, kind, value):
        for h in range(2):
            ref[pl.ds(8 * h + kind, 8, stride=16), :] = value[:, 128 * h:128 * h + 128]

    def take(ref, kind):
        return jnp.concatenate(
            [ref[pl.ds(8 * h + kind, 8, stride=16), :] for h in range(2)], axis=1
        )

    def tile(index):
        return pl.ds(pl.multiple_of(8 * index, 8), 8)

    def everyone(src, dst, phase):
        def copy(peer, slot, who):
            return pltpu.make_async_remote_copy(
                src_ref=src.at[tile(peer)], dst_ref=dst.at[tile(slot)],
                send_sem=gz_send.at[phase, peer], recv_sem=gz_recv.at[phase, slot],
                device_id={"gz": who}, device_id_type=MESH,
            )

        def start(i, carry):
            peer = lax.rem(gz + i, GZ)
            copy(peer, gz, peer).start()
            return carry

        def finish(i, carry):
            peer = lax.rem(gz + GZ - i, GZ)
            copy(peer, peer, peer).wait_recv()
            return carry

        def drain(i, carry):
            peer = lax.rem(gz + i, GZ)
            copy(peer, gz, peer).wait_send()
            return carry

        lax.fori_loop(1, GZ, start, 0)
        dst[tile(gz), :] = src[tile(gz), :]
        lax.fori_loop(1, GZ, finish, 0)
        return lambda: lax.fori_loop(1, GZ, drain, 0)

    put(msg, 0, dd[0])
    put(msg, 1, dd[DEPTH - 1])
    put(msg, 2, cc[0])
    put(msg, 3, perm[0])
    put(msg, 4, perm[DEPTH - 1])
    put(msg, 5, ff[0])
    put(msg, 6, ff[DEPTH - 1])
    put(msg, 7, ff[0])
    drains.append(everyone(msg, got, 0))

    def kind(ref, k):
        return ref[pl.ds(k, GZ, stride=8), :]

    d0, d1, c, p0, p1 = (kind(got, k) for k in range(5))
    f0, f1 = kind(got, 5), kind(got, 6)
    segment = lax.broadcasted_iota(jnp.int32, (GZ, 128), 0)
    w = jnp.where(segment < GZ - 1, VERT * harmonic(p1, pltpu.roll(p0, GZ - 1, 0)), 0.0)
    last_inv = 1.0 / (d1 + c + w)
    last_l, last_r = c * last_inv, w * last_inv

    def up(value, step):
        return pltpu.roll(value, step, 0)

    def down(value, step):
        return pltpu.roll(value, GZ - step, 0)

    e = d0 + last_l * d1 + up(last_r * d1, 1)
    b = last_l * w
    a = up(b, 1)
    alphas = []
    for step in (1, 2, 4, 8):
        inv = 1.0 / (e + a + b)
        alpha, beta = a * up(inv, step), b * down(inv, step)
        alphas.append((step, alpha, beta))
        e = e + alpha * up(e, step) + beta * down(e, step)
        if step < 8:
            a, b = alpha * up(a, step), beta * down(b, step)
    final_inv = 1.0 / e

    def reduced(f0, f1, ans):
        f = f0 + last_l * f1 + up(last_r * f1, 1)
        for step, alpha, beta in alphas:
            f = f + alpha * up(f, step) + beta * down(f, step)
        first = f * final_inv
        last = f1 * last_inv + last_l * first + last_r * down(first, 1)
        ans[pl.ds(0, GZ, stride=8), :] = first
        ans[pl.ds(1, GZ, stride=8), :] = last

    msg2[...] = jnp.zeros_like(msg2)
    ans[...] = jnp.zeros_like(ans)
    ans2[...] = jnp.zeros_like(ans2)
    reduced(f0, f1, ans)
    drains.append(everyone(ans, sol, 1))

    def substitute(sol, merge):
        u = {0: take(sol, 0), DEPTH - 1: take(sol, 1)}
        merge(0, u[0])
        merge(DEPTH - 1, u[DEPTH - 1])
        for level in reversed(LEVELS):
            for n, a, b in level:
                u[n] = ff[n] * iv[n] + ll[n] * u[a] + rr[n] * u[b]
                merge(n, u[n])

    tint = colour[...]

    def merge_half(z, u):
        half[z] = jnp.where(tint == 0, u, pressure[z])

    substitute(sol, merge_half)
    pack(half, xs2, ys2)
    halo(2, xs2, xh2, ys2, yh2)()
    for z in range(DEPTH):
        vw, ve, vs, vn = beside(half[z], *edges(z, xh2, yh2))
        ff[z] = source[z] + ww[z] * vw + we[z] * ve + ws[z] * vs + wn[z] * vn
    for level in LEVELS:
        for n, a, b in level:
            f = ff[n]
            ff[a] = ff[a] + ll[n] * f
            ff[b] = ff[b] + rr[n] * f
    put(msg2, 0, ff[0])
    put(msg2, 1, ff[DEPTH - 1])
    drains.append(everyone(msg2, got2, 2))
    reduced(kind(got2, 0), kind(got2, 1), ans2)
    drains.append(everyone(ans2, sol2, 3))

    def merge_out(z, u):
        out[z] = jnp.where(tint == 1, u, half[z])

    substitute(sol2, merge_out)
    for drain in drains:
        drain()


def field_call(spectral, shifts, colour, pressure, source):
    dft_pair, twiddle, order = tables()
    vmem = pl.BlockSpec(memory_space=pltpu.VMEM)
    hbm = pl.BlockSpec(memory_space=pltpu.HBM)
    block = (DEPTH, ITEMS, WIDTH)
    field = pltpu.VMEM(block, F32)
    board = pltpu.VMEM((8 * GZ, 128), F32)
    columns = pltpu.VMEM((2, ITEMS, 128), F32)
    rows = pltpu.VMEM((2, DEPTH, WIDTH), F32)
    dma = pltpu.SemaphoreType.DMA
    return pl.pallas_call(
        field_kernel,
        out_shape=[jax.ShapeDtypeStruct(block, F32)] * 2,
        in_specs=[hbm, vmem] + [hbm] * 6,
        out_specs=[hbm, vmem],
        scratch_shapes=[
            pltpu.VMEM((GX, 2, 4, 8, WIDTH), F32),
            pltpu.VMEM((2, GX, ROWS, WIDTH), F32),
            pltpu.VMEM((256, 512), BF16),
            pltpu.VMEM((256, 512), BF16),
            pltpu.VMEM((256, WIDTH), F32),
            pltpu.VMEM((256, WIDTH), BF16),
            pltpu.VMEM((256, WIDTH), BF16),
            pltpu.VMEM((GX, 4, 8, WIDTH), F32),
            pltpu.VMEM((2, 512, WIDTH), BF16),
            pltpu.VMEM((2, GX, WIDTH), F32),
            pltpu.VMEM((WIDTH, WIDTH), BF16),
            dma((GX,)), dma((GX,)), dma((GX,)), dma((GX,)), dma((8,)),
            field, field, pltpu.VMEM((ITEMS, WIDTH), jnp.int32), field,
        ]
        + [field] * 12
        + [columns, columns, rows, rows] * 3
        + [board] * 8
        + [dma((3, 4)), dma((3, 4)), dma((4, GZ)), dma((4, GZ))],
        compiler_params=pltpu.CompilerParams(
            collective_id=0, has_side_effects=True, vmem_limit_bytes=56 << 20
        ),
        name="field",
    )(
        spectral, shifts.T, jnp.asarray(dft_pair), jnp.asarray(twiddle), jnp.asarray(order),
        pressure, source, colour,
    )


def body(spectral, shifts, colour, pressure, source):
    log_perm, smoothed = field_call(spectral, shifts, colour, pressure, source)
    return (log_perm, smoothed)


def solution(mesh):
    in_specs = (
        P(None, "gz", "gy", "gx"),
        P("gz", "gy"),
        P("gy", "gx"),
        P("gz", "gy", "gx"),
        P("gz", "gy", "gx"),
    )
    out_specs = (P("gz", "gy", "gx"), P("gz", "gy", "gx"))
    return jax.shard_map(body, mesh=mesh, in_specs=in_specs, out_specs=out_specs, check_vma=False)
```

```python
import functools
import math

import jax
import jax.numpy as jnp
import ml_dtypes
import numpy as np
from jax import lax
from jax.experimental import pallas as pl
from jax.experimental.pallas import tpu as pltpu
from jax.sharding import PartitionSpec as P

NX = 2048
STORE = 1.0
VERT = 65536.0
MESH = pl.DeviceIdType.MESH
GX = 8
GY = 4
GZ = 16
DEPTH = 32
ITEMS = 8
WIDTH = 256
ROWS = 32
F32 = jnp.float32
BF16 = jnp.bfloat16


def tables():
    j = np.arange(WIDTH)
    angle = 2.0 * np.pi * ((j[:, None] * j[None, :]) % WIDTH) / WIDTH
    dft = np.concatenate([np.cos(angle), -np.sin(angle)], axis=0) / math.sqrt(NX)
    high = dft.astype(ml_dtypes.bfloat16)
    low = (dft - high.astype(np.float64)).astype(ml_dtypes.bfloat16)
    dft_pair = np.stack([high, low])
    r = np.arange(GX)
    turn = 2.0 * np.pi * (r[:, None] * j[None, :]) / NX
    twiddle = np.stack([np.cos(turn), np.sin(turn)]).astype(np.float32)
    order = np.zeros((WIDTH, WIDTH), np.float32)
    for rr in range(8):
        for p in range(32):
            order[32 * rr + p, 8 * p + rr] = 1.0
    return dft_pair, twiddle, order.astype(ml_dtypes.bfloat16)


def cos_sin(turns):
    quadrant = (turns + 256) >> 9
    x = (turns - (quadrant << 9)).astype(F32) * (2.0 * math.pi / NX)
    x2 = x * x
    sine = x * (1.0 + x2 * (-1.0 / 6 + x2 * (1.0 / 120 + x2 * (-1.0 / 5040 + x2 * (1.0 / 362880)))))
    cosine = 1.0 + x2 * (-0.5 + x2 * (1.0 / 24 + x2 * (-1.0 / 720 + x2 * (1.0 / 40320))))
    swap = (quadrant & 1) == 1
    c = jnp.where(swap, sine, cosine)
    s = jnp.where(swap, cosine, sine)
    c = jnp.where(((quadrant + 1) & 2) == 2, -c, c)
    s = jnp.where((quadrant & 2) == 2, -s, s)
    return c, s


def dft4(z):
    (r0, i0), (r1, i1), (r2, i2), (r3, i3) = z
    ar, ai, br, bi = r0 + r2, i0 + i2, r0 - r2, i0 - i2
    cr, ci, dr, di = r1 + r3, i1 + i3, r1 - r3, i1 - i3
    return [(ar + cr, ai + ci), (br - di, bi + dr), (ar - cr, ai - ci), (br + di, bi - dr)]


def dft8(t):
    root = math.sqrt(0.5)
    even = [(t[k][0] + t[k + 4][0], t[k][1] + t[k + 4][1]) for k in range(4)]
    odd = [(t[k][0] - t[k + 4][0], t[k][1] - t[k + 4][1]) for k in range(4)]
    o1 = (root * (odd[1][0] - odd[1][1]), root * (odd[1][0] + odd[1][1]))
    o2 = (-odd[2][1], odd[2][0])
    o3 = (-root * (odd[3][0] + odd[3][1]), root * (odd[3][0] - odd[3][1]))
    ev = dft4(even)
    od = dft4([odd[0], o1, o2, o3])
    out = []
    for m in range(4):
        out += [ev[m], od[m]]
    return out


def split(value):
    high = value.astype(BF16)
    return high, (value - high.astype(F32)).astype(BF16)


def spectral_part(
    spec, shifts, dft_hbm, twiddle_hbm, order_hbm, out,
    xb, trig, lhs_hi, lhs_lo, zb, wb_hi, wb_lo, sb, dft, twiddle, order,
    send1, recv1, send2, recv2, local, greet_all, meanwhile,
):
    me = lax.axis_index("gx")

    def mine(slot):
        return pl.ds(4 * slot, 4)

    own = pltpu.make_async_copy(spec.at[:, mine(me)], xb.at[me], local.at[0])
    own.start()
    dft_copy = pltpu.make_async_copy(dft_hbm, dft, local.at[1])
    dft_copy.start()
    order_copy = pltpu.make_async_copy(order_hbm, order, local.at[2])
    order_copy.start()
    twiddle_copy = pltpu.make_async_copy(twiddle_hbm, twiddle, local.at[3])
    twiddle_copy.start()
    greet_all()

    def first(peer, slot, who):
        return pltpu.make_async_remote_copy(
            src_ref=spec.at[:, mine(peer)], dst_ref=xb.at[slot],
            send_sem=send1.at[peer], recv_sem=recv1.at[slot],
            device_id={"gx": who}, device_id_type=MESH,
        )

    for i in range(1, GX):
        peer = lax.rem(me + i, GX)
        first(peer, me, peer).start()
    meanwhile()

    lane = lax.broadcasted_iota(jnp.int32, (8, WIDTH), 1)
    lane0 = lax.broadcasted_iota(jnp.int32, (ITEMS, DEPTH), 1)
    for z in range(4):
        row = jnp.where(lane0 == 4 * me + z, shifts[...].astype(F32), 0.0)
        shift = jnp.sum(row, axis=1, keepdims=True).astype(jnp.int32)
        shift = jnp.broadcast_to(shift, (8, WIDTH))

        def make_trig(d, carry, z=z, shift=shift):
            c, s = cos_sin((shift * (lane + d * WIDTH)) & (NX - 1))
            trig[0, d, pl.ds(8 * z, 8), :] = c
            trig[1, d, pl.ds(8 * z, 8), :] = s
            return carry

        lax.fori_loop(0, GX, make_trig, 0)

    own.wait()
    for i in range(1, GX):
        peer = lax.rem(me + GX - i, GX)
        first(peer, peer, peer).wait_recv()

    twiddle_copy.wait()
    for zz in range(2):
        rows = pl.ds(16 * zz, 16)
        for h in range(2):
            cols = pl.ds(128 * h, 128)
            t = []
            for d in range(GX):
                xr = xb[d, 0, pl.ds(2 * zz, 2), :, cols].reshape(16, 128)
                xi = xb[d, 1, pl.ds(2 * zz, 2), :, cols].reshape(16, 128)
                c = trig[0, d, rows, cols]
                s = trig[1, d, rows, cols]
                t.append((xr * c - xi * s, xr * s + xi * c))
            y = dft8(t)
            for r in range(8):
                yr, yi = y[r]
                if r > 0:
                    c = twiddle[0, pl.ds(r, 1), cols]
                    s = twiddle[1, pl.ds(r, 1), cols]
                    yr, yi = yr * c - yi * s, yr * s + yi * c
                place = pl.ds(32 * r + 16 * zz, 16)
                hi, lo = split(yr)
                lhs_hi[place, pl.ds(128 * h, 128)] = hi
                lhs_lo[place, pl.ds(128 * h, 128)] = lo
                hi, lo = split(yi)
                lhs_hi[place, pl.ds(256 + 128 * h, 128)] = hi
                lhs_lo[place, pl.ds(256 + 128 * h, 128)] = lo

    dft_copy.wait()
    zb[...] = (
        jnp.dot(lhs_hi[...], dft[0], preferred_element_type=F32)
        + jnp.dot(lhs_hi[...], dft[1], preferred_element_type=F32)
        + jnp.dot(lhs_lo[...], dft[0], preferred_element_type=F32)
    )
    group = lax.broadcasted_iota(jnp.int32, (ROWS, 128), 1) // 32
    for e in range(8):
        column, g = e // 4, e % 4
        for h in range(2):
            total = None
            for rr in range(4):
                r = 4 * h + rr
                tile = zb[pl.ds(32 * r, 32), pl.ds(128 * column, 128)]
                turn = (32 * (rr - g)) % 128
                if turn:
                    tile = pltpu.roll(tile, turn, 1)
                total = tile if total is None else jnp.where(group == rr, tile, total)
            hi, lo = split(total)
            wb_hi[pl.ds(32 * e, 32), pl.ds(128 * h, 128)] = hi
            wb_lo[pl.ds(32 * e, 32), pl.ds(128 * h, 128)] = lo
    order_copy.wait()
    natural = jnp.dot(wb_hi[...], order[...], preferred_element_type=F32) + jnp.dot(
        wb_lo[...], order[...], preferred_element_type=F32
    )
    sb[...] = natural.reshape(8, 4, 8, WIDTH)

    def second(peer, slot, who):
        return pltpu.make_async_remote_copy(
            src_ref=sb.at[peer], dst_ref=out.at[mine(slot)],
            send_sem=send2.at[peer], recv_sem=recv2.at[slot],
            device_id={"gx": who}, device_id_type=MESH,
        )

    for i in range(1, GX):
        peer = lax.rem(me + i, GX)
        second(peer, me, peer).start()
    out[mine(me)] = sb[me]
    for i in range(1, GX):
        peer = lax.rem(me + GX - i, GX)
        second(peer, peer, peer).wait_recv()

    def drain():
        for i in range(1, GX):
            peer = lax.rem(me + i, GX)
            first(peer, me, peer).wait_send()
            second(peer, me, peer).wait_send()

    return drain


def harmonic(center, beside):
    return 2.0 * center * beside / (center + beside)


LEVELS = (
    [(n, n - 1, n + 1) for n in range(1, 31, 2)],
    [(n, n - 2, min(n + 2, 31)) for n in range(2, 31, 4)],
    [(n, n - 4, min(n + 4, 31)) for n in range(4, 31, 8)],
    [(8, 0, 16), (24, 16, 31)],
    [(16, 0, 31)],
)


def field_kernel(
    spec, shifts_hbm, dft_hbm, twiddle_hbm, order_hbm, pressure_hbm, source_hbm, colour_hbm,
    log_perm, out, *scratch,
):
    (
        xb, trig, lhs_hi, lhs_lo, zb, wb_hi, wb_lo, sb, dft, twiddle, order,
        send1, recv1, send2, recv2, local,
        pressure, source, colour, shifts,
        perm, half, ww, we, ws, wn, dd, ff, cc, ll, rr, iv,
        xs0, xh0, ys0, yh0, xs1, xh1, ys1, yh1, xs2, xh2, ys2, yh2,
        msg, got, ans, sol, gains, taken, chain, sums, others,
        halo_send, halo_recv, gz_send, gz_recv,
    ) = scratch
    gx = lax.axis_index("gx")
    gy = lax.axis_index("gy")
    gz = lax.axis_index("gz")
    left, right = lax.rem(gx + GX - 1, GX), lax.rem(gx + 1, GX)
    south, north = lax.rem(gy + GY - 1, GY), lax.rem(gy + 1, GY)
    drains = []

    pressure_copy = pltpu.make_async_copy(pressure_hbm, pressure, local.at[4])
    source_copy = pltpu.make_async_copy(source_hbm, source, local.at[5])
    shifts_copy = pltpu.make_async_copy(shifts_hbm, shifts, local.at[7])
    colour_copy = pltpu.make_async_copy(colour_hbm, colour, local.at[6])

    def greet_all():
        barrier = pltpu.get_barrier_semaphore()

        def greet(i, carry):
            peer = lax.rem(gz + i, GZ)
            pl.semaphore_signal(barrier, inc=1, device_id={"gz": peer}, device_id_type=MESH)
            return carry

        lax.fori_loop(1, GZ, greet, 0)
        for i in range(1, GX):
            peer = lax.rem(gx + i, GX)
            pl.semaphore_signal(barrier, inc=1, device_id={"gx": peer}, device_id_type=MESH)
        for who in (south, north):
            pl.semaphore_signal(barrier, inc=1, device_id={"gy": who}, device_id_type=MESH)
        shifts_copy.start()
        pressure_copy.start()
        source_copy.start()
        colour_copy.start()
        pl.semaphore_wait(barrier, GX - 1 + GZ - 1 + 2)

    lane1 = lax.broadcasted_iota(jnp.int32, (8, 128), 1)
    lane = lax.broadcasted_iota(jnp.int32, (8, WIDTH), 1)
    sub = lax.broadcasted_iota(jnp.int32, (8, WIDTH), 0)

    def pack(source_ref, xs, ys):
        west = jnp.zeros((8, 128), F32)
        east = jnp.zeros((8, 128), F32)
        for z in range(DEPTH):
            tile = source_ref[z]
            west = jnp.where(lane1 == z, tile[:, 0:1], west)
            east = jnp.where(lane1 == z, tile[:, 255:256], east)
            ys[0, pl.ds(z, 1), :] = tile[0:1, :]
            ys[1, pl.ds(z, 1), :] = tile[7:8, :]
        xs[0] = west
        xs[1] = east

    sides = (
        (0, 1, {"gx": left}, gx > 0, gx < GX - 1),
        (1, 0, {"gx": right}, gx < GX - 1, gx > 0),
        (0, 1, {"gy": south}, gy > 0, gy < GY - 1),
        (1, 0, {"gy": north}, gy < GY - 1, gy > 0),
    )

    def halo(phase, xs, xh, ys, yh):
        def copy(k):
            src, dst = (xs, xh) if k < 2 else (ys, yh)
            side, there, who, _, _ = sides[k]
            return pltpu.make_async_remote_copy(
                src_ref=src.at[side], dst_ref=dst.at[there],
                send_sem=halo_send.at[phase, k], recv_sem=halo_recv.at[phase, k],
                device_id=who, device_id_type=MESH,
            )

        def each(which, action):
            for k in range(4):
                pl.when(sides[k][which])(functools.partial(action, k))

        def blank(k):
            dst = xh if k < 2 else yh
            there = sides[k][1]

            def fill():
                dst[there] = jnp.zeros(dst.shape[1:], F32)

            pl.when(jnp.logical_not(sides[k][4]))(fill)

        each(3, lambda k: copy(k).start())
        for k in range(4):
            blank(k)
        drains.append(lambda: each(3, lambda k: copy(k).wait_send()))
        return lambda: each(4, lambda k: copy(k).wait_recv())

    arrived = []

    def meanwhile():
        pressure_copy.wait()
        pack(pressure, xs0, ys0)
        arrived.append(halo(0, xs0, xh0, ys0, yh0))
        shifts_copy.wait()

    drains.append(
        spectral_part(
            spec, shifts, dft_hbm, twiddle_hbm, order_hbm, log_perm,
            xb, trig, lhs_hi, lhs_lo, zb, wb_hi, wb_lo, sb, dft, twiddle, order,
            send1, recv1, send2, recv2, local, greet_all, meanwhile,
        )
    )

    def make_perm(z, carry):
        perm[z] = jnp.exp(log_perm[z])
        return carry

    lax.fori_loop(0, DEPTH, make_perm, 0, unroll=4)
    pack(perm, xs1, ys1)
    wait_perm = halo(1, xs1, xh1, ys1, yh1)
    source_copy.wait()
    colour_copy.wait()
    arrived[0]()
    wait_perm()

    def beside(value, west, east, lower, upper):
        vw = jnp.where(lane == 0, west, pltpu.roll(value, 1, 1))
        ve = jnp.where(lane == WIDTH - 1, east, pltpu.roll(value, WIDTH - 1, 1))
        vs = jnp.where(sub == 0, lower, pltpu.roll(value, 1, 0))
        vn = jnp.where(sub == 7, upper, pltpu.roll(value, 7, 0))
        return vw, ve, vs, vn

    def edges(z, xh, yh):
        west = xh[0][:, z:z + 1]
        east = xh[1][:, z:z + 1]
        lower = yh[0, pl.ds(z, 1), :]
        upper = yh[1, pl.ds(z, 1), :]
        return west, east, lower, upper

    for z in range(DEPTH):
        p = perm[z]
        pw, pe, ps, pn = beside(p, *edges(z, xh1, yh1))
        aw, ae, as_, an = harmonic(p, pw), harmonic(p, pe), harmonic(p, ps), harmonic(p, pn)
        ww[z], we[z], ws[z], wn[z] = aw, ae, as_, an
        dd[z] = STORE + aw + ae + as_ + an
        vw, ve, vs, vn = beside(pressure[z], *edges(z, xh0, yh0))
        ff[z] = source[z] + aw * vw + ae * ve + as_ * vs + an * vn
        if z < DEPTH - 1:
            cc[z] = VERT * harmonic(p, perm[z + 1])

    for level in LEVELS:
        for n, a, b in level:
            wl, wr, d, f = cc[a], cc[n], dd[n], ff[n]
            inv = 1.0 / (d + wl + wr)
            l, r = wl * inv, wr * inv
            ll[n], rr[n], iv[n] = l, r, inv
            cc[a] = l * wr
            dd[a] = dd[a] + l * d
            dd[b] = dd[b] + r * d
            ff[a] = ff[a] + l * f
            ff[b] = ff[b] + r * f

    def put(ref, kind, value):
        for h in range(2):
            ref[pl.ds(8 * h + kind, 8, stride=16), :] = value[:, 128 * h:128 * h + 128]

    def take(ref, kind):
        return jnp.concatenate(
            [ref[pl.ds(8 * h + kind, 8, stride=16), :] for h in range(2)], axis=1
        )

    def everyone(src, dst, phase, size):
        def tile(index):
            return pl.ds(pl.multiple_of(size * index, 8), size)

        def copy(peer, slot):
            return pltpu.make_async_remote_copy(
                src_ref=src.at[tile(peer)], dst_ref=dst.at[tile(slot)],
                send_sem=gz_send.at[phase, peer], recv_sem=gz_recv.at[phase, slot],
                device_id={"gz": peer}, device_id_type=MESH,
            )

        def start(i, carry):
            peer = lax.rem(gz + i, GZ)
            copy(peer, gz).start()
            return carry

        def finish(i, carry):
            peer = lax.rem(gz + GZ - i, GZ)
            copy(peer, peer).wait_recv()
            return carry

        def drain(i, carry):
            peer = lax.rem(gz + i, GZ)
            copy(peer, gz).wait_send()
            return carry

        lax.fori_loop(1, GZ, start, 0)
        dst[tile(gz), :] = src[tile(gz), :]
        drains.append(lambda: lax.fori_loop(1, GZ, drain, 0))
        return lambda: lax.fori_loop(1, GZ, finish, 0)

    put(msg, 0, dd[0])
    put(msg, 1, dd[DEPTH - 1])
    put(msg, 2, cc[0])
    put(msg, 3, perm[0])
    put(msg, 4, perm[DEPTH - 1])
    put(msg, 5, ff[0])
    put(msg, 6, ff[DEPTH - 1])
    put(msg, 7, ff[0])
    everyone(msg, got, 0, 8)()

    def kind(ref, k):
        return ref[pl.ds(k, GZ, stride=8), :]

    d0, d1, c, p0, p1 = (kind(got, k) for k in range(5))
    f0, f1 = kind(got, 5), kind(got, 6)
    segment = lax.broadcasted_iota(jnp.int32, (GZ, 128), 0)
    w = jnp.where(segment < GZ - 1, VERT * harmonic(p1, pltpu.roll(p0, GZ - 1, 0)), 0.0)
    last_inv = 1.0 / (d1 + c + w)
    last_l, last_r = c * last_inv, w * last_inv

    def up(value, step):
        return pltpu.roll(value, step, 0)

    def down(value, step):
        return pltpu.roll(value, GZ - step, 0)

    e = d0 + last_l * d1 + up(last_r * d1, 1)
    b = last_l * w
    a = up(b, 1)
    f = f0 + last_l * f1 + up(last_r * f1, 1)
    for step in (1, 2, 4, 8):
        inv = 1.0 / (e + a + b)
        alpha, beta = a * up(inv, step), b * down(inv, step)
        e = e + alpha * up(e, step) + beta * down(e, step)
        f = f + alpha * up(f, step) + beta * down(f, step)
        if step < 8:
            a, b = alpha * up(a, step), beta * down(b, step)
    first = f / e
    ans[...] = jnp.zeros_like(ans)
    ans[pl.ds(0, GZ, stride=8), :] = first
    ans[pl.ds(1, GZ, stride=8), :] = (
        f1 * last_inv + last_l * first + last_r * down(first, 1)
    )
    wait_sol = everyone(ans, sol, 1, 8)

    links = [jnp.zeros((1, 128), F32)] * 2
    for i in range(GZ):
        j = GZ - 1 - i
        eb, et = links
        at_i, at_j = pl.ds(i, 1), pl.ds(j, 1)
        chain[2, at_i, :] = eb
        chain[5, at_j, :] = et
        low = d0[i:i + 1] + eb
        rho = c[i:i + 1] / (low + c[i:i + 1])
        low = d1[i:i + 1] + rho * low
        tau = w[i:i + 1] / (low + w[i:i + 1])
        chain[0, at_i, :] = rho
        chain[1, at_i, :] = tau
        high = d1[j:j + 1] + et
        sigma = c[j:j + 1] / (high + c[j:j + 1])
        high = d0[j:j + 1] + sigma * high
        chain[3, at_j, :] = sigma
        if j > 0:
            upsilon = w[j - 1:j] / (high + w[j - 1:j])
            chain[4, pl.ds(j - 1, 1), :] = upsilon
        links = [tau * low, upsilon * high]
    chain[4, pl.ds(GZ - 1, 1), :] = jnp.zeros((1, 128), F32)
    tau, upsilon = chain[1], chain[4]
    climb = up(tau * chain[0], 1)
    descend = upsilon * down(chain[3], 1)
    from_below, from_above = [None, up(tau, 1)], [None, upsilon]
    for k in range(2, GZ):
        from_below.append(climb * up(from_below[-1], 1))
        from_above.append(descend * down(from_above[-1], 1))
    gains[...] = jnp.zeros_like(gains)
    for k in range(1, GZ):
        gains[pl.ds(k, GZ, stride=24), :] = from_below[k] + from_above[GZ - k]
    gains[pl.ds(GZ, GZ, stride=24), :] = chain[2]
    gains[pl.ds(GZ + 1, GZ, stride=24), :] = chain[5]
    wait_gains = everyone(gains, taken, 2, 24)
    wait_sol()

    def substitute(first, last, merge):
        u = {0: first, DEPTH - 1: last}
        merge(0, u[0])
        merge(DEPTH - 1, u[DEPTH - 1])
        for level in reversed(LEVELS):
            for n, a, b in level:
                u[n] = ff[n] * iv[n] + ll[n] * u[a] + rr[n] * u[b]
                merge(n, u[n])

    tint = colour[...]

    def merge_half(z, u):
        half[z] = jnp.where(tint == 0, u, pressure[z])

    substitute(take(sol, 0), take(sol, 1), merge_half)
    pack(half, xs2, ys2)
    wait_half = halo(2, xs2, xh2, ys2, yh2)

    def gain(k):
        return jnp.concatenate(
            [taken[pl.ds(24 * h + k, 8, stride=48), :] for h in range(2)], axis=1
        )

    wait_gains()
    c = cc[0]
    low = dd[0] + gain(GZ)
    high = dd[DEPTH - 1] + gain(GZ + 1)
    low_inv = 1.0 / (low + c)
    rho = c * low_inv
    sigma = c / (high + c)
    high_inv = 1.0 / (high + rho * low)
    wait_half()
    for z in range(DEPTH):
        vw, ve, vs, vn = beside(half[z], *edges(z, xh2, yh2))
        ff[z] = source[z] + ww[z] * vw + we[z] * ve + ws[z] * vs + wn[z] * vn
    for level in LEVELS:
        for n, a, b in level:
            f = ff[n]
            ff[a] = ff[a] + ll[n] * f
            ff[b] = ff[b] + rr[n] * f
    f0, f1 = ff[0], ff[DEPTH - 1]
    sums[0] = f1 + rho * f0
    sums[1] = f0 + sigma * f1

    def cast(i):
        peer = lax.rem(gz + i, GZ)
        return pltpu.make_async_remote_copy(
            src_ref=sums.at[lax.div(gz + i, GZ)], dst_ref=others.at[gz],
            send_sem=gz_send.at[3, peer], recv_sem=gz_recv.at[3, gz],
            device_id={"gz": peer}, device_id_type=MESH,
        )

    def heard(i):
        peer = lax.rem(gz + GZ - i, GZ)
        return pltpu.make_async_remote_copy(
            src_ref=sums.at[0], dst_ref=others.at[peer],
            send_sem=gz_send.at[3, peer], recv_sem=gz_recv.at[3, peer],
            device_id={"gz": peer}, device_id_type=MESH,
        )

    def start_cast(i, carry):
        cast(i).start()
        return carry

    def drain_cast(i, carry):
        cast(i).wait_send()
        return carry

    def wait_heard(i, carry):
        heard(i).wait_recv()
        return carry

    lax.fori_loop(1, GZ, start_cast, 0)
    drains.append(lambda: lax.fori_loop(1, GZ, drain_cast, 0))
    lax.fori_loop(1, GZ, wait_heard, 0)
    for i in range(1, GZ):
        part = gain(i) * others[lax.rem(gz + GZ - i, GZ)]
        f0 = f0 + jnp.where(gz >= i, part, 0.0)
        f1 = f1 + jnp.where(gz >= i, 0.0, part)
    last = (f1 + rho * f0) * high_inv
    first = f0 * low_inv + rho * last

    def merge_out(z, u):
        out[z] = jnp.where(tint == 1, u, half[z])

    substitute(first, last, merge_out)
    for drain in drains:
        drain()


def pin(value):
    return pltpu.with_memory_space_constraint(value, pltpu.HBM)


def field_call(spectral, shifts, colour, pressure, source):
    vmem = pl.BlockSpec(memory_space=pltpu.VMEM)
    hbm = pl.BlockSpec(memory_space=pltpu.HBM)
    block = (DEPTH, ITEMS, WIDTH)
    field = pltpu.VMEM(block, F32)
    board = pltpu.VMEM((8 * GZ, 128), F32)
    columns = pltpu.VMEM((2, ITEMS, 128), F32)
    rows = pltpu.VMEM((2, DEPTH, WIDTH), F32)
    dma = pltpu.SemaphoreType.DMA
    return pl.pallas_call(
        field_kernel,
        out_shape=[jax.ShapeDtypeStruct(block, F32)] * 2,
        in_specs=[hbm] * 8,
        out_specs=[vmem, vmem],
        scratch_shapes=[
            pltpu.VMEM((GX, 2, 4, 8, WIDTH), F32),
            pltpu.VMEM((2, GX, ROWS, WIDTH), F32),
            pltpu.VMEM((256, 512), BF16),
            pltpu.VMEM((256, 512), BF16),
            pltpu.VMEM((256, WIDTH), F32),
            pltpu.VMEM((256, WIDTH), BF16),
            pltpu.VMEM((256, WIDTH), BF16),
            pltpu.VMEM((GX, 4, 8, WIDTH), F32),
            pltpu.VMEM((2, 512, WIDTH), BF16),
            pltpu.VMEM((2, GX, WIDTH), F32),
            pltpu.VMEM((WIDTH, WIDTH), BF16),
            dma((GX,)), dma((GX,)), dma((GX,)), dma((GX,)), dma((8,)),
            field, field, pltpu.VMEM((ITEMS, WIDTH), jnp.int32),
            pltpu.VMEM((ITEMS, DEPTH), jnp.int32),
        ]
        + [field] * 12
        + [columns, columns, rows, rows] * 3
        + [board] * 4
        + [
            pltpu.VMEM((24 * GZ, 128), F32),
            pltpu.VMEM((24 * GZ, 128), F32),
            pltpu.VMEM((6, GZ, 128), F32),
            pltpu.VMEM((2, ITEMS, WIDTH), F32),
            pltpu.VMEM((GZ, ITEMS, WIDTH), F32),
        ]
        + [dma((3, 4)), dma((3, 4)), dma((4, GZ)), dma((4, GZ))],
        compiler_params=pltpu.CompilerParams(
            collective_id=0, has_side_effects=True, vmem_limit_bytes=32 << 20
        ),
        name="field",
    )(
        *map(pin, (spectral, shifts.T, *map(jnp.asarray, tables()), pressure, source, colour))
    )


def body(spectral, shifts, colour, pressure, source):
    log_perm, smoothed = field_call(spectral, shifts, colour, pressure, source)
    return (log_perm, smoothed)


def solution(mesh):
    in_specs = (
        P(None, "gz", "gy", "gx"),
        P("gz", "gy"),
        P("gy", "gx"),
        P("gz", "gy", "gx"),
        P("gz", "gy", "gx"),
    )
    out_specs = (P("gz", "gy", "gx"), P("gz", "gy", "gx"))
    return jax.shard_map(body, mesh=mesh, in_specs=in_specs, out_specs=out_specs, check_vma=False)
```

```python
import functools
import math

import jax
import jax.numpy as jnp
import ml_dtypes
import numpy as np
from jax import lax
from jax.experimental import pallas as pl
from jax.experimental.pallas import tpu as pltpu
from jax.sharding import PartitionSpec as P

NX = 2048
STORE = 1.0
VERT = 65536.0
MESH = pl.DeviceIdType.MESH
GX = 8
GY = 4
GZ = 16
DEPTH = 32
ITEMS = 8
WIDTH = 256
ROWS = 32
FAR_FIRST = (9, 7, 11, 5, 13, 3, 8, 15, 1, 10, 6, 12, 4, 14, 2)
ROUND_FIRST = (8, 6, 10, 4, 12, 2, 14)
F32 = jnp.float32
BF16 = jnp.bfloat16


def tables():
    j = np.arange(WIDTH)
    angle = 2.0 * np.pi * ((j[:, None] * j[None, :]) % WIDTH) / WIDTH
    dft = np.concatenate([np.cos(angle), -np.sin(angle)], axis=0) / math.sqrt(NX)
    high = dft.astype(ml_dtypes.bfloat16)
    low = (dft - high.astype(np.float64)).astype(ml_dtypes.bfloat16)
    dft_pair = np.stack([high, low])
    r = np.arange(GX)
    turn = 2.0 * np.pi * (r[:, None] * j[None, :]) / NX
    twiddle = np.stack([np.cos(turn), np.sin(turn)]).astype(np.float32)
    order = np.zeros((WIDTH, WIDTH), np.float32)
    for rr in range(8):
        for p in range(32):
            order[32 * rr + p, 8 * p + rr] = 1.0
    return dft_pair, twiddle, order.astype(ml_dtypes.bfloat16)


def cos_sin(turns):
    quadrant = (turns + 256) >> 9
    x = (turns - (quadrant << 9)).astype(F32) * (2.0 * math.pi / NX)
    x2 = x * x
    sine = x * (1.0 + x2 * (-1.0 / 6 + x2 * (1.0 / 120 + x2 * (-1.0 / 5040 + x2 * (1.0 / 362880)))))
    cosine = 1.0 + x2 * (-0.5 + x2 * (1.0 / 24 + x2 * (-1.0 / 720 + x2 * (1.0 / 40320))))
    swap = (quadrant & 1) == 1
    c = jnp.where(swap, sine, cosine)
    s = jnp.where(swap, cosine, sine)
    c = jnp.where(((quadrant + 1) & 2) == 2, -c, c)
    s = jnp.where((quadrant & 2) == 2, -s, s)
    return c, s


def dft4(z):
    (r0, i0), (r1, i1), (r2, i2), (r3, i3) = z
    ar, ai, br, bi = r0 + r2, i0 + i2, r0 - r2, i0 - i2
    cr, ci, dr, di = r1 + r3, i1 + i3, r1 - r3, i1 - i3
    return [(ar + cr, ai + ci), (br - di, bi + dr), (ar - cr, ai - ci), (br + di, bi - dr)]


def dft8(t):
    root = math.sqrt(0.5)
    even = [(t[k][0] + t[k + 4][0], t[k][1] + t[k + 4][1]) for k in range(4)]
    odd = [(t[k][0] - t[k + 4][0], t[k][1] - t[k + 4][1]) for k in range(4)]
    o1 = (root * (odd[1][0] - odd[1][1]), root * (odd[1][0] + odd[1][1]))
    o2 = (-odd[2][1], odd[2][0])
    o3 = (-root * (odd[3][0] + odd[3][1]), root * (odd[3][0] - odd[3][1]))
    ev = dft4(even)
    od = dft4([odd[0], o1, o2, o3])
    out = []
    for m in range(4):
        out += [ev[m], od[m]]
    return out


def split(value):
    high = value.astype(BF16)
    return high, (value - high.astype(F32)).astype(BF16)


def spectral_part(
    spec, shifts, dft_hbm, twiddle_hbm, order_hbm, out,
    xb, trig, lhs_hi, lhs_lo, zb, wb_hi, wb_lo, sb, dft, twiddle, order,
    send1, recv1, send2, recv2, local, greet_all, meanwhile,
):
    me = lax.axis_index("gx")

    def mine(slot):
        return pl.ds(4 * slot, 4)

    own = pltpu.make_async_copy(spec.at[:, mine(me)], xb.at[me], local.at[0])
    own.start()
    dft_copy = pltpu.make_async_copy(dft_hbm, dft, local.at[1])
    dft_copy.start()
    order_copy = pltpu.make_async_copy(order_hbm, order, local.at[2])
    order_copy.start()
    twiddle_copy = pltpu.make_async_copy(twiddle_hbm, twiddle, local.at[3])
    twiddle_copy.start()
    greet_all()

    def first(peer, slot, who):
        return pltpu.make_async_remote_copy(
            src_ref=spec.at[:, mine(peer)], dst_ref=xb.at[slot],
            send_sem=send1.at[peer], recv_sem=recv1.at[slot],
            device_id={"gx": who}, device_id_type=MESH,
        )

    for i in range(1, GX):
        peer = lax.rem(me + i, GX)
        first(peer, me, peer).start()
    meanwhile()

    lane = lax.broadcasted_iota(jnp.int32, (8, WIDTH), 1)
    lane0 = lax.broadcasted_iota(jnp.int32, (ITEMS, DEPTH), 1)
    for z in range(4):
        row = jnp.where(lane0 == 4 * me + z, shifts[...].astype(F32), 0.0)
        shift = jnp.sum(row, axis=1, keepdims=True).astype(jnp.int32)
        shift = jnp.broadcast_to(shift, (8, WIDTH))

        def make_trig(d, carry, z=z, shift=shift):
            c, s = cos_sin((shift * (lane + d * WIDTH)) & (NX - 1))
            trig[0, d, pl.ds(8 * z, 8), :] = c
            trig[1, d, pl.ds(8 * z, 8), :] = s
            return carry

        lax.fori_loop(0, GX, make_trig, 0)

    own.wait()
    for i in range(1, GX):
        peer = lax.rem(me + GX - i, GX)
        first(peer, peer, peer).wait_recv()

    twiddle_copy.wait()
    for zz in range(2):
        rows = pl.ds(16 * zz, 16)
        for h in range(2):
            cols = pl.ds(128 * h, 128)
            t = []
            for d in range(GX):
                xr = xb[d, 0, pl.ds(2 * zz, 2), :, cols].reshape(16, 128)
                xi = xb[d, 1, pl.ds(2 * zz, 2), :, cols].reshape(16, 128)
                c = trig[0, d, rows, cols]
                s = trig[1, d, rows, cols]
                t.append((xr * c - xi * s, xr * s + xi * c))
            y = dft8(t)
            for r in range(8):
                yr, yi = y[r]
                if r > 0:
                    c = twiddle[0, pl.ds(r, 1), cols]
                    s = twiddle[1, pl.ds(r, 1), cols]
                    yr, yi = yr * c - yi * s, yr * s + yi * c
                place = pl.ds(32 * r + 16 * zz, 16)
                hi, lo = split(yr)
                lhs_hi[place, pl.ds(128 * h, 128)] = hi
                lhs_lo[place, pl.ds(128 * h, 128)] = lo
                hi, lo = split(yi)
                lhs_hi[place, pl.ds(256 + 128 * h, 128)] = hi
                lhs_lo[place, pl.ds(256 + 128 * h, 128)] = lo

    dft_copy.wait()
    zb[...] = (
        jnp.dot(lhs_hi[...], dft[0], preferred_element_type=F32)
        + jnp.dot(lhs_hi[...], dft[1], preferred_element_type=F32)
        + jnp.dot(lhs_lo[...], dft[0], preferred_element_type=F32)
    )
    group = lax.broadcasted_iota(jnp.int32, (ROWS, 128), 1) // 32
    for e in range(8):
        column, g = e // 4, e % 4
        for h in range(2):
            total = None
            for rr in range(4):
                r = 4 * h + rr
                tile = zb[pl.ds(32 * r, 32), pl.ds(128 * column, 128)]
                turn = (32 * (rr - g)) % 128
                if turn:
                    tile = pltpu.roll(tile, turn, 1)
                total = tile if total is None else jnp.where(group == rr, tile, total)
            hi, lo = split(total)
            wb_hi[pl.ds(32 * e, 32), pl.ds(128 * h, 128)] = hi
            wb_lo[pl.ds(32 * e, 32), pl.ds(128 * h, 128)] = lo
    order_copy.wait()
    natural = jnp.dot(wb_hi[...], order[...], preferred_element_type=F32) + jnp.dot(
        wb_lo[...], order[...], preferred_element_type=F32
    )
    sb[...] = natural.reshape(8, 4, 8, WIDTH)

    def second(peer, slot, who):
        return pltpu.make_async_remote_copy(
            src_ref=sb.at[peer], dst_ref=out.at[mine(slot)],
            send_sem=send2.at[peer], recv_sem=recv2.at[slot],
            device_id={"gx": who}, device_id_type=MESH,
        )

    for i in range(1, GX):
        peer = lax.rem(me + i, GX)
        second(peer, me, peer).start()
    out[mine(me)] = sb[me]
    for i in range(1, GX):
        peer = lax.rem(me + GX - i, GX)
        second(peer, peer, peer).wait_recv()

    def drain():
        for i in range(1, GX):
            peer = lax.rem(me + i, GX)
            first(peer, me, peer).wait_send()
            second(peer, me, peer).wait_send()

    return drain


def harmonic(center, beside):
    return 2.0 * center * beside / (center + beside)


LEVELS = (
    [(n, n - 1, n + 1) for n in range(1, 31, 2)],
    [(n, n - 2, min(n + 2, 31)) for n in range(2, 31, 4)],
    [(n, n - 4, min(n + 4, 31)) for n in range(4, 31, 8)],
    [(8, 0, 16), (24, 16, 31)],
    [(16, 0, 31)],
)


def field_kernel(
    spec, shifts_hbm, dft_hbm, twiddle_hbm, order_hbm, pressure_hbm, source_hbm, colour_hbm,
    log_perm, out, *scratch,
):
    (
        xb, trig, lhs_hi, lhs_lo, zb, wb_hi, wb_lo, sb, dft, twiddle, order,
        send1, recv1, send2, recv2, local,
        pressure, source, colour, shifts,
        perm, half, ww, we, ws, wn, dd, ff, cc, ll, rr, iv,
        xs0, xh0, ys0, yh0, xs1, xh1, ys1, yh1, xs2, xh2, ys2, yh2,
        msg, got, ans, sol, gains, taken, chain, sums, others,
        halo_send, halo_recv, gz_send, gz_recv,
    ) = scratch
    gx = lax.axis_index("gx")
    gy = lax.axis_index("gy")
    gz = lax.axis_index("gz")
    left, right = lax.rem(gx + GX - 1, GX), lax.rem(gx + 1, GX)
    south, north = lax.rem(gy + GY - 1, GY), lax.rem(gy + 1, GY)
    drains = []

    pressure_copy = pltpu.make_async_copy(pressure_hbm, pressure, local.at[4])
    source_copy = pltpu.make_async_copy(source_hbm, source, local.at[5])
    shifts_copy = pltpu.make_async_copy(shifts_hbm, shifts, local.at[7])
    colour_copy = pltpu.make_async_copy(colour_hbm, colour, local.at[6])

    def greet_all():
        barrier = pltpu.get_barrier_semaphore()

        for i in FAR_FIRST:
            peer = lax.rem(gz + i, GZ)
            pl.semaphore_signal(barrier, inc=1, device_id={"gz": peer}, device_id_type=MESH)
        for i in range(1, GX):
            peer = lax.rem(gx + i, GX)
            pl.semaphore_signal(barrier, inc=1, device_id={"gx": peer}, device_id_type=MESH)
        for who in (south, north):
            pl.semaphore_signal(barrier, inc=1, device_id={"gy": who}, device_id_type=MESH)
        shifts_copy.start()
        pressure_copy.start()
        source_copy.start()
        colour_copy.start()
        pl.semaphore_wait(barrier, GX - 1 + GZ - 1 + 2)

    lane1 = lax.broadcasted_iota(jnp.int32, (8, 128), 1)
    lane = lax.broadcasted_iota(jnp.int32, (8, WIDTH), 1)
    sub = lax.broadcasted_iota(jnp.int32, (8, WIDTH), 0)

    def pack(source_ref, xs, ys):
        west = jnp.zeros((8, 128), F32)
        east = jnp.zeros((8, 128), F32)
        for z in range(DEPTH):
            tile = source_ref[z]
            west = jnp.where(lane1 == z, tile[:, 0:1], west)
            east = jnp.where(lane1 == z, tile[:, 255:256], east)
            ys[0, pl.ds(z, 1), :] = tile[0:1, :]
            ys[1, pl.ds(z, 1), :] = tile[7:8, :]
        xs[0] = west
        xs[1] = east

    sides = (
        (0, 1, {"gx": left}, gx > 0, gx < GX - 1),
        (1, 0, {"gx": right}, gx < GX - 1, gx > 0),
        (0, 1, {"gy": south}, gy > 0, gy < GY - 1),
        (1, 0, {"gy": north}, gy < GY - 1, gy > 0),
    )

    def halo(phase, xs, xh, ys, yh):
        def copy(k):
            src, dst = (xs, xh) if k < 2 else (ys, yh)
            side, there, who, _, _ = sides[k]
            return pltpu.make_async_remote_copy(
                src_ref=src.at[side], dst_ref=dst.at[there],
                send_sem=halo_send.at[phase, k], recv_sem=halo_recv.at[phase, k],
                device_id=who, device_id_type=MESH,
            )

        def each(which, action):
            for k in range(4):
                pl.when(sides[k][which])(functools.partial(action, k))

        def blank(k):
            dst = xh if k < 2 else yh
            there = sides[k][1]

            def fill():
                dst[there] = jnp.zeros(dst.shape[1:], F32)

            pl.when(jnp.logical_not(sides[k][4]))(fill)

        each(3, lambda k: copy(k).start())
        for k in range(4):
            blank(k)
        drains.append(lambda: each(3, lambda k: copy(k).wait_send()))
        return lambda: each(4, lambda k: copy(k).wait_recv())

    arrived = []

    def meanwhile():
        pressure_copy.wait()
        pack(pressure, xs0, ys0)
        arrived.append(halo(0, xs0, xh0, ys0, yh0))
        shifts_copy.wait()

    drains.append(
        spectral_part(
            spec, shifts, dft_hbm, twiddle_hbm, order_hbm, log_perm,
            xb, trig, lhs_hi, lhs_lo, zb, wb_hi, wb_lo, sb, dft, twiddle, order,
            send1, recv1, send2, recv2, local, greet_all, meanwhile,
        )
    )

    def make_perm(z, carry):
        perm[z] = jnp.exp(log_perm[z])
        return carry

    lax.fori_loop(0, DEPTH, make_perm, 0, unroll=4)
    pack(perm, xs1, ys1)
    wait_perm = halo(1, xs1, xh1, ys1, yh1)
    source_copy.wait()
    colour_copy.wait()
    arrived[0]()
    wait_perm()

    def beside(value, west, east, lower, upper):
        vw = jnp.where(lane == 0, west, pltpu.roll(value, 1, 1))
        ve = jnp.where(lane == WIDTH - 1, east, pltpu.roll(value, WIDTH - 1, 1))
        vs = jnp.where(sub == 0, lower, pltpu.roll(value, 1, 0))
        vn = jnp.where(sub == 7, upper, pltpu.roll(value, 7, 0))
        return vw, ve, vs, vn

    def edges(z, xh, yh):
        west = xh[0][:, z:z + 1]
        east = xh[1][:, z:z + 1]
        lower = yh[0, pl.ds(z, 1), :]
        upper = yh[1, pl.ds(z, 1), :]
        return west, east, lower, upper

    for z in range(DEPTH):
        p = perm[z]
        pw, pe, ps, pn = beside(p, *edges(z, xh1, yh1))
        aw, ae, as_, an = harmonic(p, pw), harmonic(p, pe), harmonic(p, ps), harmonic(p, pn)
        ww[z], we[z], ws[z], wn[z] = aw, ae, as_, an
        dd[z] = STORE + aw + ae + as_ + an
        vw, ve, vs, vn = beside(pressure[z], *edges(z, xh0, yh0))
        ff[z] = source[z] + aw * vw + ae * ve + as_ * vs + an * vn
        if z < DEPTH - 1:
            cc[z] = VERT * harmonic(p, perm[z + 1])

    for level in LEVELS:
        for n, a, b in level:
            wl, wr, d, f = cc[a], cc[n], dd[n], ff[n]
            inv = 1.0 / (d + wl + wr)
            l, r = wl * inv, wr * inv
            ll[n], rr[n], iv[n] = l, r, inv
            cc[a] = l * wr
            dd[a] = dd[a] + l * d
            dd[b] = dd[b] + r * d
            ff[a] = ff[a] + l * f
            ff[b] = ff[b] + r * f

    def put(ref, kind, value):
        for h in range(2):
            ref[pl.ds(8 * h + kind, 8, stride=16), :] = value[:, 128 * h:128 * h + 128]

    def take(ref, kind):
        return jnp.concatenate(
            [ref[pl.ds(8 * h + kind, 8, stride=16), :] for h in range(2)], axis=1
        )

    row = lax.div(gz, 2)

    def everyone(src, dst, phase, size, offsets, to_owner):
        def tile(index):
            return pl.ds(pl.multiple_of(size * index, 8), size)

        def copy(peer, slot, first, then):
            return pltpu.make_async_remote_copy(
                src_ref=src.at[tile(first)], dst_ref=dst.at[tile(then)],
                send_sem=gz_send.at[phase, peer], recv_sem=gz_recv.at[phase, slot],
                device_id={"gz": peer}, device_id_type=MESH,
            )

        def outward(i):
            peer = lax.rem(gz + i, GZ)
            if to_owner:
                return copy(peer, gz, lax.div(peer, 2), gz)
            return copy(peer, gz, peer, row)

        def inward(i):
            peer = lax.rem(gz + GZ - i, GZ)
            if to_owner:
                return copy(peer, peer, 0, peer)
            return copy(peer, peer, 0, lax.div(peer, 2))

        def finish():
            for i in offsets:
                inward(i).wait_recv()

        def drain():
            for i in offsets:
                outward(i).wait_send()

        for i in offsets:
            outward(i).start()
        if to_owner:
            dst[tile(gz), :] = src[tile(row), :]
        else:
            dst[tile(row), :] = src[tile(gz), :]
        drains.append(drain)
        return finish

    put(msg, 0, dd[0])
    put(msg, 1, dd[DEPTH - 1])
    put(msg, 2, cc[0])
    put(msg, 3, perm[0])
    put(msg, 4, perm[DEPTH - 1])
    put(msg, 5, ff[0])
    put(msg, 6, ff[DEPTH - 1])
    put(msg, 7, ff[0])
    everyone(msg, got, 0, 16, FAR_FIRST, True)()

    def kind(ref, k):
        return jnp.concatenate(
            [ref[pl.ds(8 * h + k, GZ, stride=16), :] for h in range(2)], axis=1
        )

    def spread(ref, size, k, value):
        for h in range(2):
            ref[pl.ds(size * h + k, GZ, stride=2 * size), :] = value[:, 128 * h:128 * h + 128]

    d0, d1, c, p0, p1 = (kind(got, k) for k in range(5))
    f0, f1 = kind(got, 5), kind(got, 6)
    segment = lax.broadcasted_iota(jnp.int32, (GZ, WIDTH), 0)
    w = jnp.where(segment < GZ - 1, VERT * harmonic(p1, pltpu.roll(p0, GZ - 1, 0)), 0.0)
    last_inv = 1.0 / (d1 + c + w)
    last_l, last_r = c * last_inv, w * last_inv

    def up(value, step):
        return pltpu.roll(value, step, 0)

    def down(value, step):
        return pltpu.roll(value, GZ - step, 0)

    e = d0 + last_l * d1 + up(last_r * d1, 1)
    b = last_l * w
    a = up(b, 1)
    f = f0 + last_l * f1 + up(last_r * f1, 1)
    for step in (1, 2, 4, 8):
        inv = 1.0 / (e + a + b)
        alpha, beta = a * up(inv, step), b * down(inv, step)
        e = e + alpha * up(e, step) + beta * down(e, step)
        f = f + alpha * up(f, step) + beta * down(f, step)
        if step < 8:
            a, b = alpha * up(a, step), beta * down(b, step)
    first = f / e
    ans[...] = jnp.zeros_like(ans)
    spread(ans, 8, 0, first)
    spread(ans, 8, 1, f1 * last_inv + last_l * first + last_r * down(first, 1))
    wait_sol = everyone(ans, sol, 1, 16, ROUND_FIRST, False)

    links = [jnp.zeros((1, WIDTH), F32)] * 2
    for i in range(GZ):
        j = GZ - 1 - i
        eb, et = links
        at_i, at_j = pl.ds(i, 1), pl.ds(j, 1)
        chain[2, at_i, :] = eb
        chain[5, at_j, :] = et
        low = d0[i:i + 1] + eb
        rho = c[i:i + 1] / (low + c[i:i + 1])
        low = d1[i:i + 1] + rho * low
        tau = w[i:i + 1] / (low + w[i:i + 1])
        chain[0, at_i, :] = rho
        chain[1, at_i, :] = tau
        high = d1[j:j + 1] + et
        sigma = c[j:j + 1] / (high + c[j:j + 1])
        high = d0[j:j + 1] + sigma * high
        chain[3, at_j, :] = sigma
        if j > 0:
            upsilon = w[j - 1:j] / (high + w[j - 1:j])
            chain[4, pl.ds(j - 1, 1), :] = upsilon
        links = [tau * low, upsilon * high]
    chain[4, pl.ds(GZ - 1, 1), :] = jnp.zeros((1, WIDTH), F32)
    tau, upsilon = chain[1], chain[4]
    climb = up(tau * chain[0], 1)
    descend = upsilon * down(chain[3], 1)
    from_below, from_above = [None, up(tau, 1)], [None, upsilon]
    for k in range(2, GZ):
        from_below.append(climb * up(from_below[-1], 1))
        from_above.append(descend * down(from_above[-1], 1))
    gains[...] = jnp.zeros_like(gains)
    for k in range(1, GZ):
        spread(gains, 24, k, from_below[k] + from_above[GZ - k])
    spread(gains, 24, GZ, chain[2])
    spread(gains, 24, GZ + 1, chain[5])
    wait_gains = everyone(gains, taken, 2, 48, ROUND_FIRST, False)
    wait_sol()

    def substitute(first, last, merge):
        u = {0: first, DEPTH - 1: last}
        merge(0, u[0])
        merge(DEPTH - 1, u[DEPTH - 1])
        for level in reversed(LEVELS):
            for n, a, b in level:
                u[n] = ff[n] * iv[n] + ll[n] * u[a] + rr[n] * u[b]
                merge(n, u[n])

    tint = colour[...]

    def merge_half(z, u):
        half[z] = jnp.where(tint == 0, u, pressure[z])

    substitute(take(sol, 0), take(sol, 1), merge_half)
    pack(half, xs2, ys2)
    wait_half = halo(2, xs2, xh2, ys2, yh2)

    def gain(k):
        return jnp.concatenate(
            [taken[pl.ds(24 * h + k, 8, stride=48), :] for h in range(2)], axis=1
        )

    wait_gains()
    c = cc[0]
    low = dd[0] + gain(GZ)
    high = dd[DEPTH - 1] + gain(GZ + 1)
    low_inv = 1.0 / (low + c)
    rho = c * low_inv
    sigma = c / (high + c)
    high_inv = 1.0 / (high + rho * low)
    wait_half()
    for z in range(DEPTH):
        vw, ve, vs, vn = beside(half[z], *edges(z, xh2, yh2))
        ff[z] = source[z] + ww[z] * vw + we[z] * ve + ws[z] * vs + wn[z] * vn
    for level in LEVELS:
        for n, a, b in level:
            f = ff[n]
            ff[a] = ff[a] + ll[n] * f
            ff[b] = ff[b] + rr[n] * f
    f0, f1 = ff[0], ff[DEPTH - 1]
    sums[0] = f1 + rho * f0
    sums[1] = f0 + sigma * f1

    def cast(i):
        peer = lax.rem(gz + i, GZ)
        return pltpu.make_async_remote_copy(
            src_ref=sums.at[lax.div(gz + i, GZ)], dst_ref=others.at[gz],
            send_sem=gz_send.at[3, peer], recv_sem=gz_recv.at[3, gz],
            device_id={"gz": peer}, device_id_type=MESH,
        )

    def heard(i):
        peer = lax.rem(gz + GZ - i, GZ)
        return pltpu.make_async_remote_copy(
            src_ref=sums.at[0], dst_ref=others.at[peer],
            send_sem=gz_send.at[3, peer], recv_sem=gz_recv.at[3, peer],
            device_id={"gz": peer}, device_id_type=MESH,
        )

    def drain_cast():
        for i in FAR_FIRST:
            cast(i).wait_send()

    for i in FAR_FIRST:
        cast(i).start()
    drains.append(drain_cast)
    for i in FAR_FIRST:
        heard(i).wait_recv()
    for i in range(1, GZ):
        part = gain(i) * others[lax.rem(gz + GZ - i, GZ)]
        f0 = f0 + jnp.where(gz >= i, part, 0.0)
        f1 = f1 + jnp.where(gz >= i, 0.0, part)
    last = (f1 + rho * f0) * high_inv
    first = f0 * low_inv + rho * last

    def merge_out(z, u):
        out[z] = jnp.where(tint == 1, u, half[z])

    substitute(first, last, merge_out)
    for drain in drains:
        drain()


def pin(value):
    return pltpu.with_memory_space_constraint(value, pltpu.HBM)


def field_call(spectral, shifts, colour, pressure, source):
    vmem = pl.BlockSpec(memory_space=pltpu.VMEM)
    hbm = pl.BlockSpec(memory_space=pltpu.HBM)
    block = (DEPTH, ITEMS, WIDTH)
    field = pltpu.VMEM(block, F32)
    board = pltpu.VMEM((8 * GZ, 128), F32)
    pair_board = pltpu.VMEM((16 * GZ, 128), F32)
    columns = pltpu.VMEM((2, ITEMS, 128), F32)
    rows = pltpu.VMEM((2, DEPTH, WIDTH), F32)
    dma = pltpu.SemaphoreType.DMA
    return pl.pallas_call(
        field_kernel,
        out_shape=[jax.ShapeDtypeStruct(block, F32)] * 2,
        in_specs=[hbm] * 8,
        out_specs=[vmem, vmem],
        scratch_shapes=[
            pltpu.VMEM((GX, 2, 4, 8, WIDTH), F32),
            pltpu.VMEM((2, GX, ROWS, WIDTH), F32),
            pltpu.VMEM((256, 512), BF16),
            pltpu.VMEM((256, 512), BF16),
            pltpu.VMEM((256, WIDTH), F32),
            pltpu.VMEM((256, WIDTH), BF16),
            pltpu.VMEM((256, WIDTH), BF16),
            pltpu.VMEM((GX, 4, 8, WIDTH), F32),
            pltpu.VMEM((2, 512, WIDTH), BF16),
            pltpu.VMEM((2, GX, WIDTH), F32),
            pltpu.VMEM((WIDTH, WIDTH), BF16),
            dma((GX,)), dma((GX,)), dma((GX,)), dma((GX,)), dma((8,)),
            field, field, pltpu.VMEM((ITEMS, WIDTH), jnp.int32),
            pltpu.VMEM((ITEMS, DEPTH), jnp.int32),
        ]
        + [field] * 12
        + [columns, columns, rows, rows] * 3
        + [board, pair_board, pair_board, board]
        + [
            pltpu.VMEM((48 * GZ, 128), F32),
            pltpu.VMEM((24 * GZ, 128), F32),
            pltpu.VMEM((6, GZ, WIDTH), F32),
            pltpu.VMEM((2, ITEMS, WIDTH), F32),
            pltpu.VMEM((GZ, ITEMS, WIDTH), F32),
        ]
        + [dma((3, 4)), dma((3, 4)), dma((4, GZ)), dma((4, GZ))],
        compiler_params=pltpu.CompilerParams(
            collective_id=0, has_side_effects=True, vmem_limit_bytes=32 << 20
        ),
        name="field",
    )(
        *map(pin, (spectral, shifts.T, *map(jnp.asarray, tables()), pressure, source, colour))
    )


def body(spectral, shifts, colour, pressure, source):
    log_perm, smoothed = field_call(spectral, shifts, colour, pressure, source)
    return (log_perm, smoothed)


def solution(mesh):
    in_specs = (
        P(None, "gz", "gy", "gx"),
        P("gz", "gy"),
        P("gy", "gx"),
        P("gz", "gy", "gx"),
        P("gz", "gy", "gx"),
    )
    out_specs = (P("gz", "gy", "gx"), P("gz", "gy", "gx"))
    return jax.shard_map(body, mesh=mesh, in_specs=in_specs, out_specs=out_specs, check_vma=False)
```

```python
import functools
import math

import jax
import jax.numpy as jnp
import ml_dtypes
import numpy as np
from jax import lax
from jax.experimental import pallas as pl
from jax.experimental.pallas import tpu as pltpu
from jax.sharding import PartitionSpec as P

NX = 2048
STORE = 1.0
VERT = 65536.0
MESH = pl.DeviceIdType.MESH
GX = 8
GY = 4
GZ = 16
DEPTH = 32
ITEMS = 8
WIDTH = 256
ROWS = 32
FAR_FIRST = (9, 7, 11, 5, 13, 3, 8, 15, 1, 10, 6, 12, 4, 14, 2)
RELAYS = 4
ROUND_FIRST = (8, 6, 10, 4, 12, 2, 14)
F32 = jnp.float32
BF16 = jnp.bfloat16


def tables():
    j = np.arange(WIDTH)
    angle = 2.0 * np.pi * ((j[:, None] * j[None, :]) % WIDTH) / WIDTH
    dft = np.concatenate([np.cos(angle), -np.sin(angle)], axis=0) / math.sqrt(NX)
    high = dft.astype(ml_dtypes.bfloat16)
    low = (dft - high.astype(np.float64)).astype(ml_dtypes.bfloat16)
    dft_pair = np.stack([high, low])
    r = np.arange(GX)
    turn = 2.0 * np.pi * (r[:, None] * j[None, :]) / NX
    twiddle = np.stack([np.cos(turn), np.sin(turn)]).astype(np.float32)
    order = np.zeros((WIDTH, WIDTH), np.float32)
    for rr in range(8):
        for p in range(32):
            order[32 * rr + p, 8 * p + rr] = 1.0
    return dft_pair, twiddle, order.astype(ml_dtypes.bfloat16)


def cos_sin(turns):
    quadrant = (turns + 256) >> 9
    x = (turns - (quadrant << 9)).astype(F32) * (2.0 * math.pi / NX)
    x2 = x * x
    sine = x * (1.0 + x2 * (-1.0 / 6 + x2 * (1.0 / 120 + x2 * (-1.0 / 5040 + x2 * (1.0 / 362880)))))
    cosine = 1.0 + x2 * (-0.5 + x2 * (1.0 / 24 + x2 * (-1.0 / 720 + x2 * (1.0 / 40320))))
    swap = (quadrant & 1) == 1
    c = jnp.where(swap, sine, cosine)
    s = jnp.where(swap, cosine, sine)
    c = jnp.where(((quadrant + 1) & 2) == 2, -c, c)
    s = jnp.where((quadrant & 2) == 2, -s, s)
    return c, s


def dft4(z):
    (r0, i0), (r1, i1), (r2, i2), (r3, i3) = z
    ar, ai, br, bi = r0 + r2, i0 + i2, r0 - r2, i0 - i2
    cr, ci, dr, di = r1 + r3, i1 + i3, r1 - r3, i1 - i3
    return [(ar + cr, ai + ci), (br - di, bi + dr), (ar - cr, ai - ci), (br + di, bi - dr)]


def dft8(t):
    root = math.sqrt(0.5)
    even = [(t[k][0] + t[k + 4][0], t[k][1] + t[k + 4][1]) for k in range(4)]
    odd = [(t[k][0] - t[k + 4][0], t[k][1] - t[k + 4][1]) for k in range(4)]
    o1 = (root * (odd[1][0] - odd[1][1]), root * (odd[1][0] + odd[1][1]))
    o2 = (-odd[2][1], odd[2][0])
    o3 = (-root * (odd[3][0] + odd[3][1]), root * (odd[3][0] - odd[3][1]))
    ev = dft4(even)
    od = dft4([odd[0], o1, o2, o3])
    out = []
    for m in range(4):
        out += [ev[m], od[m]]
    return out


def split(value):
    high = value.astype(BF16)
    return high, (value - high.astype(F32)).astype(BF16)


def spectral_part(
    spec, shifts, dft_hbm, twiddle_hbm, order_hbm, out,
    xb, trig, lhs_hi, lhs_lo, zb, wb_hi, wb_lo, sb, dft, twiddle, order,
    send1, recv1, send2, recv2, local, greet_all, meanwhile,
):
    me = lax.axis_index("gx")

    def mine(slot):
        return pl.ds(4 * slot, 4)

    own = pltpu.make_async_copy(spec.at[:, mine(me)], xb.at[me], local.at[0])
    own.start()
    dft_copy = pltpu.make_async_copy(dft_hbm, dft, local.at[1])
    dft_copy.start()
    order_copy = pltpu.make_async_copy(order_hbm, order, local.at[2])
    order_copy.start()
    twiddle_copy = pltpu.make_async_copy(twiddle_hbm, twiddle, local.at[3])
    twiddle_copy.start()
    greet_all()

    def first(peer, slot, who):
        return pltpu.make_async_remote_copy(
            src_ref=spec.at[:, mine(peer)], dst_ref=xb.at[slot],
            send_sem=send1.at[peer], recv_sem=recv1.at[slot],
            device_id={"gx": who}, device_id_type=MESH,
        )

    for i in range(1, GX):
        peer = lax.rem(me + i, GX)
        first(peer, me, peer).start()
    meanwhile()

    lane = lax.broadcasted_iota(jnp.int32, (8, WIDTH), 1)
    lane0 = lax.broadcasted_iota(jnp.int32, (ITEMS, DEPTH), 1)
    for z in range(4):
        row = jnp.where(lane0 == 4 * me + z, shifts[...].astype(F32), 0.0)
        shift = jnp.sum(row, axis=1, keepdims=True).astype(jnp.int32)
        shift = jnp.broadcast_to(shift, (8, WIDTH))

        def make_trig(d, carry, z=z, shift=shift):
            c, s = cos_sin((shift * (lane + d * WIDTH)) & (NX - 1))
            trig[0, d, pl.ds(8 * z, 8), :] = c
            trig[1, d, pl.ds(8 * z, 8), :] = s
            return carry

        lax.fori_loop(0, GX, make_trig, 0)

    own.wait()
    for i in range(1, GX):
        peer = lax.rem(me + GX - i, GX)
        first(peer, peer, peer).wait_recv()

    twiddle_copy.wait()
    for zz in range(2):
        rows = pl.ds(16 * zz, 16)
        for h in range(2):
            cols = pl.ds(128 * h, 128)
            t = []
            for d in range(GX):
                xr = xb[d, 0, pl.ds(2 * zz, 2), :, cols].reshape(16, 128)
                xi = xb[d, 1, pl.ds(2 * zz, 2), :, cols].reshape(16, 128)
                c = trig[0, d, rows, cols]
                s = trig[1, d, rows, cols]
                t.append((xr * c - xi * s, xr * s + xi * c))
            y = dft8(t)
            for r in range(8):
                yr, yi = y[r]
                if r > 0:
                    c = twiddle[0, pl.ds(r, 1), cols]
                    s = twiddle[1, pl.ds(r, 1), cols]
                    yr, yi = yr * c - yi * s, yr * s + yi * c
                place = pl.ds(32 * r + 16 * zz, 16)
                hi, lo = split(yr)
                lhs_hi[place, pl.ds(128 * h, 128)] = hi
                lhs_lo[place, pl.ds(128 * h, 128)] = lo
                hi, lo = split(yi)
                lhs_hi[place, pl.ds(256 + 128 * h, 128)] = hi
                lhs_lo[place, pl.ds(256 + 128 * h, 128)] = lo

    dft_copy.wait()
    zb[...] = (
        jnp.dot(lhs_hi[...], dft[0], preferred_element_type=F32)
        + jnp.dot(lhs_hi[...], dft[1], preferred_element_type=F32)
        + jnp.dot(lhs_lo[...], dft[0], preferred_element_type=F32)
    )
    group = lax.broadcasted_iota(jnp.int32, (ROWS, 128), 1) // 32
    for e in range(8):
        column, g = e // 4, e % 4
        for h in range(2):
            total = None
            for rr in range(4):
                r = 4 * h + rr
                tile = zb[pl.ds(32 * r, 32), pl.ds(128 * column, 128)]
                turn = (32 * (rr - g)) % 128
                if turn:
                    tile = pltpu.roll(tile, turn, 1)
                total = tile if total is None else jnp.where(group == rr, tile, total)
            hi, lo = split(total)
            wb_hi[pl.ds(32 * e, 32), pl.ds(128 * h, 128)] = hi
            wb_lo[pl.ds(32 * e, 32), pl.ds(128 * h, 128)] = lo
    order_copy.wait()
    natural = jnp.dot(wb_hi[...], order[...], preferred_element_type=F32) + jnp.dot(
        wb_lo[...], order[...], preferred_element_type=F32
    )
    sb[...] = natural.reshape(8, 4, 8, WIDTH)

    def second(peer, slot, who):
        return pltpu.make_async_remote_copy(
            src_ref=sb.at[peer], dst_ref=out.at[mine(slot)],
            send_sem=send2.at[peer], recv_sem=recv2.at[slot],
            device_id={"gx": who}, device_id_type=MESH,
        )

    for i in range(1, GX):
        peer = lax.rem(me + i, GX)
        second(peer, me, peer).start()
    out[mine(me)] = sb[me]
    for i in range(1, GX):
        peer = lax.rem(me + GX - i, GX)
        second(peer, peer, peer).wait_recv()

    def drain():
        for i in range(1, GX):
            peer = lax.rem(me + i, GX)
            first(peer, me, peer).wait_send()
            second(peer, me, peer).wait_send()

    return drain


def harmonic(center, beside):
    return 2.0 * center * beside / (center + beside)


LEVELS = (
    [(n, n - 1, n + 1) for n in range(1, 31, 2)],
    [(n, n - 2, min(n + 2, 31)) for n in range(2, 31, 4)],
    [(n, n - 4, min(n + 4, 31)) for n in range(4, 31, 8)],
    [(8, 0, 16), (24, 16, 31)],
    [(16, 0, 31)],
)


def field_kernel(
    spec, shifts_hbm, dft_hbm, twiddle_hbm, order_hbm, pressure_hbm, source_hbm, colour_hbm,
    log_perm, out, *scratch,
):
    (
        xb, trig, lhs_hi, lhs_lo, zb, wb_hi, wb_lo, sb, dft, twiddle, order,
        send1, recv1, send2, recv2, local,
        pressure, source, colour, shifts,
        perm, half, ww, we, ws, wn, dd, ff, cc, ll, rr, iv,
        xs0, xh0, ys0, yh0, xs1, xh1, ys1, yh1, xs2, xh2, ys2, yh2,
        msg, got, ans, sol, gains, taken, chain, sums, others,
        halo_send, halo_recv, gz_send, gz_recv, relay,
    ) = scratch
    gx = lax.axis_index("gx")
    gy = lax.axis_index("gy")
    gz = lax.axis_index("gz")
    left, right = lax.rem(gx + GX - 1, GX), lax.rem(gx + 1, GX)
    south, north = lax.rem(gy + GY - 1, GY), lax.rem(gy + 1, GY)
    drains = []
    twin = gz + 1 - 2 * lax.rem(gz, 2)
    round_neighbours = (lax.rem(gz + 2, GZ), lax.rem(gz + GZ - 2, GZ))

    pressure_copy = pltpu.make_async_copy(pressure_hbm, pressure, local.at[4])
    source_copy = pltpu.make_async_copy(source_hbm, source, local.at[5])
    shifts_copy = pltpu.make_async_copy(shifts_hbm, shifts, local.at[7])
    colour_copy = pltpu.make_async_copy(colour_hbm, colour, local.at[6])

    def greet_all():
        barrier = pltpu.get_barrier_semaphore()

        for peer in (twin, *round_neighbours):
            pl.semaphore_signal(barrier, inc=1, device_id={"gz": peer}, device_id_type=MESH)
        for i in range(1, GX):
            peer = lax.rem(gx + i, GX)
            pl.semaphore_signal(barrier, inc=1, device_id={"gx": peer}, device_id_type=MESH)
        for who in (south, north):
            pl.semaphore_signal(barrier, inc=1, device_id={"gy": who}, device_id_type=MESH)
        shifts_copy.start()
        pressure_copy.start()
        source_copy.start()
        colour_copy.start()
        pl.semaphore_wait(barrier, GX - 1 + 3 + 2)

    lane1 = lax.broadcasted_iota(jnp.int32, (8, 128), 1)
    lane = lax.broadcasted_iota(jnp.int32, (8, WIDTH), 1)
    sub = lax.broadcasted_iota(jnp.int32, (8, WIDTH), 0)

    def pack(source_ref, xs, ys):
        west = jnp.zeros((8, 128), F32)
        east = jnp.zeros((8, 128), F32)
        for z in range(DEPTH):
            tile = source_ref[z]
            west = jnp.where(lane1 == z, tile[:, 0:1], west)
            east = jnp.where(lane1 == z, tile[:, 255:256], east)
            ys[0, pl.ds(z, 1), :] = tile[0:1, :]
            ys[1, pl.ds(z, 1), :] = tile[7:8, :]
        xs[0] = west
        xs[1] = east

    sides = (
        (0, 1, {"gx": left}, gx > 0, gx < GX - 1),
        (1, 0, {"gx": right}, gx < GX - 1, gx > 0),
        (0, 1, {"gy": south}, gy > 0, gy < GY - 1),
        (1, 0, {"gy": north}, gy < GY - 1, gy > 0),
    )

    def halo(phase, xs, xh, ys, yh):
        def copy(k):
            src, dst = (xs, xh) if k < 2 else (ys, yh)
            side, there, who, _, _ = sides[k]
            return pltpu.make_async_remote_copy(
                src_ref=src.at[side], dst_ref=dst.at[there],
                send_sem=halo_send.at[phase, k], recv_sem=halo_recv.at[phase, k],
                device_id=who, device_id_type=MESH,
            )

        def each(which, action):
            for k in range(4):
                pl.when(sides[k][which])(functools.partial(action, k))

        def blank(k):
            dst = xh if k < 2 else yh
            there = sides[k][1]

            def fill():
                dst[there] = jnp.zeros(dst.shape[1:], F32)

            pl.when(jnp.logical_not(sides[k][4]))(fill)

        each(3, lambda k: copy(k).start())
        for k in range(4):
            blank(k)
        drains.append(lambda: each(3, lambda k: copy(k).wait_send()))
        return lambda: each(4, lambda k: copy(k).wait_recv())

    arrived = []

    def meanwhile():
        pressure_copy.wait()
        pack(pressure, xs0, ys0)
        arrived.append(halo(0, xs0, xh0, ys0, yh0))
        shifts_copy.wait()
        for turn in range(RELAYS):
            for peer in round_neighbours:
                pl.semaphore_signal(
                    relay.at[turn], inc=1, device_id={"gz": peer}, device_id_type=MESH
                )
            pl.semaphore_wait(relay.at[turn], 2)

    drains.append(
        spectral_part(
            spec, shifts, dft_hbm, twiddle_hbm, order_hbm, log_perm,
            xb, trig, lhs_hi, lhs_lo, zb, wb_hi, wb_lo, sb, dft, twiddle, order,
            send1, recv1, send2, recv2, local, greet_all, meanwhile,
        )
    )

    def make_perm(z, carry):
        perm[z] = jnp.exp(log_perm[z])
        return carry

    lax.fori_loop(0, DEPTH, make_perm, 0, unroll=4)
    pack(perm, xs1, ys1)
    wait_perm = halo(1, xs1, xh1, ys1, yh1)
    source_copy.wait()
    colour_copy.wait()
    arrived[0]()
    wait_perm()

    def beside(value, west, east, lower, upper):
        vw = jnp.where(lane == 0, west, pltpu.roll(value, 1, 1))
        ve = jnp.where(lane == WIDTH - 1, east, pltpu.roll(value, WIDTH - 1, 1))
        vs = jnp.where(sub == 0, lower, pltpu.roll(value, 1, 0))
        vn = jnp.where(sub == 7, upper, pltpu.roll(value, 7, 0))
        return vw, ve, vs, vn

    def edges(z, xh, yh):
        west = xh[0][:, z:z + 1]
        east = xh[1][:, z:z + 1]
        lower = yh[0, pl.ds(z, 1), :]
        upper = yh[1, pl.ds(z, 1), :]
        return west, east, lower, upper

    for z in range(DEPTH):
        p = perm[z]
        pw, pe, ps, pn = beside(p, *edges(z, xh1, yh1))
        aw, ae, as_, an = harmonic(p, pw), harmonic(p, pe), harmonic(p, ps), harmonic(p, pn)
        ww[z], we[z], ws[z], wn[z] = aw, ae, as_, an
        dd[z] = STORE + aw + ae + as_ + an
        vw, ve, vs, vn = beside(pressure[z], *edges(z, xh0, yh0))
        ff[z] = source[z] + aw * vw + ae * ve + as_ * vs + an * vn
        if z < DEPTH - 1:
            cc[z] = VERT * harmonic(p, perm[z + 1])

    for level in LEVELS:
        for n, a, b in level:
            wl, wr, d, f = cc[a], cc[n], dd[n], ff[n]
            inv = 1.0 / (d + wl + wr)
            l, r = wl * inv, wr * inv
            ll[n], rr[n], iv[n] = l, r, inv
            cc[a] = l * wr
            dd[a] = dd[a] + l * d
            dd[b] = dd[b] + r * d
            ff[a] = ff[a] + l * f
            ff[b] = ff[b] + r * f

    def put(ref, kind, value):
        for h in range(2):
            ref[pl.ds(8 * h + kind, 8, stride=16), :] = value[:, 128 * h:128 * h + 128]

    def take(ref, kind):
        return jnp.concatenate(
            [ref[pl.ds(8 * h + kind, 8, stride=16), :] for h in range(2)], axis=1
        )

    row = lax.div(gz, 2)

    def everyone(src, dst, phase, size, offsets, to_owner):
        def tile(index):
            return pl.ds(pl.multiple_of(size * index, 8), size)

        def copy(peer, slot, first, then):
            return pltpu.make_async_remote_copy(
                src_ref=src.at[tile(first)], dst_ref=dst.at[tile(then)],
                send_sem=gz_send.at[phase, peer], recv_sem=gz_recv.at[phase, slot],
                device_id={"gz": peer}, device_id_type=MESH,
            )

        def outward(i):
            peer = lax.rem(gz + i, GZ)
            if to_owner:
                return copy(peer, gz, lax.div(peer, 2), gz)
            return copy(peer, gz, peer, row)

        def inward(i):
            peer = lax.rem(gz + GZ - i, GZ)
            if to_owner:
                return copy(peer, peer, 0, peer)
            return copy(peer, peer, 0, lax.div(peer, 2))

        def finish():
            for i in offsets:
                inward(i).wait_recv()

        def drain():
            for i in offsets:
                outward(i).wait_send()

        for i in offsets:
            outward(i).start()
        if to_owner:
            dst[tile(gz), :] = src[tile(row), :]
        else:
            dst[tile(row), :] = src[tile(gz), :]
        drains.append(drain)
        return finish

    put(msg, 0, dd[0])
    put(msg, 1, dd[DEPTH - 1])
    put(msg, 2, cc[0])
    put(msg, 3, perm[0])
    put(msg, 4, perm[DEPTH - 1])
    put(msg, 5, ff[0])
    put(msg, 6, ff[DEPTH - 1])
    put(msg, 7, ff[0])
    everyone(msg, got, 0, 16, FAR_FIRST, True)()

    def kind(ref, k):
        return jnp.concatenate(
            [ref[pl.ds(8 * h + k, GZ, stride=16), :] for h in range(2)], axis=1
        )

    def spread(ref, size, k, value):
        for h in range(2):
            ref[pl.ds(size * h + k, GZ, stride=2 * size), :] = value[:, 128 * h:128 * h + 128]

    d0, d1, c, p0, p1 = (kind(got, k) for k in range(5))
    f0, f1 = kind(got, 5), kind(got, 6)
    segment = lax.broadcasted_iota(jnp.int32, (GZ, WIDTH), 0)
    w = jnp.where(segment < GZ - 1, VERT * harmonic(p1, pltpu.roll(p0, GZ - 1, 0)), 0.0)
    last_inv = 1.0 / (d1 + c + w)
    last_l, last_r = c * last_inv, w * last_inv

    def up(value, step):
        return pltpu.roll(value, step, 0)

    def down(value, step):
        return pltpu.roll(value, GZ - step, 0)

    e = d0 + last_l * d1 + up(last_r * d1, 1)
    b = last_l * w
    a = up(b, 1)
    f = f0 + last_l * f1 + up(last_r * f1, 1)
    for step in (1, 2, 4, 8):
        inv = 1.0 / (e + a + b)
        alpha, beta = a * up(inv, step), b * down(inv, step)
        e = e + alpha * up(e, step) + beta * down(e, step)
        f = f + alpha * up(f, step) + beta * down(f, step)
        if step < 8:
            a, b = alpha * up(a, step), beta * down(b, step)
    first = f / e
    ans[...] = jnp.zeros_like(ans)
    spread(ans, 8, 0, first)
    spread(ans, 8, 1, f1 * last_inv + last_l * first + last_r * down(first, 1))
    wait_sol = everyone(ans, sol, 1, 16, ROUND_FIRST, False)

    links = [jnp.zeros((1, WIDTH), F32)] * 2
    for i in range(GZ):
        j = GZ - 1 - i
        eb, et = links
        at_i, at_j = pl.ds(i, 1), pl.ds(j, 1)
        chain[2, at_i, :] = eb
        chain[5, at_j, :] = et
        low = d0[i:i + 1] + eb
        rho = c[i:i + 1] / (low + c[i:i + 1])
        low = d1[i:i + 1] + rho * low
        tau = w[i:i + 1] / (low + w[i:i + 1])
        chain[0, at_i, :] = rho
        chain[1, at_i, :] = tau
        high = d1[j:j + 1] + et
        sigma = c[j:j + 1] / (high + c[j:j + 1])
        high = d0[j:j + 1] + sigma * high
        chain[3, at_j, :] = sigma
        if j > 0:
            upsilon = w[j - 1:j] / (high + w[j - 1:j])
            chain[4, pl.ds(j - 1, 1), :] = upsilon
        links = [tau * low, upsilon * high]
    chain[4, pl.ds(GZ - 1, 1), :] = jnp.zeros((1, WIDTH), F32)
    tau, upsilon = chain[1], chain[4]
    climb = up(tau * chain[0], 1)
    descend = upsilon * down(chain[3], 1)
    from_below, from_above = [None, up(tau, 1)], [None, upsilon]
    for k in range(2, GZ):
        from_below.append(climb * up(from_below[-1], 1))
        from_above.append(descend * down(from_above[-1], 1))
    gains[...] = jnp.zeros_like(gains)
    for k in range(1, GZ):
        spread(gains, 24, k, from_below[k] + from_above[GZ - k])
    spread(gains, 24, GZ, chain[2])
    spread(gains, 24, GZ + 1, chain[5])
    wait_gains = everyone(gains, taken, 2, 48, ROUND_FIRST, False)
    wait_sol()

    def substitute(first, last, merge):
        u = {0: first, DEPTH - 1: last}
        merge(0, u[0])
        merge(DEPTH - 1, u[DEPTH - 1])
        for level in reversed(LEVELS):
            for n, a, b in level:
                u[n] = ff[n] * iv[n] + ll[n] * u[a] + rr[n] * u[b]
                merge(n, u[n])

    tint = colour[...]

    def merge_half(z, u):
        half[z] = jnp.where(tint == 0, u, pressure[z])

    substitute(take(sol, 0), take(sol, 1), merge_half)
    pack(half, xs2, ys2)
    wait_half = halo(2, xs2, xh2, ys2, yh2)

    def gain(k):
        return jnp.concatenate(
            [taken[pl.ds(24 * h + k, 8, stride=48), :] for h in range(2)], axis=1
        )

    wait_gains()
    c = cc[0]
    low = dd[0] + gain(GZ)
    high = dd[DEPTH - 1] + gain(GZ + 1)
    low_inv = 1.0 / (low + c)
    rho = c * low_inv
    sigma = c / (high + c)
    high_inv = 1.0 / (high + rho * low)
    wait_half()
    for z in range(DEPTH):
        vw, ve, vs, vn = beside(half[z], *edges(z, xh2, yh2))
        ff[z] = source[z] + ww[z] * vw + we[z] * ve + ws[z] * vs + wn[z] * vn
    for level in LEVELS:
        for n, a, b in level:
            f = ff[n]
            ff[a] = ff[a] + ll[n] * f
            ff[b] = ff[b] + rr[n] * f
    f0, f1 = ff[0], ff[DEPTH - 1]
    sums[0] = f1 + rho * f0
    sums[1] = f0 + sigma * f1

    def cast(i):
        peer = lax.rem(gz + i, GZ)
        return pltpu.make_async_remote_copy(
            src_ref=sums.at[lax.div(gz + i, GZ)], dst_ref=others.at[gz],
            send_sem=gz_send.at[3, peer], recv_sem=gz_recv.at[3, gz],
            device_id={"gz": peer}, device_id_type=MESH,
        )

    def heard(i):
        peer = lax.rem(gz + GZ - i, GZ)
        return pltpu.make_async_remote_copy(
            src_ref=sums.at[0], dst_ref=others.at[peer],
            send_sem=gz_send.at[3, peer], recv_sem=gz_recv.at[3, peer],
            device_id={"gz": peer}, device_id_type=MESH,
        )

    def drain_cast():
        for i in FAR_FIRST:
            cast(i).wait_send()

    for i in FAR_FIRST:
        cast(i).start()
    drains.append(drain_cast)
    for i in FAR_FIRST:
        heard(i).wait_recv()
    for i in range(1, GZ):
        part = gain(i) * others[lax.rem(gz + GZ - i, GZ)]
        f0 = f0 + jnp.where(gz >= i, part, 0.0)
        f1 = f1 + jnp.where(gz >= i, 0.0, part)
    last = (f1 + rho * f0) * high_inv
    first = f0 * low_inv + rho * last

    def merge_out(z, u):
        out[z] = jnp.where(tint == 1, u, half[z])

    substitute(first, last, merge_out)
    for drain in drains:
        drain()


def pin(value):
    return pltpu.with_memory_space_constraint(value, pltpu.HBM)


def field_call(spectral, shifts, colour, pressure, source):
    vmem = pl.BlockSpec(memory_space=pltpu.VMEM)
    hbm = pl.BlockSpec(memory_space=pltpu.HBM)
    block = (DEPTH, ITEMS, WIDTH)
    field = pltpu.VMEM(block, F32)
    board = pltpu.VMEM((8 * GZ, 128), F32)
    pair_board = pltpu.VMEM((16 * GZ, 128), F32)
    columns = pltpu.VMEM((2, ITEMS, 128), F32)
    rows = pltpu.VMEM((2, DEPTH, WIDTH), F32)
    dma = pltpu.SemaphoreType.DMA
    return pl.pallas_call(
        field_kernel,
        out_shape=[jax.ShapeDtypeStruct(block, F32)] * 2,
        in_specs=[hbm] * 8,
        out_specs=[vmem, vmem],
        scratch_shapes=[
            pltpu.VMEM((GX, 2, 4, 8, WIDTH), F32),
            pltpu.VMEM((2, GX, ROWS, WIDTH), F32),
            pltpu.VMEM((256, 512), BF16),
            pltpu.VMEM((256, 512), BF16),
            pltpu.VMEM((256, WIDTH), F32),
            pltpu.VMEM((256, WIDTH), BF16),
            pltpu.VMEM((256, WIDTH), BF16),
            pltpu.VMEM((GX, 4, 8, WIDTH), F32),
            pltpu.VMEM((2, 512, WIDTH), BF16),
            pltpu.VMEM((2, GX, WIDTH), F32),
            pltpu.VMEM((WIDTH, WIDTH), BF16),
            dma((GX,)), dma((GX,)), dma((GX,)), dma((GX,)), dma((8,)),
            field, field, pltpu.VMEM((ITEMS, WIDTH), jnp.int32),
            pltpu.VMEM((ITEMS, DEPTH), jnp.int32),
        ]
        + [field] * 12
        + [columns, columns, rows, rows] * 3
        + [board, pair_board, pair_board, board]
        + [
            pltpu.VMEM((48 * GZ, 128), F32),
            pltpu.VMEM((24 * GZ, 128), F32),
            pltpu.VMEM((6, GZ, WIDTH), F32),
            pltpu.VMEM((2, ITEMS, WIDTH), F32),
            pltpu.VMEM((GZ, ITEMS, WIDTH), F32),
        ]
        + [dma((3, 4)), dma((3, 4)), dma((4, GZ)), dma((4, GZ))]
        + [pltpu.SemaphoreType.REGULAR((RELAYS,))],
        compiler_params=pltpu.CompilerParams(
            collective_id=0, has_side_effects=True, vmem_limit_bytes=32 << 20
        ),
        name="field",
    )(
        *map(pin, (spectral, shifts.T, *map(jnp.asarray, tables()), pressure, source, colour))
    )


def body(spectral, shifts, colour, pressure, source):
    log_perm, smoothed = field_call(spectral, shifts, colour, pressure, source)
    return (log_perm, smoothed)


def solution(mesh):
    in_specs = (
        P(None, "gz", "gy", "gx"),
        P("gz", "gy"),
        P("gy", "gx"),
        P("gz", "gy", "gx"),
        P("gz", "gy", "gx"),
    )
    out_specs = (P("gz", "gy", "gx"), P("gz", "gy", "gx"))
    return jax.shard_map(body, mesh=mesh, in_specs=in_specs, out_specs=out_specs, check_vma=False)
```

```python
import functools
import math

import jax
import jax.numpy as jnp
import ml_dtypes
import numpy as np
from jax import lax
from jax.experimental import pallas as pl
from jax.experimental.pallas import tpu as pltpu
from jax.sharding import PartitionSpec as P

NX = 2048
STORE = 1.0
VERT = 65536.0
MESH = pl.DeviceIdType.MESH
GX = 8
GY = 4
GZ = 16
DEPTH = 32
ITEMS = 8
WIDTH = 256
ROWS = 32
FAR_FIRST = (9, 7, 11, 5, 13, 3, 8, 15, 1, 10, 6, 12, 4, 14, 2)
RELAYS = 4
ROUND_FIRST = (8, 6, 10, 4, 12, 2, 14)
F32 = jnp.float32
BF16 = jnp.bfloat16


def tables():
    j = np.arange(WIDTH)
    angle = 2.0 * np.pi * ((j[:, None] * j[None, :]) % WIDTH) / WIDTH
    dft = np.concatenate([np.cos(angle), -np.sin(angle)], axis=0) / math.sqrt(NX)
    high = dft.astype(ml_dtypes.bfloat16)
    low = (dft - high.astype(np.float64)).astype(ml_dtypes.bfloat16)
    dft_pair = np.stack([high, low])
    r = np.arange(GX)
    turn = 2.0 * np.pi * (r[:, None] * j[None, :]) / NX
    twiddle = np.stack([np.cos(turn), np.sin(turn)]).astype(np.float32)
    order = np.zeros((WIDTH, WIDTH), np.float32)
    for rr in range(8):
        for p in range(32):
            order[32 * rr + p, 8 * p + rr] = 1.0
    return dft_pair, twiddle, order.astype(ml_dtypes.bfloat16)


def cos_sin(turns):
    quadrant = (turns + 256) >> 9
    x = (turns - (quadrant << 9)).astype(F32) * (2.0 * math.pi / NX)
    x2 = x * x
    sine = x * (1.0 + x2 * (-1.0 / 6 + x2 * (1.0 / 120 + x2 * (-1.0 / 5040 + x2 * (1.0 / 362880)))))
    cosine = 1.0 + x2 * (-0.5 + x2 * (1.0 / 24 + x2 * (-1.0 / 720 + x2 * (1.0 / 40320))))
    swap = (quadrant & 1) == 1
    c = jnp.where(swap, sine, cosine)
    s = jnp.where(swap, cosine, sine)
    c = jnp.where(((quadrant + 1) & 2) == 2, -c, c)
    s = jnp.where((quadrant & 2) == 2, -s, s)
    return c, s


def dft4(z):
    (r0, i0), (r1, i1), (r2, i2), (r3, i3) = z
    ar, ai, br, bi = r0 + r2, i0 + i2, r0 - r2, i0 - i2
    cr, ci, dr, di = r1 + r3, i1 + i3, r1 - r3, i1 - i3
    return [(ar + cr, ai + ci), (br - di, bi + dr), (ar - cr, ai - ci), (br + di, bi - dr)]


def dft8(t):
    root = math.sqrt(0.5)
    even = [(t[k][0] + t[k + 4][0], t[k][1] + t[k + 4][1]) for k in range(4)]
    odd = [(t[k][0] - t[k + 4][0], t[k][1] - t[k + 4][1]) for k in range(4)]
    o1 = (root * (odd[1][0] - odd[1][1]), root * (odd[1][0] + odd[1][1]))
    o2 = (-odd[2][1], odd[2][0])
    o3 = (-root * (odd[3][0] + odd[3][1]), root * (odd[3][0] - odd[3][1]))
    ev = dft4(even)
    od = dft4([odd[0], o1, o2, o3])
    out = []
    for m in range(4):
        out += [ev[m], od[m]]
    return out


def split(value):
    high = value.astype(BF16)
    return high, (value - high.astype(F32)).astype(BF16)


def spectral_part(
    spec, shifts, dft_hbm, twiddle_hbm, order_hbm, out,
    xb, trig, lhs_hi, lhs_lo, zb, wb_hi, wb_lo, sb, dft, twiddle, order,
    send1, recv1, send2, recv2, local, greet_all, meanwhile, spill,
):
    me = lax.axis_index("gx")

    def mine(slot):
        return pl.ds(4 * slot, 4)

    own = pltpu.make_async_copy(spec.at[:, mine(me)], xb.at[me], local.at[0])
    own.start()
    dft_copy = pltpu.make_async_copy(dft_hbm, dft, local.at[1])
    dft_copy.start()
    order_copy = pltpu.make_async_copy(order_hbm, order, local.at[2])
    order_copy.start()
    twiddle_copy = pltpu.make_async_copy(twiddle_hbm, twiddle, local.at[3])
    twiddle_copy.start()
    greet_all()

    def first(peer, slot, who):
        return pltpu.make_async_remote_copy(
            src_ref=spec.at[:, mine(peer)], dst_ref=xb.at[slot],
            send_sem=send1.at[peer], recv_sem=recv1.at[slot],
            device_id={"gx": who}, device_id_type=MESH,
        )

    for i in range(1, GX):
        peer = lax.rem(me + i, GX)
        first(peer, me, peer).start()
    meanwhile()

    lane = lax.broadcasted_iota(jnp.int32, (8, WIDTH), 1)
    lane0 = lax.broadcasted_iota(jnp.int32, (ITEMS, DEPTH), 1)
    for z in range(4):
        row = jnp.where(lane0 == 4 * me + z, shifts[...].astype(F32), 0.0)
        shift = jnp.sum(row, axis=1, keepdims=True).astype(jnp.int32)
        shift = jnp.broadcast_to(shift, (8, WIDTH))

        def make_trig(d, carry, z=z, shift=shift):
            c, s = cos_sin((shift * (lane + d * WIDTH)) & (NX - 1))
            trig[0, d, pl.ds(8 * z, 8), :] = c
            trig[1, d, pl.ds(8 * z, 8), :] = s
            return carry

        lax.fori_loop(0, GX, make_trig, 0)

    own.wait()
    for i in range(1, GX):
        peer = lax.rem(me + GX - i, GX)
        first(peer, peer, peer).wait_recv()

    twiddle_copy.wait()
    for zz in range(2):
        rows = pl.ds(16 * zz, 16)
        for h in range(2):
            cols = pl.ds(128 * h, 128)
            t = []
            for d in range(GX):
                xr = xb[d, 0, pl.ds(2 * zz, 2), :, cols].reshape(16, 128)
                xi = xb[d, 1, pl.ds(2 * zz, 2), :, cols].reshape(16, 128)
                c = trig[0, d, rows, cols]
                s = trig[1, d, rows, cols]
                t.append((xr * c - xi * s, xr * s + xi * c))
            y = dft8(t)
            for r in range(8):
                yr, yi = y[r]
                if r > 0:
                    c = twiddle[0, pl.ds(r, 1), cols]
                    s = twiddle[1, pl.ds(r, 1), cols]
                    yr, yi = yr * c - yi * s, yr * s + yi * c
                place = pl.ds(32 * r + 16 * zz, 16)
                hi, lo = split(yr)
                lhs_hi[place, pl.ds(128 * h, 128)] = hi
                lhs_lo[place, pl.ds(128 * h, 128)] = lo
                hi, lo = split(yi)
                lhs_hi[place, pl.ds(256 + 128 * h, 128)] = hi
                lhs_lo[place, pl.ds(256 + 128 * h, 128)] = lo

    dft_copy.wait()
    zb[...] = (
        jnp.dot(lhs_hi[...], dft[0], preferred_element_type=F32)
        + jnp.dot(lhs_hi[...], dft[1], preferred_element_type=F32)
        + jnp.dot(lhs_lo[...], dft[0], preferred_element_type=F32)
    )
    group = lax.broadcasted_iota(jnp.int32, (ROWS, 128), 1) // 32
    for e in range(8):
        column, g = e // 4, e % 4
        for h in range(2):
            total = None
            for rr in range(4):
                r = 4 * h + rr
                tile = zb[pl.ds(32 * r, 32), pl.ds(128 * column, 128)]
                turn = (32 * (rr - g)) % 128
                if turn:
                    tile = pltpu.roll(tile, turn, 1)
                total = tile if total is None else jnp.where(group == rr, tile, total)
            hi, lo = split(total)
            wb_hi[pl.ds(32 * e, 32), pl.ds(128 * h, 128)] = hi
            wb_lo[pl.ds(32 * e, 32), pl.ds(128 * h, 128)] = lo
    order_copy.wait()
    natural = jnp.dot(wb_hi[...], order[...], preferred_element_type=F32) + jnp.dot(
        wb_lo[...], order[...], preferred_element_type=F32
    )
    sb[...] = natural.reshape(8, 4, 8, WIDTH)

    def second(peer, slot, who):
        return pltpu.make_async_remote_copy(
            src_ref=sb.at[peer], dst_ref=out.at[mine(slot)],
            send_sem=send2.at[peer], recv_sem=recv2.at[slot],
            device_id={"gx": who}, device_id_type=MESH,
        )

    spill()
    for i in range(1, GX):
        peer = lax.rem(me + i, GX)
        second(peer, me, peer).start()
    out[mine(me)] = sb[me]
    for i in range(1, GX):
        peer = lax.rem(me + GX - i, GX)
        second(peer, peer, peer).wait_recv()

    def drain():
        for i in range(1, GX):
            peer = lax.rem(me + i, GX)
            first(peer, me, peer).wait_send()
            second(peer, me, peer).wait_send()

    return drain


def harmonic(center, beside):
    return 2.0 * center * beside / (center + beside)


LEVELS = (
    [(n, n - 1, n + 1) for n in range(1, 31, 2)],
    [(n, n - 2, min(n + 2, 31)) for n in range(2, 31, 4)],
    [(n, n - 4, min(n + 4, 31)) for n in range(4, 31, 8)],
    [(8, 0, 16), (24, 16, 31)],
    [(16, 0, 31)],
)


def field_kernel(
    spec, shifts_hbm, dft_hbm, twiddle_hbm, order_hbm, pressure_hbm, source_hbm, colour_hbm,
    log_perm, out, *scratch,
):
    (
        xb, trig, lhs_hi, lhs_lo, zb, wb_hi, wb_lo, sb, dft, twiddle, order,
        send1, recv1, send2, recv2, local,
        pressure, source, colour, shifts,
        perm, half, ww, we, ws, wn, dd, ff, cc, ll, rr, iv,
        xs0, xh0, ys0, yh0, xspill, xgot, yspill, ygot, xs2, xh2, ys2, yh2,
        msg, got, ans, sol, gains, taken, chain, sums, others,
        halo_send, halo_recv, gz_send, gz_recv, relay, spill_send, spill_recv,
    ) = scratch
    gx = lax.axis_index("gx")
    gy = lax.axis_index("gy")
    gz = lax.axis_index("gz")
    left, right = lax.rem(gx + GX - 1, GX), lax.rem(gx + 1, GX)
    south, north = lax.rem(gy + GY - 1, GY), lax.rem(gy + 1, GY)
    drains = []
    twin = gz + 1 - 2 * lax.rem(gz, 2)
    round_neighbours = (lax.rem(gz + 2, GZ), lax.rem(gz + GZ - 2, GZ))

    pressure_copy = pltpu.make_async_copy(pressure_hbm, pressure, local.at[4])
    source_copy = pltpu.make_async_copy(source_hbm, source, local.at[5])
    shifts_copy = pltpu.make_async_copy(shifts_hbm, shifts, local.at[7])
    colour_copy = pltpu.make_async_copy(colour_hbm, colour, local.at[6])

    def greet_all():
        barrier = pltpu.get_barrier_semaphore()

        for peer in (twin, *round_neighbours):
            pl.semaphore_signal(barrier, inc=1, device_id={"gz": peer}, device_id_type=MESH)
        for i in range(1, GX):
            peer = lax.rem(gx + i, GX)
            pl.semaphore_signal(barrier, inc=1, device_id={"gx": peer}, device_id_type=MESH)
        for who in (south, north):
            pl.semaphore_signal(barrier, inc=1, device_id={"gy": who}, device_id_type=MESH)
        shifts_copy.start()
        pressure_copy.start()
        source_copy.start()
        colour_copy.start()
        pl.semaphore_wait(barrier, GX - 1 + 3 + 2)

    lane1 = lax.broadcasted_iota(jnp.int32, (8, 128), 1)
    lane = lax.broadcasted_iota(jnp.int32, (8, WIDTH), 1)
    sub = lax.broadcasted_iota(jnp.int32, (8, WIDTH), 0)

    def pack(source_ref, xs, ys):
        west = jnp.zeros((8, 128), F32)
        east = jnp.zeros((8, 128), F32)
        for z in range(DEPTH):
            tile = source_ref[z]
            west = jnp.where(lane1 == z, tile[:, 0:1], west)
            east = jnp.where(lane1 == z, tile[:, 255:256], east)
            ys[0, pl.ds(z, 1), :] = tile[0:1, :]
            ys[1, pl.ds(z, 1), :] = tile[7:8, :]
        xs[0] = west
        xs[1] = east

    sides = (
        (0, 1, {"gx": left}, gx > 0, gx < GX - 1),
        (1, 0, {"gx": right}, gx < GX - 1, gx > 0),
        (0, 1, {"gy": south}, gy > 0, gy < GY - 1),
        (1, 0, {"gy": north}, gy < GY - 1, gy > 0),
    )

    def halo(phase, xs, xh, ys, yh):
        def copy(k):
            src, dst = (xs, xh) if k < 2 else (ys, yh)
            side, there, who, _, _ = sides[k]
            return pltpu.make_async_remote_copy(
                src_ref=src.at[side], dst_ref=dst.at[there],
                send_sem=halo_send.at[phase, k], recv_sem=halo_recv.at[phase, k],
                device_id=who, device_id_type=MESH,
            )

        def each(which, action):
            for k in range(4):
                pl.when(sides[k][which])(functools.partial(action, k))

        def blank(k):
            dst = xh if k < 2 else yh
            there = sides[k][1]

            def fill():
                dst[there] = jnp.zeros(dst.shape[1:], F32)

            pl.when(jnp.logical_not(sides[k][4]))(fill)

        each(3, lambda k: copy(k).start())
        for k in range(4):
            blank(k)
        drains.append(lambda: each(3, lambda k: copy(k).wait_send()))
        return lambda: each(4, lambda k: copy(k).wait_recv())

    arrived = []

    def meanwhile():
        pressure_copy.wait()
        pack(pressure, xs0, ys0)
        arrived.append(halo(0, xs0, xh0, ys0, yh0))
        shifts_copy.wait()
        for turn in range(RELAYS):
            for peer in round_neighbours:
                pl.semaphore_signal(
                    relay.at[turn], inc=1, device_id={"gz": peer}, device_id_type=MESH
                )
            pl.semaphore_wait(relay.at[turn], 2)
        for who in (south, north):
            pl.semaphore_signal(
                relay.at[RELAYS], inc=1, device_id={"gy": who}, device_id_type=MESH
            )
        pl.semaphore_wait(relay.at[RELAYS], 2)

    def column_copy(peer, slot):
        return pltpu.make_async_remote_copy(
            src_ref=xspill.at[peer], dst_ref=xgot.at[slot],
            send_sem=spill_send.at[2, peer], recv_sem=spill_recv.at[2, slot],
            device_id={"gx": peer}, device_id_type=MESH,
        )

    rims = ((1, south, gy > 0, gy < GY - 1), (0, north, gy < GY - 1, gy > 0))

    def rim_copy(k, peer, slot):
        there, who, _, _ = rims[k]
        return pltpu.make_async_remote_copy(
            src_ref=yspill.at[k, peer], dst_ref=ygot.at[there, slot],
            send_sem=spill_send.at[k, peer], recv_sem=spill_recv.at[k, slot],
            device_id={"gx": peer, "gy": who}, device_id_type=MESH,
        )

    def spill():
        for k, y in ((0, 0), (1, 7)):
            for e in range(GX):
                for z in range(4):
                    edge = sb[e, z][y:y + 1, :]
                    for h in range(2):
                        yspill[k, e, pl.ds(2 * z + h, 1), :] = edge[:, 128 * h:128 * h + 128]
            yspill[k] = jnp.exp(yspill[k])
            there, _, sends, receives = rims[k]

            def start(k=k):
                for i in range(GX):
                    rim_copy(k, lax.rem(gx + i, GX), gx).start()

            def drain(k=k):
                for i in range(GX):
                    rim_copy(k, lax.rem(gx + i, GX), gx).wait_send()

            def blank(there=there):
                ygot[there] = jnp.zeros(ygot.shape[1:], F32)

            pl.when(sends)(start)
            pl.when(jnp.logical_not(receives))(blank)
            drains.append(lambda sends=sends, drain=drain: pl.when(sends)(drain))
        for e in range(GX):
            tile = jnp.zeros((8, 128), F32)
            for z in range(4):
                if e > 0:
                    tile = jnp.where(lane1 == 2 * z, sb[e - 1, z][:, 255:256], tile)
                if e < GX - 1:
                    tile = jnp.where(lane1 == 2 * z + 1, sb[e + 1, z][:, 0:1], tile)
            tile = jnp.exp(tile)
            if e == 0:
                tile = jnp.where(lane1 % 2 == 0, 0.0, tile)
            if e == GX - 1:
                tile = jnp.where(lane1 % 2 == 1, 0.0, tile)
            xspill[e] = tile
        for i in range(1, GX):
            column_copy(lax.rem(gx + i, GX), gx).start()
        xgot[gx] = xspill[gx]

        def drain_columns():
            for i in range(1, GX):
                column_copy(lax.rem(gx + i, GX), gx).wait_send()

        drains.append(drain_columns)

    def wait_spill():
        for i in range(1, GX):
            peer = lax.rem(gx + GX - i, GX)
            column_copy(peer, peer).wait_recv()
        for k in range(2):

            def wait(k=k):
                for i in range(GX):
                    peer = lax.rem(gx + GX - i, GX)
                    rim_copy(k, peer, peer).wait_recv()

            pl.when(rims[k][3])(wait)

    drains.append(
        spectral_part(
            spec, shifts, dft_hbm, twiddle_hbm, order_hbm, log_perm,
            xb, trig, lhs_hi, lhs_lo, zb, wb_hi, wb_lo, sb, dft, twiddle, order,
            send1, recv1, send2, recv2, local, greet_all, meanwhile, spill,
        )
    )

    def make_perm(z, carry):
        perm[z] = jnp.exp(log_perm[z])
        return carry

    lax.fori_loop(0, DEPTH, make_perm, 0, unroll=4)
    source_copy.wait()
    colour_copy.wait()
    arrived[0]()
    wait_spill()

    def beside(value, west, east, lower, upper):
        vw = jnp.where(lane == 0, west, pltpu.roll(value, 1, 1))
        ve = jnp.where(lane == WIDTH - 1, east, pltpu.roll(value, WIDTH - 1, 1))
        vs = jnp.where(sub == 0, lower, pltpu.roll(value, 1, 0))
        vn = jnp.where(sub == 7, upper, pltpu.roll(value, 7, 0))
        return vw, ve, vs, vn

    def spilled(z):
        owner, place = z // 4, 2 * (z % 4)
        west = xgot[owner][:, place:place + 1]
        east = xgot[owner][:, place + 1:place + 2]
        lower, upper = (
            jnp.concatenate(
                [ygot[k, owner, pl.ds(place + h, 1), :] for h in range(2)], axis=1
            )
            for k in range(2)
        )
        return west, east, lower, upper

    def edges(z, xh, yh):
        west = xh[0][:, z:z + 1]
        east = xh[1][:, z:z + 1]
        lower = yh[0, pl.ds(z, 1), :]
        upper = yh[1, pl.ds(z, 1), :]
        return west, east, lower, upper

    for z in range(DEPTH):
        p = perm[z]
        pw, pe, ps, pn = beside(p, *spilled(z))
        aw, ae, as_, an = harmonic(p, pw), harmonic(p, pe), harmonic(p, ps), harmonic(p, pn)
        ww[z], we[z], ws[z], wn[z] = aw, ae, as_, an
        dd[z] = STORE + aw + ae + as_ + an
        vw, ve, vs, vn = beside(pressure[z], *edges(z, xh0, yh0))
        ff[z] = source[z] + aw * vw + ae * ve + as_ * vs + an * vn
        if z < DEPTH - 1:
            cc[z] = VERT * harmonic(p, perm[z + 1])

    for level in LEVELS:
        for n, a, b in level:
            wl, wr, d, f = cc[a], cc[n], dd[n], ff[n]
            inv = 1.0 / (d + wl + wr)
            l, r = wl * inv, wr * inv
            ll[n], rr[n], iv[n] = l, r, inv
            cc[a] = l * wr
            dd[a] = dd[a] + l * d
            dd[b] = dd[b] + r * d
            ff[a] = ff[a] + l * f
            ff[b] = ff[b] + r * f

    def put(ref, kind, value):
        for h in range(2):
            ref[pl.ds(8 * h + kind, 8, stride=16), :] = value[:, 128 * h:128 * h + 128]

    def take(ref, kind):
        return jnp.concatenate(
            [ref[pl.ds(8 * h + kind, 8, stride=16), :] for h in range(2)], axis=1
        )

    row = lax.div(gz, 2)

    def everyone(src, dst, phase, size, offsets, to_owner):
        def tile(index):
            return pl.ds(pl.multiple_of(size * index, 8), size)

        def copy(peer, slot, first, then):
            return pltpu.make_async_remote_copy(
                src_ref=src.at[tile(first)], dst_ref=dst.at[tile(then)],
                send_sem=gz_send.at[phase, peer], recv_sem=gz_recv.at[phase, slot],
                device_id={"gz": peer}, device_id_type=MESH,
            )

        def outward(i):
            peer = lax.rem(gz + i, GZ)
            if to_owner:
                return copy(peer, gz, lax.div(peer, 2), gz)
            return copy(peer, gz, peer, row)

        def inward(i):
            peer = lax.rem(gz + GZ - i, GZ)
            if to_owner:
                return copy(peer, peer, 0, peer)
            return copy(peer, peer, 0, lax.div(peer, 2))

        def finish():
            for i in offsets:
                inward(i).wait_recv()

        def drain():
            for i in offsets:
                outward(i).wait_send()

        for i in offsets:
            outward(i).start()
        if to_owner:
            dst[tile(gz), :] = src[tile(row), :]
        else:
            dst[tile(row), :] = src[tile(gz), :]
        drains.append(drain)
        return finish

    put(msg, 0, dd[0])
    put(msg, 1, dd[DEPTH - 1])
    put(msg, 2, cc[0])
    put(msg, 3, perm[0])
    put(msg, 4, perm[DEPTH - 1])
    put(msg, 5, ff[0])
    put(msg, 6, ff[DEPTH - 1])
    put(msg, 7, ff[0])
    everyone(msg, got, 0, 16, FAR_FIRST, True)()

    def kind(ref, k):
        return jnp.concatenate(
            [ref[pl.ds(8 * h + k, GZ, stride=16), :] for h in range(2)], axis=1
        )

    def spread(ref, size, k, value):
        for h in range(2):
            ref[pl.ds(size * h + k, GZ, stride=2 * size), :] = value[:, 128 * h:128 * h + 128]

    d0, d1, c, p0, p1 = (kind(got, k) for k in range(5))
    f0, f1 = kind(got, 5), kind(got, 6)
    segment = lax.broadcasted_iota(jnp.int32, (GZ, WIDTH), 0)
    w = jnp.where(segment < GZ - 1, VERT * harmonic(p1, pltpu.roll(p0, GZ - 1, 0)), 0.0)
    last_inv = 1.0 / (d1 + c + w)
    last_l, last_r = c * last_inv, w * last_inv

    def up(value, step):
        return pltpu.roll(value, step, 0)

    def down(value, step):
        return pltpu.roll(value, GZ - step, 0)

    e = d0 + last_l * d1 + up(last_r * d1, 1)
    b = last_l * w
    a = up(b, 1)
    f = f0 + last_l * f1 + up(last_r * f1, 1)
    for step in (1, 2, 4, 8):
        inv = 1.0 / (e + a + b)
        alpha, beta = a * up(inv, step), b * down(inv, step)
        e = e + alpha * up(e, step) + beta * down(e, step)
        f = f + alpha * up(f, step) + beta * down(f, step)
        if step < 8:
            a, b = alpha * up(a, step), beta * down(b, step)
    first = f / e
    ans[...] = jnp.zeros_like(ans)
    spread(ans, 8, 0, first)
    spread(ans, 8, 1, f1 * last_inv + last_l * first + last_r * down(first, 1))
    wait_sol = everyone(ans, sol, 1, 16, ROUND_FIRST, False)

    links = [jnp.zeros((1, WIDTH), F32)] * 2
    for i in range(GZ):
        j = GZ - 1 - i
        eb, et = links
        at_i, at_j = pl.ds(i, 1), pl.ds(j, 1)
        chain[2, at_i, :] = eb
        chain[5, at_j, :] = et
        low = d0[i:i + 1] + eb
        rho = c[i:i + 1] / (low + c[i:i + 1])
        low = d1[i:i + 1] + rho * low
        tau = w[i:i + 1] / (low + w[i:i + 1])
        chain[0, at_i, :] = rho
        chain[1, at_i, :] = tau
        high = d1[j:j + 1] + et
        sigma = c[j:j + 1] / (high + c[j:j + 1])
        high = d0[j:j + 1] + sigma * high
        chain[3, at_j, :] = sigma
        if j > 0:
            upsilon = w[j - 1:j] / (high + w[j - 1:j])
            chain[4, pl.ds(j - 1, 1), :] = upsilon
        links = [tau * low, upsilon * high]
    chain[4, pl.ds(GZ - 1, 1), :] = jnp.zeros((1, WIDTH), F32)
    tau, upsilon = chain[1], chain[4]
    climb = up(tau * chain[0], 1)
    descend = upsilon * down(chain[3], 1)
    from_below, from_above = [None, up(tau, 1)], [None, upsilon]
    for k in range(2, GZ):
        from_below.append(climb * up(from_below[-1], 1))
        from_above.append(descend * down(from_above[-1], 1))
    gains[...] = jnp.zeros_like(gains)
    for k in range(1, GZ):
        spread(gains, 24, k, from_below[k] + from_above[GZ - k])
    spread(gains, 24, GZ, chain[2])
    spread(gains, 24, GZ + 1, chain[5])
    wait_gains = everyone(gains, taken, 2, 48, ROUND_FIRST, False)
    wait_sol()

    def substitute(first, last, merge):
        u = {0: first, DEPTH - 1: last}
        merge(0, u[0])
        merge(DEPTH - 1, u[DEPTH - 1])
        for level in reversed(LEVELS):
            for n, a, b in level:
                u[n] = ff[n] * iv[n] + ll[n] * u[a] + rr[n] * u[b]
                merge(n, u[n])

    tint = colour[...]

    def merge_half(z, u):
        half[z] = jnp.where(tint == 0, u, pressure[z])

    substitute(take(sol, 0), take(sol, 1), merge_half)
    pack(half, xs2, ys2)
    wait_half = halo(2, xs2, xh2, ys2, yh2)

    def gain(k):
        return jnp.concatenate(
            [taken[pl.ds(24 * h + k, 8, stride=48), :] for h in range(2)], axis=1
        )

    wait_gains()
    c = cc[0]
    low = dd[0] + gain(GZ)
    high = dd[DEPTH - 1] + gain(GZ + 1)
    low_inv = 1.0 / (low + c)
    rho = c * low_inv
    sigma = c / (high + c)
    high_inv = 1.0 / (high + rho * low)
    wait_half()
    for z in range(DEPTH):
        vw, ve, vs, vn = beside(half[z], *edges(z, xh2, yh2))
        ff[z] = source[z] + ww[z] * vw + we[z] * ve + ws[z] * vs + wn[z] * vn
    for level in LEVELS:
        for n, a, b in level:
            f = ff[n]
            ff[a] = ff[a] + ll[n] * f
            ff[b] = ff[b] + rr[n] * f
    f0, f1 = ff[0], ff[DEPTH - 1]
    sums[0] = f1 + rho * f0
    sums[1] = f0 + sigma * f1

    def cast(i):
        peer = lax.rem(gz + i, GZ)
        return pltpu.make_async_remote_copy(
            src_ref=sums.at[lax.div(gz + i, GZ)], dst_ref=others.at[gz],
            send_sem=gz_send.at[3, peer], recv_sem=gz_recv.at[3, gz],
            device_id={"gz": peer}, device_id_type=MESH,
        )

    def heard(i):
        peer = lax.rem(gz + GZ - i, GZ)
        return pltpu.make_async_remote_copy(
            src_ref=sums.at[0], dst_ref=others.at[peer],
            send_sem=gz_send.at[3, peer], recv_sem=gz_recv.at[3, peer],
            device_id={"gz": peer}, device_id_type=MESH,
        )

    def drain_cast():
        for i in FAR_FIRST:
            cast(i).wait_send()

    for i in FAR_FIRST:
        cast(i).start()
    drains.append(drain_cast)
    for i in FAR_FIRST:
        heard(i).wait_recv()
    for i in range(1, GZ):
        part = gain(i) * others[lax.rem(gz + GZ - i, GZ)]
        f0 = f0 + jnp.where(gz >= i, part, 0.0)
        f1 = f1 + jnp.where(gz >= i, 0.0, part)
    last = (f1 + rho * f0) * high_inv
    first = f0 * low_inv + rho * last

    def merge_out(z, u):
        out[z] = jnp.where(tint == 1, u, half[z])

    substitute(first, last, merge_out)
    for drain in drains:
        drain()


def pin(value):
    return pltpu.with_memory_space_constraint(value, pltpu.HBM)


def field_call(spectral, shifts, colour, pressure, source):
    vmem = pl.BlockSpec(memory_space=pltpu.VMEM)
    hbm = pl.BlockSpec(memory_space=pltpu.HBM)
    block = (DEPTH, ITEMS, WIDTH)
    field = pltpu.VMEM(block, F32)
    board = pltpu.VMEM((8 * GZ, 128), F32)
    pair_board = pltpu.VMEM((16 * GZ, 128), F32)
    columns = pltpu.VMEM((2, ITEMS, 128), F32)
    rows = pltpu.VMEM((2, DEPTH, WIDTH), F32)
    tiles = pltpu.VMEM((GX, 8, 128), F32)
    dma = pltpu.SemaphoreType.DMA
    return pl.pallas_call(
        field_kernel,
        out_shape=[jax.ShapeDtypeStruct(block, F32)] * 2,
        in_specs=[hbm] * 8,
        out_specs=[vmem, vmem],
        scratch_shapes=[
            pltpu.VMEM((GX, 2, 4, 8, WIDTH), F32),
            pltpu.VMEM((2, GX, ROWS, WIDTH), F32),
            pltpu.VMEM((256, 512), BF16),
            pltpu.VMEM((256, 512), BF16),
            pltpu.VMEM((256, WIDTH), F32),
            pltpu.VMEM((256, WIDTH), BF16),
            pltpu.VMEM((256, WIDTH), BF16),
            pltpu.VMEM((GX, 4, 8, WIDTH), F32),
            pltpu.VMEM((2, 512, WIDTH), BF16),
            pltpu.VMEM((2, GX, WIDTH), F32),
            pltpu.VMEM((WIDTH, WIDTH), BF16),
            dma((GX,)), dma((GX,)), dma((GX,)), dma((GX,)), dma((8,)),
            field, field, pltpu.VMEM((ITEMS, WIDTH), jnp.int32),
            pltpu.VMEM((ITEMS, DEPTH), jnp.int32),
        ]
        + [field] * 12
        + [columns, columns, rows, rows]
        + [tiles, tiles, pltpu.VMEM((2, GX, 8, 128), F32), pltpu.VMEM((2, GX, 8, 128), F32)]
        + [columns, columns, rows, rows]
        + [board, pair_board, pair_board, board]
        + [
            pltpu.VMEM((48 * GZ, 128), F32),
            pltpu.VMEM((24 * GZ, 128), F32),
            pltpu.VMEM((6, GZ, WIDTH), F32),
            pltpu.VMEM((2, ITEMS, WIDTH), F32),
            pltpu.VMEM((GZ, ITEMS, WIDTH), F32),
        ]
        + [dma((3, 4)), dma((3, 4)), dma((4, GZ)), dma((4, GZ))]
        + [pltpu.SemaphoreType.REGULAR((RELAYS + 1,)), dma((3, GX)), dma((3, GX))],
        compiler_params=pltpu.CompilerParams(
            collective_id=0, has_side_effects=True, vmem_limit_bytes=32 << 20
        ),
        name="field",
    )(
        *map(pin, (spectral, shifts.T, *map(jnp.asarray, tables()), pressure, source, colour))
    )


def body(spectral, shifts, colour, pressure, source):
    log_perm, smoothed = field_call(spectral, shifts, colour, pressure, source)
    return (log_perm, smoothed)


def solution(mesh):
    in_specs = (
        P(None, "gz", "gy", "gx"),
        P("gz", "gy"),
        P("gy", "gx"),
        P("gz", "gy", "gx"),
        P("gz", "gy", "gx"),
    )
    out_specs = (P("gz", "gy", "gx"), P("gz", "gy", "gx"))
    return jax.shard_map(body, mesh=mesh, in_specs=in_specs, out_specs=out_specs, check_vma=False)
```

```python
import functools
import math

import jax
import jax.numpy as jnp
import ml_dtypes
import numpy as np
from jax import lax
from jax.experimental import pallas as pl
from jax.experimental.pallas import tpu as pltpu
from jax.sharding import PartitionSpec as P

NX = 2048
STORE = 1.0
VERT = 65536.0
MESH = pl.DeviceIdType.MESH
GX = 8
GY = 4
GZ = 16
DEPTH = 32
ITEMS = 8
WIDTH = 256
ROWS = 32
FAR_FIRST = (9, 7, 11, 5, 13, 3, 8, 15, 1, 10, 6, 12, 4, 14, 2)
RELAYS = 4
ROUND_FIRST = (8, 6, 10, 4, 12, 2, 14)
F32 = jnp.float32
BF16 = jnp.bfloat16


def tables():
    j = np.arange(WIDTH)
    angle = 2.0 * np.pi * ((j[:, None] * j[None, :]) % WIDTH) / WIDTH
    dft = np.concatenate([np.cos(angle), -np.sin(angle)], axis=0) / math.sqrt(NX)
    high = dft.astype(ml_dtypes.bfloat16)
    low = (dft - high.astype(np.float64)).astype(ml_dtypes.bfloat16)
    dft_pair = np.stack([high, low])
    r = np.arange(GX)
    turn = 2.0 * np.pi * (r[:, None] * j[None, :]) / NX
    twiddle = np.stack([np.cos(turn), np.sin(turn)]).astype(np.float32)
    order = np.zeros((WIDTH, WIDTH), np.float32)
    for rr in range(8):
        for p in range(32):
            order[32 * rr + p, 8 * p + rr] = 1.0
    return dft_pair, twiddle, order.astype(ml_dtypes.bfloat16)


def cos_sin(turns):
    quadrant = (turns + 256) >> 9
    x = (turns - (quadrant << 9)).astype(F32) * (2.0 * math.pi / NX)
    x2 = x * x
    sine = x * (1.0 + x2 * (-1.0 / 6 + x2 * (1.0 / 120 + x2 * (-1.0 / 5040 + x2 * (1.0 / 362880)))))
    cosine = 1.0 + x2 * (-0.5 + x2 * (1.0 / 24 + x2 * (-1.0 / 720 + x2 * (1.0 / 40320))))
    swap = (quadrant & 1) == 1
    c = jnp.where(swap, sine, cosine)
    s = jnp.where(swap, cosine, sine)
    c = jnp.where(((quadrant + 1) & 2) == 2, -c, c)
    s = jnp.where((quadrant & 2) == 2, -s, s)
    return c, s


def dft4(z):
    (r0, i0), (r1, i1), (r2, i2), (r3, i3) = z
    ar, ai, br, bi = r0 + r2, i0 + i2, r0 - r2, i0 - i2
    cr, ci, dr, di = r1 + r3, i1 + i3, r1 - r3, i1 - i3
    return [(ar + cr, ai + ci), (br - di, bi + dr), (ar - cr, ai - ci), (br + di, bi - dr)]


def dft8(t):
    root = math.sqrt(0.5)
    even = [(t[k][0] + t[k + 4][0], t[k][1] + t[k + 4][1]) for k in range(4)]
    odd = [(t[k][0] - t[k + 4][0], t[k][1] - t[k + 4][1]) for k in range(4)]
    o1 = (root * (odd[1][0] - odd[1][1]), root * (odd[1][0] + odd[1][1]))
    o2 = (-odd[2][1], odd[2][0])
    o3 = (-root * (odd[3][0] + odd[3][1]), root * (odd[3][0] - odd[3][1]))
    ev = dft4(even)
    od = dft4([odd[0], o1, o2, o3])
    out = []
    for m in range(4):
        out += [ev[m], od[m]]
    return out


def split(value):
    high = value.astype(BF16)
    return high, (value - high.astype(F32)).astype(BF16)


def spectral_part(
    spec, shifts, dft_hbm, twiddle_hbm, order_hbm, out,
    xb, trig, lhs_hi, lhs_lo, zb, wb_hi, wb_lo, sb, dft, twiddle, order,
    send1, recv1, send2, recv2, local, greet_all, meanwhile, spill,
):
    me = lax.axis_index("gx")

    def mine(slot):
        return pl.ds(4 * slot, 4)

    own = pltpu.make_async_copy(spec.at[:, mine(me)], xb.at[me], local.at[0])
    own.start()
    dft_copy = pltpu.make_async_copy(dft_hbm, dft, local.at[1])
    dft_copy.start()
    order_copy = pltpu.make_async_copy(order_hbm, order, local.at[2])
    order_copy.start()
    twiddle_copy = pltpu.make_async_copy(twiddle_hbm, twiddle, local.at[3])
    twiddle_copy.start()
    greet_all()

    def first(peer, slot, who):
        return pltpu.make_async_remote_copy(
            src_ref=spec.at[:, mine(peer)], dst_ref=xb.at[slot],
            send_sem=send1.at[peer], recv_sem=recv1.at[slot],
            device_id={"gx": who}, device_id_type=MESH,
        )

    for i in range(1, GX):
        peer = lax.rem(me + i, GX)
        first(peer, me, peer).start()
    meanwhile()

    lane = lax.broadcasted_iota(jnp.int32, (8, WIDTH), 1)
    lane0 = lax.broadcasted_iota(jnp.int32, (ITEMS, DEPTH), 1)
    for z in range(4):
        row = jnp.where(lane0 == 4 * me + z, shifts[...].astype(F32), 0.0)
        shift = jnp.sum(row, axis=1, keepdims=True).astype(jnp.int32)
        shift = jnp.broadcast_to(shift, (8, WIDTH))

        def make_trig(d, carry, z=z, shift=shift):
            c, s = cos_sin((shift * (lane + d * WIDTH)) & (NX - 1))
            trig[0, d, pl.ds(8 * z, 8), :] = c
            trig[1, d, pl.ds(8 * z, 8), :] = s
            return carry

        lax.fori_loop(0, GX, make_trig, 0)

    own.wait()
    for i in range(1, GX):
        peer = lax.rem(me + GX - i, GX)
        first(peer, peer, peer).wait_recv()

    twiddle_copy.wait()
    for zz in range(2):
        rows = pl.ds(16 * zz, 16)
        for h in range(2):
            cols = pl.ds(128 * h, 128)
            t = []
            for d in range(GX):
                xr = xb[d, 0, pl.ds(2 * zz, 2), :, cols].reshape(16, 128)
                xi = xb[d, 1, pl.ds(2 * zz, 2), :, cols].reshape(16, 128)
                c = trig[0, d, rows, cols]
                s = trig[1, d, rows, cols]
                t.append((xr * c - xi * s, xr * s + xi * c))
            y = dft8(t)
            for r in range(8):
                yr, yi = y[r]
                if r > 0:
                    c = twiddle[0, pl.ds(r, 1), cols]
                    s = twiddle[1, pl.ds(r, 1), cols]
                    yr, yi = yr * c - yi * s, yr * s + yi * c
                place = pl.ds(32 * r + 16 * zz, 16)
                hi, lo = split(yr)
                lhs_hi[place, pl.ds(128 * h, 128)] = hi
                lhs_lo[place, pl.ds(128 * h, 128)] = lo
                hi, lo = split(yi)
                lhs_hi[place, pl.ds(256 + 128 * h, 128)] = hi
                lhs_lo[place, pl.ds(256 + 128 * h, 128)] = lo

    dft_copy.wait()
    zb[...] = (
        jnp.dot(lhs_hi[...], dft[0], preferred_element_type=F32)
        + jnp.dot(lhs_hi[...], dft[1], preferred_element_type=F32)
        + jnp.dot(lhs_lo[...], dft[0], preferred_element_type=F32)
    )
    group = lax.broadcasted_iota(jnp.int32, (ROWS, 128), 1) // 32
    for e in range(8):
        column, g = e // 4, e % 4
        for h in range(2):
            total = None
            for rr in range(4):
                r = 4 * h + rr
                tile = zb[pl.ds(32 * r, 32), pl.ds(128 * column, 128)]
                turn = (32 * (rr - g)) % 128
                if turn:
                    tile = pltpu.roll(tile, turn, 1)
                total = tile if total is None else jnp.where(group == rr, tile, total)
            hi, lo = split(total)
            wb_hi[pl.ds(32 * e, 32), pl.ds(128 * h, 128)] = hi
            wb_lo[pl.ds(32 * e, 32), pl.ds(128 * h, 128)] = lo
    order_copy.wait()
    natural = jnp.dot(wb_hi[...], order[...], preferred_element_type=F32) + jnp.dot(
        wb_lo[...], order[...], preferred_element_type=F32
    )
    sb[...] = natural.reshape(8, 4, 8, WIDTH)

    def second(peer, slot, who):
        return pltpu.make_async_remote_copy(
            src_ref=sb.at[peer], dst_ref=out.at[mine(slot)],
            send_sem=send2.at[peer], recv_sem=recv2.at[slot],
            device_id={"gx": who}, device_id_type=MESH,
        )

    spill()
    for i in range(1, GX):
        peer = lax.rem(me + i, GX)
        second(peer, me, peer).start()
    out[mine(me)] = sb[me]
    for i in range(1, GX):
        peer = lax.rem(me + GX - i, GX)
        second(peer, peer, peer).wait_recv()

    def drain():
        for i in range(1, GX):
            peer = lax.rem(me + i, GX)
            first(peer, me, peer).wait_send()
            second(peer, me, peer).wait_send()

    return drain


def harmonic(center, beside):
    return 2.0 * center * beside / (center + beside)


LEVELS = (
    [(n, n - 1, n + 1) for n in range(1, 31, 2)],
    [(n, n - 2, min(n + 2, 31)) for n in range(2, 31, 4)],
    [(n, n - 4, min(n + 4, 31)) for n in range(4, 31, 8)],
    [(8, 0, 16), (24, 16, 31)],
    [(16, 0, 31)],
)


def field_kernel(
    spec, shifts_hbm, dft_hbm, twiddle_hbm, order_hbm, pressure_hbm, source_hbm, colour_hbm,
    both, *scratch,
):
    log_perm, out = both.at[0], both.at[1]
    (
        xb, trig, lhs_hi, lhs_lo, zb, wb_hi, wb_lo, sb, dft, twiddle, order,
        send1, recv1, send2, recv2, local,
        pressure, source, colour, shifts,
        perm, half, ww, we, ws, wn, dd, ff, cc, ll, rr, iv,
        xs0, xh0, ys0, yh0, xspill, xgot, yspill, ygot, xs2, xh2, ys2, yh2,
        msg, got, ans, sol, gains, taken, chain, sums, others,
        halo_send, halo_recv, gz_send, gz_recv, relay, spill_send, spill_recv,
    ) = scratch
    gx = lax.axis_index("gx")
    gy = lax.axis_index("gy")
    gz = lax.axis_index("gz")
    left, right = lax.rem(gx + GX - 1, GX), lax.rem(gx + 1, GX)
    south, north = lax.rem(gy + GY - 1, GY), lax.rem(gy + 1, GY)
    drains = []
    twin = gz + 1 - 2 * lax.rem(gz, 2)
    round_neighbours = (lax.rem(gz + 2, GZ), lax.rem(gz + GZ - 2, GZ))

    pressure_copy = pltpu.make_async_copy(pressure_hbm, pressure, local.at[4])
    source_copy = pltpu.make_async_copy(source_hbm, source, local.at[5])
    shifts_copy = pltpu.make_async_copy(shifts_hbm, shifts, local.at[7])
    colour_copy = pltpu.make_async_copy(colour_hbm, colour, local.at[6])

    def greet_all():
        barrier = pltpu.get_barrier_semaphore()

        for peer in (twin, *round_neighbours):
            pl.semaphore_signal(barrier, inc=1, device_id={"gz": peer}, device_id_type=MESH)
        for i in range(1, GX):
            peer = lax.rem(gx + i, GX)
            pl.semaphore_signal(barrier, inc=1, device_id={"gx": peer}, device_id_type=MESH)
        for who in (south, north):
            pl.semaphore_signal(barrier, inc=1, device_id={"gy": who}, device_id_type=MESH)
        shifts_copy.start()
        pressure_copy.start()
        source_copy.start()
        colour_copy.start()
        pl.semaphore_wait(barrier, GX - 1 + 3 + 2)

    lane1 = lax.broadcasted_iota(jnp.int32, (8, 128), 1)
    lane = lax.broadcasted_iota(jnp.int32, (8, WIDTH), 1)
    sub = lax.broadcasted_iota(jnp.int32, (8, WIDTH), 0)

    def pack(source_ref, xs, ys):
        west = jnp.zeros((8, 128), F32)
        east = jnp.zeros((8, 128), F32)
        for z in range(DEPTH):
            tile = source_ref[z]
            west = jnp.where(lane1 == z, tile[:, 0:1], west)
            east = jnp.where(lane1 == z, tile[:, 255:256], east)
            ys[0, pl.ds(z, 1), :] = tile[0:1, :]
            ys[1, pl.ds(z, 1), :] = tile[7:8, :]
        xs[0] = west
        xs[1] = east

    sides = (
        (0, 1, {"gx": left}, gx > 0, gx < GX - 1),
        (1, 0, {"gx": right}, gx < GX - 1, gx > 0),
        (0, 1, {"gy": south}, gy > 0, gy < GY - 1),
        (1, 0, {"gy": north}, gy < GY - 1, gy > 0),
    )

    def halo(phase, xs, xh, ys, yh):
        def copy(k):
            src, dst = (xs, xh) if k < 2 else (ys, yh)
            side, there, who, _, _ = sides[k]
            return pltpu.make_async_remote_copy(
                src_ref=src.at[side], dst_ref=dst.at[there],
                send_sem=halo_send.at[phase, k], recv_sem=halo_recv.at[phase, k],
                device_id=who, device_id_type=MESH,
            )

        def each(which, action):
            for k in range(4):
                pl.when(sides[k][which])(functools.partial(action, k))

        def blank(k):
            dst = xh if k < 2 else yh
            there = sides[k][1]

            def fill():
                dst[there] = jnp.zeros(dst.shape[1:], F32)

            pl.when(jnp.logical_not(sides[k][4]))(fill)

        each(3, lambda k: copy(k).start())
        for k in range(4):
            blank(k)
        drains.append(lambda: each(3, lambda k: copy(k).wait_send()))
        return lambda: each(4, lambda k: copy(k).wait_recv())

    arrived = []

    def meanwhile():
        pressure_copy.wait()
        pack(pressure, xs0, ys0)
        arrived.append(halo(0, xs0, xh0, ys0, yh0))
        shifts_copy.wait()
        for turn in range(RELAYS):
            for peer in round_neighbours:
                pl.semaphore_signal(
                    relay.at[turn], inc=1, device_id={"gz": peer}, device_id_type=MESH
                )
            pl.semaphore_wait(relay.at[turn], 2)
        for who in (south, north):
            pl.semaphore_signal(
                relay.at[RELAYS], inc=1, device_id={"gy": who}, device_id_type=MESH
            )
        pl.semaphore_wait(relay.at[RELAYS], 2)

    def column_copy(peer, slot):
        return pltpu.make_async_remote_copy(
            src_ref=xspill.at[peer], dst_ref=xgot.at[slot],
            send_sem=spill_send.at[2, peer], recv_sem=spill_recv.at[2, slot],
            device_id={"gx": peer}, device_id_type=MESH,
        )

    rims = ((1, south, gy > 0, gy < GY - 1), (0, north, gy < GY - 1, gy > 0))

    def rim_copy(k, peer, slot):
        there, who, _, _ = rims[k]
        return pltpu.make_async_remote_copy(
            src_ref=yspill.at[k, peer], dst_ref=ygot.at[there, slot],
            send_sem=spill_send.at[k, peer], recv_sem=spill_recv.at[k, slot],
            device_id={"gx": peer, "gy": who}, device_id_type=MESH,
        )

    def spill():
        for k, y in ((0, 0), (1, 7)):
            for e in range(GX):
                for z in range(4):
                    edge = sb[e, z][y:y + 1, :]
                    for h in range(2):
                        yspill[k, e, pl.ds(2 * z + h, 1), :] = edge[:, 128 * h:128 * h + 128]
            yspill[k] = jnp.exp(yspill[k])
            there, _, sends, receives = rims[k]

            def start(k=k):
                for i in range(GX):
                    rim_copy(k, lax.rem(gx + i, GX), gx).start()

            def drain(k=k):
                for i in range(GX):
                    rim_copy(k, lax.rem(gx + i, GX), gx).wait_send()

            def blank(there=there):
                ygot[there] = jnp.zeros(ygot.shape[1:], F32)

            pl.when(sends)(start)
            pl.when(jnp.logical_not(receives))(blank)
            drains.append(lambda sends=sends, drain=drain: pl.when(sends)(drain))
        for e in range(GX):
            tile = jnp.zeros((8, 128), F32)
            for z in range(4):
                if e > 0:
                    tile = jnp.where(lane1 == 2 * z, sb[e - 1, z][:, 255:256], tile)
                if e < GX - 1:
                    tile = jnp.where(lane1 == 2 * z + 1, sb[e + 1, z][:, 0:1], tile)
            tile = jnp.exp(tile)
            if e == 0:
                tile = jnp.where(lane1 % 2 == 0, 0.0, tile)
            if e == GX - 1:
                tile = jnp.where(lane1 % 2 == 1, 0.0, tile)
            xspill[e] = tile
        for i in range(1, GX):
            column_copy(lax.rem(gx + i, GX), gx).start()
        xgot[gx] = xspill[gx]

        def drain_columns():
            for i in range(1, GX):
                column_copy(lax.rem(gx + i, GX), gx).wait_send()

        drains.append(drain_columns)

    def wait_spill():
        for i in range(1, GX):
            peer = lax.rem(gx + GX - i, GX)
            column_copy(peer, peer).wait_recv()
        for k in range(2):

            def wait(k=k):
                for i in range(GX):
                    peer = lax.rem(gx + GX - i, GX)
                    rim_copy(k, peer, peer).wait_recv()

            pl.when(rims[k][3])(wait)

    drains.append(
        spectral_part(
            spec, shifts, dft_hbm, twiddle_hbm, order_hbm, log_perm,
            xb, trig, lhs_hi, lhs_lo, zb, wb_hi, wb_lo, sb, dft, twiddle, order,
            send1, recv1, send2, recv2, local, greet_all, meanwhile, spill,
        )
    )

    def make_perm(z, carry):
        perm[z] = jnp.exp(log_perm[z])
        return carry

    lax.fori_loop(0, DEPTH, make_perm, 0, unroll=4)
    source_copy.wait()
    colour_copy.wait()
    arrived[0]()
    wait_spill()

    def beside(value, west, east, lower, upper):
        vw = jnp.where(lane == 0, west, pltpu.roll(value, 1, 1))
        ve = jnp.where(lane == WIDTH - 1, east, pltpu.roll(value, WIDTH - 1, 1))
        vs = jnp.where(sub == 0, lower, pltpu.roll(value, 1, 0))
        vn = jnp.where(sub == 7, upper, pltpu.roll(value, 7, 0))
        return vw, ve, vs, vn

    def spilled(z):
        owner, place = z // 4, 2 * (z % 4)
        west = xgot[owner][:, place:place + 1]
        east = xgot[owner][:, place + 1:place + 2]
        lower, upper = (
            jnp.concatenate(
                [ygot[k, owner, pl.ds(place + h, 1), :] for h in range(2)], axis=1
            )
            for k in range(2)
        )
        return west, east, lower, upper

    def edges(z, xh, yh):
        west = xh[0][:, z:z + 1]
        east = xh[1][:, z:z + 1]
        lower = yh[0, pl.ds(z, 1), :]
        upper = yh[1, pl.ds(z, 1), :]
        return west, east, lower, upper

    for z in range(DEPTH):
        p = perm[z]
        pw, pe, ps, pn = beside(p, *spilled(z))
        aw, ae, as_, an = harmonic(p, pw), harmonic(p, pe), harmonic(p, ps), harmonic(p, pn)
        ww[z], we[z], ws[z], wn[z] = aw, ae, as_, an
        dd[z] = STORE + aw + ae + as_ + an
        vw, ve, vs, vn = beside(pressure[z], *edges(z, xh0, yh0))
        ff[z] = source[z] + aw * vw + ae * ve + as_ * vs + an * vn
        if z < DEPTH - 1:
            cc[z] = VERT * harmonic(p, perm[z + 1])

    for level in LEVELS:
        for n, a, b in level:
            wl, wr, d, f = cc[a], cc[n], dd[n], ff[n]
            inv = 1.0 / (d + wl + wr)
            l, r = wl * inv, wr * inv
            ll[n], rr[n], iv[n] = l, r, inv
            cc[a] = l * wr
            dd[a] = dd[a] + l * d
            dd[b] = dd[b] + r * d
            ff[a] = ff[a] + l * f
            ff[b] = ff[b] + r * f

    def put(ref, kind, value):
        for h in range(2):
            ref[pl.ds(8 * h + kind, 8, stride=16), :] = value[:, 128 * h:128 * h + 128]

    def take(ref, kind):
        return jnp.concatenate(
            [ref[pl.ds(8 * h + kind, 8, stride=16), :] for h in range(2)], axis=1
        )

    row = lax.div(gz, 2)

    def everyone(src, dst, phase, size, offsets, to_owner):
        def tile(index):
            return pl.ds(pl.multiple_of(size * index, 8), size)

        def copy(peer, slot, first, then):
            return pltpu.make_async_remote_copy(
                src_ref=src.at[tile(first)], dst_ref=dst.at[tile(then)],
                send_sem=gz_send.at[phase, peer], recv_sem=gz_recv.at[phase, slot],
                device_id={"gz": peer}, device_id_type=MESH,
            )

        def outward(i):
            peer = lax.rem(gz + i, GZ)
            if to_owner:
                return copy(peer, gz, lax.div(peer, 2), gz)
            return copy(peer, gz, peer, row)

        def inward(i):
            peer = lax.rem(gz + GZ - i, GZ)
            if to_owner:
                return copy(peer, peer, 0, peer)
            return copy(peer, peer, 0, lax.div(peer, 2))

        def finish():
            for i in offsets:
                inward(i).wait_recv()

        def drain():
            for i in offsets:
                outward(i).wait_send()

        for i in offsets:
            outward(i).start()
        if to_owner:
            dst[tile(gz), :] = src[tile(row), :]
        else:
            dst[tile(row), :] = src[tile(gz), :]
        drains.append(drain)
        return finish

    put(msg, 0, dd[0])
    put(msg, 1, dd[DEPTH - 1])
    put(msg, 2, cc[0])
    put(msg, 3, perm[0])
    put(msg, 4, perm[DEPTH - 1])
    put(msg, 5, ff[0])
    put(msg, 6, ff[DEPTH - 1])
    put(msg, 7, ff[0])
    everyone(msg, got, 0, 16, FAR_FIRST, True)()

    def kind(ref, k):
        return jnp.concatenate(
            [ref[pl.ds(8 * h + k, GZ, stride=16), :] for h in range(2)], axis=1
        )

    def spread(ref, size, k, value):
        for h in range(2):
            ref[pl.ds(size * h + k, GZ, stride=2 * size), :] = value[:, 128 * h:128 * h + 128]

    d0, d1, c, p0, p1 = (kind(got, k) for k in range(5))
    f0, f1 = kind(got, 5), kind(got, 6)
    segment = lax.broadcasted_iota(jnp.int32, (GZ, WIDTH), 0)
    w = jnp.where(segment < GZ - 1, VERT * harmonic(p1, pltpu.roll(p0, GZ - 1, 0)), 0.0)
    last_inv = 1.0 / (d1 + c + w)
    last_l, last_r = c * last_inv, w * last_inv

    def up(value, step):
        return pltpu.roll(value, step, 0)

    def down(value, step):
        return pltpu.roll(value, GZ - step, 0)

    e = d0 + last_l * d1 + up(last_r * d1, 1)
    b = last_l * w
    a = up(b, 1)
    f = f0 + last_l * f1 + up(last_r * f1, 1)
    for step in (1, 2, 4, 8):
        inv = 1.0 / (e + a + b)
        alpha, beta = a * up(inv, step), b * down(inv, step)
        e = e + alpha * up(e, step) + beta * down(e, step)
        f = f + alpha * up(f, step) + beta * down(f, step)
        if step < 8:
            a, b = alpha * up(a, step), beta * down(b, step)
    first = f / e
    ans[...] = jnp.zeros_like(ans)
    spread(ans, 8, 0, first)
    spread(ans, 8, 1, f1 * last_inv + last_l * first + last_r * down(first, 1))
    wait_sol = everyone(ans, sol, 1, 16, ROUND_FIRST, False)

    links = [jnp.zeros((1, WIDTH), F32)] * 2
    for i in range(GZ):
        j = GZ - 1 - i
        eb, et = links
        at_i, at_j = pl.ds(i, 1), pl.ds(j, 1)
        chain[2, at_i, :] = eb
        chain[5, at_j, :] = et
        low = d0[i:i + 1] + eb
        rho = c[i:i + 1] / (low + c[i:i + 1])
        low = d1[i:i + 1] + rho * low
        tau = w[i:i + 1] / (low + w[i:i + 1])
        chain[0, at_i, :] = rho
        chain[1, at_i, :] = tau
        high = d1[j:j + 1] + et
        sigma = c[j:j + 1] / (high + c[j:j + 1])
        high = d0[j:j + 1] + sigma * high
        chain[3, at_j, :] = sigma
        if j > 0:
            upsilon = w[j - 1:j] / (high + w[j - 1:j])
            chain[4, pl.ds(j - 1, 1), :] = upsilon
        links = [tau * low, upsilon * high]
    chain[4, pl.ds(GZ - 1, 1), :] = jnp.zeros((1, WIDTH), F32)
    tau, upsilon = chain[1], chain[4]
    climb = up(tau * chain[0], 1)
    descend = upsilon * down(chain[3], 1)
    from_below, from_above = [None, up(tau, 1)], [None, upsilon]
    for k in range(2, GZ):
        from_below.append(climb * up(from_below[-1], 1))
        from_above.append(descend * down(from_above[-1], 1))
    gains[...] = jnp.zeros_like(gains)
    for k in range(1, GZ):
        spread(gains, 24, k, from_below[k] + from_above[GZ - k])
    spread(gains, 24, GZ, chain[2])
    spread(gains, 24, GZ + 1, chain[5])
    wait_gains = everyone(gains, taken, 2, 48, ROUND_FIRST, False)
    wait_sol()

    def substitute(first, last, merge):
        u = {0: first, DEPTH - 1: last}
        merge(0, u[0])
        merge(DEPTH - 1, u[DEPTH - 1])
        for level in reversed(LEVELS):
            for n, a, b in level:
                u[n] = ff[n] * iv[n] + ll[n] * u[a] + rr[n] * u[b]
                merge(n, u[n])

    tint = colour[...]

    def merge_half(z, u):
        half[z] = jnp.where(tint == 0, u, pressure[z])

    substitute(take(sol, 0), take(sol, 1), merge_half)
    pack(half, xs2, ys2)
    wait_half = halo(2, xs2, xh2, ys2, yh2)

    def gain(k):
        return jnp.concatenate(
            [taken[pl.ds(24 * h + k, 8, stride=48), :] for h in range(2)], axis=1
        )

    wait_gains()
    c = cc[0]
    low = dd[0] + gain(GZ)
    high = dd[DEPTH - 1] + gain(GZ + 1)
    low_inv = 1.0 / (low + c)
    rho = c * low_inv
    sigma = c / (high + c)
    high_inv = 1.0 / (high + rho * low)
    wait_half()
    for z in range(DEPTH):
        vw, ve, vs, vn = beside(half[z], *edges(z, xh2, yh2))
        ff[z] = source[z] + ww[z] * vw + we[z] * ve + ws[z] * vs + wn[z] * vn
    for level in LEVELS:
        for n, a, b in level:
            f = ff[n]
            ff[a] = ff[a] + ll[n] * f
            ff[b] = ff[b] + rr[n] * f
    f0, f1 = ff[0], ff[DEPTH - 1]
    sums[0] = f1 + rho * f0
    sums[1] = f0 + sigma * f1

    def cast(i):
        peer = lax.rem(gz + i, GZ)
        return pltpu.make_async_remote_copy(
            src_ref=sums.at[lax.div(gz + i, GZ)], dst_ref=others.at[gz],
            send_sem=gz_send.at[3, peer], recv_sem=gz_recv.at[3, gz],
            device_id={"gz": peer}, device_id_type=MESH,
        )

    def heard(i):
        peer = lax.rem(gz + GZ - i, GZ)
        return pltpu.make_async_remote_copy(
            src_ref=sums.at[0], dst_ref=others.at[peer],
            send_sem=gz_send.at[3, peer], recv_sem=gz_recv.at[3, peer],
            device_id={"gz": peer}, device_id_type=MESH,
        )

    def drain_cast():
        for i in FAR_FIRST:
            cast(i).wait_send()

    for i in FAR_FIRST:
        cast(i).start()
    drains.append(drain_cast)
    for i in FAR_FIRST:
        heard(i).wait_recv()
    for i in range(1, GZ):
        part = gain(i) * others[lax.rem(gz + GZ - i, GZ)]
        f0 = f0 + jnp.where(gz >= i, part, 0.0)
        f1 = f1 + jnp.where(gz >= i, 0.0, part)
    last = (f1 + rho * f0) * high_inv
    first = f0 * low_inv + rho * last

    def merge_out(z, u):
        out[z] = jnp.where(tint == 1, u, half[z])

    substitute(first, last, merge_out)
    for drain in drains:
        drain()


def pin(value):
    return pltpu.with_memory_space_constraint(value, pltpu.HBM)


def field_call(spectral, shifts, colour, pressure, source):
    vmem = pl.BlockSpec(memory_space=pltpu.VMEM)
    hbm = pl.BlockSpec(memory_space=pltpu.HBM)
    block = (DEPTH, ITEMS, WIDTH)
    field = pltpu.VMEM(block, F32)
    board = pltpu.VMEM((8 * GZ, 128), F32)
    pair_board = pltpu.VMEM((16 * GZ, 128), F32)
    columns = pltpu.VMEM((2, ITEMS, 128), F32)
    rows = pltpu.VMEM((2, DEPTH, WIDTH), F32)
    tiles = pltpu.VMEM((GX, 8, 128), F32)
    dma = pltpu.SemaphoreType.DMA
    return pl.pallas_call(
        field_kernel,
        out_shape=jax.ShapeDtypeStruct((2, *block), F32),
        in_specs=[hbm] * 8,
        out_specs=vmem,
        scratch_shapes=[
            pltpu.VMEM((GX, 2, 4, 8, WIDTH), F32),
            pltpu.VMEM((2, GX, ROWS, WIDTH), F32),
            pltpu.VMEM((256, 512), BF16),
            pltpu.VMEM((256, 512), BF16),
            pltpu.VMEM((256, WIDTH), F32),
            pltpu.VMEM((256, WIDTH), BF16),
            pltpu.VMEM((256, WIDTH), BF16),
            pltpu.VMEM((GX, 4, 8, WIDTH), F32),
            pltpu.VMEM((2, 512, WIDTH), BF16),
            pltpu.VMEM((2, GX, WIDTH), F32),
            pltpu.VMEM((WIDTH, WIDTH), BF16),
            dma((GX,)), dma((GX,)), dma((GX,)), dma((GX,)), dma((8,)),
            field, field, pltpu.VMEM((ITEMS, WIDTH), jnp.int32),
            pltpu.VMEM((ITEMS, DEPTH), jnp.int32),
        ]
        + [field] * 12
        + [columns, columns, rows, rows]
        + [tiles, tiles, pltpu.VMEM((2, GX, 8, 128), F32), pltpu.VMEM((2, GX, 8, 128), F32)]
        + [columns, columns, rows, rows]
        + [board, pair_board, pair_board, board]
        + [
            pltpu.VMEM((48 * GZ, 128), F32),
            pltpu.VMEM((24 * GZ, 128), F32),
            pltpu.VMEM((6, GZ, WIDTH), F32),
            pltpu.VMEM((2, ITEMS, WIDTH), F32),
            pltpu.VMEM((GZ, ITEMS, WIDTH), F32),
        ]
        + [dma((3, 4)), dma((3, 4)), dma((4, GZ)), dma((4, GZ))]
        + [pltpu.SemaphoreType.REGULAR((RELAYS + 1,)), dma((3, GX)), dma((3, GX))],
        compiler_params=pltpu.CompilerParams(
            collective_id=0, has_side_effects=True, vmem_limit_bytes=32 << 20
        ),
        name="field",
    )(
        *map(pin, (spectral, shifts.T, *map(jnp.asarray, tables()), pressure, source, colour))
    )


def body(spectral, shifts, colour, pressure, source):
    both = field_call(spectral, shifts, colour, pressure, source)
    return (both[0], both[1])


def solution(mesh):
    in_specs = (
        P(None, "gz", "gy", "gx"),
        P("gz", "gy"),
        P("gy", "gx"),
        P("gz", "gy", "gx"),
        P("gz", "gy", "gx"),
    )
    out_specs = (P("gz", "gy", "gx"), P("gz", "gy", "gx"))
    return jax.shard_map(body, mesh=mesh, in_specs=in_specs, out_specs=out_specs, check_vma=False)
```
